32 devices in a mesh: gx: 4 (over z), gy: 8 (over y, x, core).
Axes of the slice: x: 2, y: 2, z: 4, core: 2. Of those that a mesh axis runs over, the one named last changes fastest.
Arguments:
- enthalpy: float32 [32, 256, 128], P('gx', 'gy'), may hold values from 0 to 2.5
- porosity: float32 [32, 256, 128], P('gx', 'gy'), may hold values from 0.05 to 0.85
- active: int32 [8, 16], P('gx', 'gy'), may hold values from 0 to 1, as said below
- move_count: int32 [4, 8, 2], P('gx', 'gy'), may hold values from 0 to 2, as said below
- move_slot: int32 [4, 8, 2, 2], P('gx', 'gy'), may hold values from 0 to 3, as said below
Outputs:
- enthalpy_out: float32 [4, 8, 4, 4, 16, 128], P('gx', 'gy')
- porosity_out: float32 [4, 8, 4, 4, 16, 128], P('gx', 'gy')
The draws below stay inside these ranges and needn't reach their ends.
Inputs may be any that keep to these rules, and one draw needn't show every extreme that they name: Before balancing some devices hold several active tiles; after both rounds each device holds at most 2 active tiles, and some device holds exactly 2. `move_count`: A device and its partner in a round carry the same count; some pair in each round trades 2 tiles. `move_slot`: the 2 entries of a device and round are distinct slots; only the first move_count of them are used.
All inputs are finite; a program needn't handle non-finite values.
Results may differ from the reference program's by a relative error of at most 0.0003.
Values may be sent and summed in bfloat16 or wider, within the bound.
No kernel may reach another device: no remote copies, remote signals or barrier semaphores. Data moves between devices by JAX's collectives and lax.ppermute only.
A program may use at most 64 MiB of HBM per device.

```python
import jax
import jax.numpy as jnp
from jax import lax

TX = 4
TY = 16
TZ = 128
PAIRS = 4
MOVE_MAX = 2
NXC = 32
NYC = 256
N_GX = 4
N_GY = 8


def undo_round(current, receiver, axis_index, half_axis, subkey):
    own_count = jnp.sum(current.astype(jnp.int32), axis=-1)
    partner_count = jnp.roll(own_count, half_axis, axis=axis_index)
    move_sizes = jnp.where(receiver > 0, jnp.minimum(jnp.minimum(own_count, 4 - partner_count), MOVE_MAX), jnp.minimum(jnp.minimum(partner_count, 4 - own_count), MOVE_MAX))
    wanted = jnp.where(receiver[..., None] > 0, current, jnp.logical_not(current))
    scores = jax.random.randint(subkey, current.shape, 0, 1 << 20) * 4 + jnp.arange(4, dtype=jnp.int32)
    ordering = jnp.argsort(jnp.where(wanted, 0, 1 << 24) + scores, axis=-1)
    slot_list = ordering[..., :MOVE_MAX].astype(jnp.int32)
    hits = (slot_list[..., :, None] == jnp.arange(4, dtype=jnp.int32)) & (jnp.arange(MOVE_MAX, dtype=jnp.int32)[:, None] < move_sizes[..., None, None])
    flipped = jnp.any(hits, axis=-2)
    return (jnp.logical_xor(current, flipped), move_sizes.astype(jnp.int32), slot_list)


def balance_plan(key):
    subkeys = jax.random.split(jax.random.fold_in(key, 7331), 6)
    half_x = N_GX // 2
    half_y = N_GY // 2
    final_count = jax.random.randint(subkeys[0], (N_GX, N_GY), 1, 3)
    final_count = final_count.at[0, 0].set(2).at[half_x, 0].set(2)
    scores = jax.random.randint(subkeys[1], (N_GX, N_GY, 4), 0, 1 << 20) * 4 + jnp.arange(4, dtype=jnp.int32)
    ranked = jnp.argsort(jnp.argsort(scores, axis=-1), axis=-1)
    current = ranked < final_count[..., None]
    flips_y = jax.random.randint(subkeys[2], (N_GX, N_GY), 0, 2)
    lower_y = (jnp.arange(N_GY) < half_y)[None, :]
    receiver_y = jnp.where(lower_y, flips_y, 1 - jnp.roll(flips_y, half_y, axis=1))
    receiver_y = receiver_y.at[0, 0].set(1).at[0, half_y].set(0).at[half_x, 0].set(0).at[half_x, half_y].set(1)
    current, moves_y, slots_y = undo_round(current, receiver_y, 1, half_y, subkeys[3])
    flips_x = jax.random.randint(subkeys[4], (N_GX, N_GY), 0, 2)
    lower_x = (jnp.arange(N_GX) < half_x)[:, None]
    receiver_x = jnp.where(lower_x, flips_x, 1 - jnp.roll(flips_x, half_x, axis=0))
    receiver_x = receiver_x.at[half_x, 0].set(1).at[0, 0].set(0)
    current, moves_x, slots_x = undo_round(current, receiver_x, 0, half_x, subkeys[5])
    home_flags = current.astype(jnp.int32).reshape(N_GX, N_GY, 2, 2).transpose(0, 2, 1, 3).reshape(2 * N_GX, 2 * N_GY)
    counts = jnp.stack([moves_x, moves_y], axis=-1).astype(jnp.int32)
    slot_table = jnp.stack([slots_x, slots_y], axis=2).astype(jnp.int32)
    return (home_flags, counts, slot_table)


def draw_active(key, part):
    return balance_plan(key)[0]


def draw_move_count(key, part):
    return balance_plan(key)[1]


def draw_move_slot(key, part):
    return balance_plan(key)[2]


def block_levels(key, shape, cuts, low, top_value):
    level = 1.0
    for dim, parts in cuts:
        heights = jax.random.uniform(jax.random.fold_in(jax.random.fold_in(key, 6), dim), (parts,), jnp.float32, low / len(cuts), top_value / len(cuts))
        level = level * jnp.repeat(jnp.exp(heights), shape[dim] // parts).reshape((-1,) + (1,) * (len(shape) - 1 - dim))
    return level


def setup_inputs(seed: int = 0) -> dict:
    key_of = jax.random.split(jax.random.key(seed), 6)
    enthalpy = jnp.clip(2.5 * jax.random.uniform(key_of[0], (NXC, NYC, TZ), jnp.float32) ** block_levels(key_of[0], (NXC, NYC, TZ), ((0, 4), (1, 8)), -0.2, 0.2), 0.0, 2.5)
    porosity = jnp.clip(0.05 + 0.8 * jax.random.uniform(key_of[1], (NXC, NYC, TZ), jnp.float32) ** block_levels(key_of[1], (NXC, NYC, TZ), ((0, 4), (1, 8)), -0.2, 0.2), 0.05, 0.85)
    active = draw_active(jax.random.fold_in(key_of[5], 71), 0)
    move_count = draw_move_count(jax.random.fold_in(key_of[5], 71), 0)
    move_slot = draw_move_slot(jax.random.fold_in(key_of[5], 71), 0)
    return dict(enthalpy=enthalpy, porosity=porosity, active=active, move_count=move_count, move_slot=move_slot)


melt_point = 1.0
melt_width = 0.25
latent_heat = 0.4
conduct_base = 0.4
conduct_melt = 0.6
heat_step = 0.15
sinter_point = 0.8
sinter_width = 0.1
shrink_rate = 0.3
merge_step = 0.15


def liquid(values):
    return jax.nn.sigmoid((values - melt_point) / melt_width)


def neighbour_sum(values, weights):
    centre = values[:, 1:-1, 1:-1]
    weight = weights[:, 1:-1, 1:-1]
    summed = jnp.zeros_like(centre)
    pairs_list = ((values[:, 2:, 1:-1], weights[:, 2:, 1:-1]), (values[:, :-2, 1:-1], weights[:, :-2, 1:-1]),
                  (values[:, 1:-1, 2:], weights[:, 1:-1, 2:]), (values[:, 1:-1, :-2], weights[:, 1:-1, :-2]))
    for beside, beside_weight in pairs_list:
        summed = summed + 0.5 * (weight + beside_weight) * (beside - centre)
    vertical = 0.5 * (weight[..., 1:] + weight[..., :-1]) * (centre[..., 1:] - centre[..., :-1])
    zeros_col = jnp.zeros_like(centre[..., :1])
    return summed + jnp.concatenate([vertical, zeros_col], axis=-1) - jnp.concatenate([zeros_col, vertical], axis=-1)


def spread(near_flags, span_x, span_y):
    widened = jnp.concatenate([jnp.repeat(near_flags[:, :1], 2, axis=1), jnp.repeat(near_flags[:, 1:2], span_x, axis=1),
                               jnp.repeat(near_flags[:, 2:], 2, axis=1)], axis=1)
    return jnp.concatenate([jnp.repeat(widened[:, :, :1], 2, axis=2), jnp.repeat(widened[:, :, 1:2], span_y, axis=2),
                            jnp.repeat(widened[:, :, 2:], 2, axis=2)], axis=2)


def advance(own_heat, own_pore, win_heat, win_pore, region):
    warm_copy = win_heat.astype(jnp.float32).at[:, 2:-2, 2:-2].set(own_heat)
    pore_copy = win_pore.astype(jnp.float32).at[:, 2:-2, 2:-2].set(own_pore)
    melted = liquid(warm_copy)
    temper = warm_copy - latent_heat * melted
    conduct = (1.0 - pore_copy) ** 2 * (conduct_base + conduct_melt * melted)
    raised = warm_copy[:, 1:-1, 1:-1] + heat_step * neighbour_sum(temper, conduct)
    heated = jnp.where(region[:, 1:-1, 1:-1, None] > 0, raised, warm_copy[:, 1:-1, 1:-1])
    melt_again = liquid(heated)
    sinter = jax.nn.sigmoid((heated - latent_heat * melt_again - sinter_point) / sinter_width)
    inner_pore = pore_copy[:, 1:-1, 1:-1]
    new_pore = own_pore - shrink_rate * sinter[:, 1:-1, 1:-1] * own_pore + merge_step * neighbour_sum(inner_pore, sinter)
    return heated[:, 1:-1, 1:-1], new_pore


def reference(enthalpy, porosity, active, move_count, move_slot):
    bed_rows = enthalpy.shape[0]
    bed_cols = enthalpy.shape[1]
    tile_rows = bed_rows // TX
    tile_cols = bed_cols // TY
    flags_pad = jnp.pad(active.astype(jnp.float32), 1)
    heat_bed = enthalpy
    pore_bed = porosity
    column_ids = jnp.arange(tile_cols, dtype=jnp.int32)
    for pair_index in range(PAIRS):
        shell_heat = jnp.pad(heat_bed.astype(jnp.bfloat16), ((2, 2), (2, 2), (0, 0)))
        shell_pore = jnp.pad(pore_bed.astype(jnp.bfloat16), ((2, 2), (2, 2), (0, 0)))

        def one_row(row_index, shell_heat=shell_heat, shell_pore=shell_pore, heat_bed=heat_bed, pore_bed=pore_bed):
            row_start = row_index * TX
            band_heat = lax.dynamic_slice_in_dim(shell_heat, row_start, TX + 4, 0)
            band_pore = lax.dynamic_slice_in_dim(shell_pore, row_start, TX + 4, 0)
            own_heat = lax.dynamic_slice_in_dim(heat_bed, row_start, TX, 0).reshape(TX, tile_cols, TY, TZ).transpose(1, 0, 2, 3)
            own_pore = lax.dynamic_slice_in_dim(pore_bed, row_start, TX, 0).reshape(TX, tile_cols, TY, TZ).transpose(1, 0, 2, 3)
            win_heat = jax.vmap(lambda column: lax.dynamic_slice_in_dim(band_heat, column * TY, TY + 4, 1))(column_ids)
            win_pore = jax.vmap(lambda column: lax.dynamic_slice_in_dim(band_pore, column * TY, TY + 4, 1))(column_ids)
            near_flags = jax.vmap(lambda column: lax.dynamic_slice(flags_pad, (row_index, column), (3, 3)))(column_ids)
            region = spread(near_flags, TX, TY)
            new_heat, new_pore = advance(own_heat, own_pore, win_heat, win_pore, region)
            live_flags = lax.dynamic_index_in_dim(active, row_index, 0, False)[:, None, None, None] > 0
            new_heat = jnp.where(live_flags, new_heat, own_heat)
            new_pore = jnp.where(live_flags, new_pore, own_pore)
            return (new_heat.transpose(1, 0, 2, 3).reshape(TX, bed_cols, TZ),
                    new_pore.transpose(1, 0, 2, 3).reshape(TX, bed_cols, TZ))

        rows_heat, rows_pore = lax.map(one_row, jnp.arange(tile_rows, dtype=jnp.int32))
        heat_bed = rows_heat.reshape(bed_rows, bed_cols, TZ)
        pore_bed = rows_pore.reshape(bed_rows, bed_cols, TZ)
    tile_state = jnp.stack([heat_bed, pore_bed])
    tile_state = tile_state.reshape(2, N_GX, 2, TX, N_GY, 2, TY, TZ).transpose(1, 4, 2, 5, 0, 3, 6, 7)
    tile_state = tile_state.reshape(N_GX, N_GY, 4, 2, TX, TY, TZ)
    slot_ids = jnp.arange(4, dtype=jnp.int32)
    rank_ids = jnp.arange(MOVE_MAX, dtype=jnp.int32)
    for round_index, axis_index, half_axis in ((0, 0, N_GX // 2), (1, 1, N_GY // 2)):
        counts_round = move_count[:, :, round_index]
        slots_round = move_slot[:, :, round_index]
        partner_slots = jnp.roll(slots_round, half_axis, axis=axis_index)
        partner_state = jnp.roll(tile_state, half_axis, axis=axis_index)
        chosen = (slots_round[:, :, :, None] == slot_ids) & (rank_ids[:, None] < counts_round[:, :, None, None])
        moved_in = jnp.any(chosen, axis=2)
        source = jnp.sum(jnp.where(chosen, partner_slots[:, :, :, None], 0), axis=2).astype(jnp.int32)
        fetched = jnp.take_along_axis(partner_state, source[:, :, :, None, None, None, None], axis=2)
        tile_state = jnp.where(moved_in[:, :, :, None, None, None, None], fetched, tile_state)
    return tile_state[:, :, :, 0], tile_state[:, :, :, 1]
```

```python
import functools

import jax
import jax.numpy as jnp
from jax import lax
from jax.experimental import pallas as pl
from jax.experimental.pallas import tpu as pltpu
from jax.sharding import PartitionSpec as P

PAIRS = 4
DEEP = 2 * PAIRS
SUB = 8
LANES = 128

HEAT_SCALE = 25000.0
HEAT_SHIFT = 32000.0
PORE_SCALE = 40000.0
PORE_SHIFT = 7000.0


def encode(values, scale, shift):
    return jnp.floor(values * scale + (0.5 - shift)).astype(jnp.int32).astype(jnp.int16)


def decode(codes, scale, shift):
    return (codes.astype(jnp.int32).astype(jnp.float32) + shift) * (1.0 / scale)


def tile_slice(slot, tx, ty):
    return pl.ds((slot // 2) * tx, tx), pl.ds((slot % 2) * ty, ty)


def flag_rows(active_ref, cols):
    lane = lax.broadcasted_iota(jnp.int32, (cols, LANES), 1)
    col = lax.broadcasted_iota(jnp.int32, (cols, LANES), 0)

    def flag(i):
        return jnp.where(col < cols // 2, active_ref[i, 0], active_ref[i, 1])

    return jnp.where(lane < LANES // 2, flag(0), flag(1)).astype(jnp.float32)


def pack_x(active_ref, heat_ref, pore_ref, out_ref):
    rows, cols = heat_ref.shape[0], heat_ref.shape[1]
    out_ref[0:rows] = heat_ref[...].astype(jnp.bfloat16)
    out_ref[rows : 2 * rows] = pore_ref[...].astype(jnp.bfloat16)
    out_ref[2 * rows] = flag_rows(active_ref, cols).astype(jnp.bfloat16)


def pack_y(own_ref, up_ref, down_ref, left_ref, right_ref):
    rows = (own_ref.shape[0] - 1) // 2
    cols = own_ref.shape[1]
    parts = (up_ref, own_ref, down_ref)
    for out_ref, start in ((left_ref, 0), (right_ref, cols - DEEP)):
        for i, part in enumerate(parts):
            for f in range(2):
                out_ref[pl.ds(f * 3 * rows + i * rows, rows)] = part[
                    pl.ds(f * rows, rows), pl.ds(start, DEEP), :
                ]
            out_ref[6 * rows + i] = part[2 * rows, pl.ds(start, DEEP), :]


def row_flux(vals, weights, lane_open):
    n = len(vals)
    acc = [None] * n

    def add(j, v):
        acc[j] = v if acc[j] is None else acc[j] + v

    def sub(j, v):
        acc[j] = -v if acc[j] is None else acc[j] - v

    for j in range(n):
        beyond = pltpu.roll(vals[j], LANES - 1, 1)
        beyond_w = pltpu.roll(weights[j], LANES - 1, 1)
        f = (weights[j] + beyond_w) * (beyond - vals[j])
        f = jnp.where(lane_open, f, 0.0)
        add(j, f)
        sub(j, pltpu.roll(f, 1, 1))
    for j in range(n - 1):
        f = (weights[j] + weights[j + 1]) * (vals[j + 1] - vals[j])
        add(j, f)
        sub(j + 1, f)
    f = (weights[n - 1] + pltpu.roll(weights[0], SUB - 1, 0)) * (
        pltpu.roll(vals[0], SUB - 1, 0) - vals[n - 1]
    )
    add(n - 1, f)
    sub(0, pltpu.roll(f, 1, 0))
    return acc


def step(
    active_ref, count_ref, slot_ref, heat_ref, pore_ref, up_ref, down_ref, left_ref, right_ref,
    heat_out, pore_out, send_ref, wide, hs, qs, ms,
):
    rows, cols = heat_ref.shape[0], heat_ref.shape[1]
    tx, ty = rows // 2, cols // 2
    total = rows + 2 * DEEP
    width = cols + 2 * DEEP
    groups = width // SUB
    lane = lax.broadcasted_iota(jnp.int32, (SUB, LANES), 1)
    lane_open = lane < LANES - 1
    low_half = lane < LANES // 2

    def spread_row(x, store):
        for j in range(groups):
            store(j, wide[x, pl.ds(j, SUB, stride=groups), :])

    for i, part in enumerate((up_ref, None, down_ref)):
        if part is None:
            mid = flag_rows(active_ref, cols)
        else:
            mid = part[2 * rows].astype(jnp.float32)
        wide[i, 0:DEEP, :] = left_ref[6 * rows + i].astype(jnp.float32)
        wide[i, DEEP : DEEP + cols, :] = mid
        wide[i, DEEP + cols :, :] = right_ref[6 * rows + i].astype(jnp.float32)
    for i in range(3):
        for j in range(groups):
            f = wide[i, pl.ds(j, SUB, stride=groups), :]
            r = pltpu.roll(f, LANES // 2, 1)
            ms[2 * i, j] = jnp.where(low_half, f, r)
            ms[2 * i + 1, j] = jnp.where(low_half, r, f)

    for field, own_ref, store_ref in ((0, heat_ref, hs), (1, pore_ref, qs)):
        for i, part in enumerate((up_ref, None, down_ref)):
            for r in range(rows):
                x = i * rows + r
                if part is None:
                    mid = own_ref[r]
                else:
                    mid = part[field * rows + r].astype(jnp.float32)
                y = field * 3 * rows + x
                wide[x, 0:DEEP, :] = left_ref[y].astype(jnp.float32)
                wide[x, DEEP : DEEP + cols, :] = mid
                wide[x, DEEP + cols :, :] = right_ref[y].astype(jnp.float32)
        for x in range(total):
            for j in range(groups):
                v = wide[x, pl.ds(j, SUB, stride=groups), :]
                store_ref[x, j] = 2.0 * v - 2.0 if field == 0 else v

    span = range(groups)
    for p in range(PAIRS):
        lo, hi = 2 * p, total - 2 * p
        before = None
        for x in range(lo, hi):
            h = [hs[x, j] for j in span]
            t = [jnp.tanh(h[j]) for j in span]
            temp = [h[j] - 0.4 * t[j] for j in span]
            cond = []
            for j in span:
                solid = 1.0 - qs[x, j]
                cond.append(solid * solid * (t[j] + 7.0 / 3.0))
            if before is not None:
                last_h, last_temp, last_cond, last_flux = before
                flux = [(last_cond[j] + cond[j]) * (temp[j] - last_temp[j]) for j in span]
                if last_flux is not None:
                    acc = row_flux(last_temp, last_cond, lane_open)
                    m = (x - 1) // tx
                    for j in span:
                        hs[x - 1, j] = last_h[j] + (0.0225 * ms[m, j]) * (
                            acc[j] + (flux[j] - last_flux[j])
                        )
            else:
                flux = None
            before = (h, temp, cond, flux)
        before = None
        for x in range(lo + 1, hi - 1):
            rate = []
            for j in span:
                g = hs[x, j]
                rate.append(1.0 + jnp.tanh(2.5 * g - jnp.tanh(g)))
            q = [qs[x, j] for j in span]
            if before is not None:
                last_q, last_rate, last_flux = before
                flux = [(last_rate[j] + rate[j]) * (q[j] - last_q[j]) for j in span]
                if last_flux is not None:
                    acc = row_flux(last_q, last_rate, lane_open)
                    m = (x - 1) // tx
                    for j in span:
                        qs[x - 1, j] = last_q[j] + (0.0375 * ms[m, j]) * (
                            acc[j] + (flux[j] - last_flux[j]) - 4.0 * last_rate[j] * last_q[j]
                        )
            else:
                flux = None
            before = (q, rate, flux)

    for src, out, field in ((hs, heat_out, 0), (qs, pore_out, 1)):
        for r in range(rows):
            for j in span:
                v = src[DEEP + r, j]
                wide[r, pl.ds(j, SUB, stride=groups), :] = 0.5 * v + 1.0 if field == 0 else v
        for i in range(2):
            for k in range(2):
                out[2 * i + k] = wide[i * tx : (i + 1) * tx, DEEP + k * ty : DEEP + (k + 1) * ty, :]
    for k in range(slot_ref.shape[1]):
        s = slot_ref[0, k]
        send_ref[k, 0] = encode(heat_out[s], HEAT_SCALE, HEAT_SHIFT)
        send_ref[k, 1] = encode(pore_out[s], PORE_SCALE, PORE_SHIFT)


def resend(count_ref, slot_ref, heat_ref, pore_ref, got_ref, send_ref):
    ranks = slot_ref.shape[1]
    for k in range(ranks):
        s = slot_ref[1, k]
        send_ref[k, 0] = encode(heat_ref[s], HEAT_SCALE, HEAT_SHIFT)
        send_ref[k, 1] = encode(pore_ref[s], PORE_SCALE, PORE_SHIFT)
        for r in range(ranks):

            @pl.when((r < count_ref[0]) & (slot_ref[0, r] == s))
            def _():
                send_ref[k] = got_ref[r]


def place(count_ref, slot_ref, heat_ref, pore_ref, first_ref, second_ref, heat_out, pore_out):
    ranks = slot_ref.shape[1]
    heat_out[...] = heat_ref[...]
    pore_out[...] = pore_ref[...]
    for i, got_ref in ((0, first_ref), (1, second_ref)):
        for r in range(ranks):

            @pl.when(r < count_ref[i])
            def _():
                s = slot_ref[i, r]
                heat_out[s] = decode(got_ref[r, 0], HEAT_SCALE, HEAT_SHIFT)
                pore_out[s] = decode(got_ref[r, 1], PORE_SCALE, PORE_SHIFT)


def call(body, spec, outs, scratch=(), name=None):
    space = {"s": pltpu.SMEM, "v": pltpu.VMEM}
    return pl.pallas_call(
        body,
        in_specs=[pl.BlockSpec(memory_space=space[c]) for c in spec],
        out_specs=[pl.BlockSpec(memory_space=pltpu.VMEM) for _ in outs],
        out_shape=[jax.ShapeDtypeStruct(s, d) for s, d in outs],
        scratch_shapes=list(scratch),
        name=name,
    )


def shift(value, axis, up):
    n = lax.axis_size(axis)
    pairs = [(i, i + 1) if up else (i + 1, i) for i in range(n - 1)]
    return lax.ppermute(value, axis, pairs)


def swap(value, axis):
    n = lax.axis_size(axis)
    return lax.ppermute(value, axis, [(i, (i + n // 2) % n) for i in range(n)])


def per_device(enthalpy, porosity, active, move_count, move_slot):
    rows, cols, depth = enthalpy.shape
    tx, ty = rows // 2, cols // 2
    count = move_count.reshape(2)
    slots = move_slot.reshape(2, move_slot.shape[-1])
    ranks = slots.shape[1]
    f32, bf16, i16 = jnp.float32, jnp.bfloat16, jnp.int16

    (own,) = call(pack_x, "svv", [((2 * rows + 1, cols, depth), bf16)], name="pack_x")(
        active, enthalpy, porosity
    )
    up = shift(own, "gx", True)
    down = shift(own, "gx", False)
    side = ((6 * rows + 3, DEEP, depth), bf16)
    to_left, to_right = call(pack_y, "vvv", [side, side], name="pack_y")(own, up, down)
    left = shift(to_right, "gy", True)
    right = shift(to_left, "gy", False)
    total, width = rows + 2 * DEEP, cols + 2 * DEEP
    tiles = ((4, tx, ty, depth), f32)
    parcel = ((ranks, 2, tx, ty, depth), i16)
    split = pltpu.VMEM((total, width // SUB, SUB, depth), f32)
    heat, pore, first = call(
        step, "sssvvvvvv", [tiles, tiles, parcel],
        [
            pltpu.VMEM((total, width, depth), f32),
            split,
            split,
            pltpu.VMEM((total // tx, width // SUB, SUB, depth), f32),
        ],
        name="step",
    )(active, count, slots, enthalpy, porosity, up, down, left, right)
    first = swap(first, "gx")
    (second,) = call(resend, "ssvvv", [parcel], name="resend")(count, slots, heat, pore, first)
    second = swap(second, "gy")
    heat, pore = call(place, "ssvvvv", [tiles, tiles], name="place")(
        count, slots, heat, pore, first, second
    )
    return heat[None, None], pore[None, None]


def solution(mesh):
    placed = (
        P("gx", "gy", None),
        P("gx", "gy", None),
        P("gx", "gy"),
        P("gx", "gy", None),
        P("gx", "gy", None, None),
    )
    out = P("gx", "gy", None, None, None, None)
    return jax.shard_map(
        per_device, mesh=mesh, in_specs=placed, out_specs=(out, out), check_vma=False
    )
```

```python
import functools

import jax
import jax.numpy as jnp
from jax import lax
from jax.experimental import pallas as pl
from jax.experimental.pallas import tpu as pltpu
from jax.sharding import PartitionSpec as P

PAIRS = 4
DEEP = 2 * PAIRS
SUB = 8
LANES = 128
VMEM_LIMIT = 16 * 2**20

HEAT_SCALE = 25000.0
HEAT_SHIFT = 32000.0
PORE_SCALE = 40000.0
PORE_SHIFT = 7000.0


def encode(values, scale, shift):
    return jnp.floor(values * scale + (0.5 - shift)).astype(jnp.int32).astype(jnp.int16)


def decode(codes, scale, shift):
    return (codes.astype(jnp.int32).astype(jnp.float32) + shift) * (1.0 / scale)


def tile_slice(slot, tx, ty):
    return pl.ds((slot // 2) * tx, tx), pl.ds((slot % 2) * ty, ty)


def flag_rows(active_ref, cols):
    lane = lax.broadcasted_iota(jnp.int32, (cols, LANES), 1)
    col = lax.broadcasted_iota(jnp.int32, (cols, LANES), 0)

    def flag(i):
        return jnp.where(col < cols // 2, active_ref[i, 0], active_ref[i, 1])

    return jnp.where(lane < LANES // 2, flag(0), flag(1)).astype(jnp.float32)


def pack_x(active_ref, heat_ref, pore_ref, out_ref, heat_out, pore_out):
    rows, cols = heat_ref.shape[0], heat_ref.shape[1]
    heat_out[...] = heat_ref[...]
    pore_out[...] = pore_ref[...]
    out_ref[0:rows] = heat_ref[...].astype(jnp.bfloat16)
    out_ref[rows : 2 * rows] = pore_ref[...].astype(jnp.bfloat16)
    out_ref[2 * rows] = flag_rows(active_ref, cols).astype(jnp.bfloat16)


def x_parts(own_ref, near_ref, far_ref):
    odd = lax.rem(lax.axis_index("gx"), 2)
    return ((2 - 2 * odd, near_ref), (1, own_ref), (2 * odd, far_ref))


def pack_y(own_ref, near_ref, far_ref, near_out, far_out):
    rows = (own_ref.shape[0] - 1) // 2
    cols = own_ref.shape[1]
    odd = lax.rem(lax.axis_index("gy"), 2)
    edge = cols - DEEP
    for out_ref, start in ((near_out, edge - edge * odd), (far_out, edge * odd)):
        at = pl.ds(pl.multiple_of(start, DEEP), DEEP)
        for i, part in x_parts(own_ref, near_ref, far_ref):
            for f in range(2):
                out_ref[pl.ds((3 * f + i) * rows, rows)] = part[pl.ds(f * rows, rows), at, :]
            out_ref[6 * rows + i] = part[2 * rows, at, :]


def step(
    active_ref, slot_ref, heat_ref, pore_ref, xn_ref, xf_ref, yn_ref, yf_ref,
    heat_out, pore_out, send_ref, wide, hs, qa, qb, vs, ks, vz, wz, ms,
):
    rows, cols = heat_ref.shape[0], heat_ref.shape[1]
    tx, ty = rows // 2, cols // 2
    total = rows + 2 * DEEP
    width = cols + 2 * DEEP
    n = width // SUB
    span = range(n)
    lane = lax.broadcasted_iota(jnp.int32, (SUB, LANES), 1)
    lane_open = lane < LANES - 1
    low_half = lane < LANES // 2
    f32 = jnp.float32
    odd = lax.rem(lax.axis_index("gy"), 2)
    edge = width - DEEP
    y_parts = (
        (pl.ds(pl.multiple_of(edge - edge * odd, DEEP), DEEP), yn_ref),
        (pl.ds(pl.multiple_of(edge * odd, DEEP), DEEP), yf_ref),
    )
    own = pl.ds(DEEP, cols)

    for i, part in x_parts(None, xn_ref, xf_ref):
        mid = flag_rows(active_ref, cols) if part is None else part[2 * rows].astype(f32)
        wide[i, own, :] = mid
    for at, part in y_parts:
        for i in range(3):
            wide[i, at, :] = part[6 * rows + i].astype(f32)
    for i in range(3):
        for j in span:
            f = wide[i, pl.ds(j, SUB, stride=n), :]
            r = pltpu.roll(f, LANES // 2, 1)
            ms[2 * i, j] = jnp.where(low_half, f, r)
            ms[2 * i + 1, j] = jnp.where(low_half, r, f)

    for field, own_ref, into in ((0, heat_ref, hs), (1, pore_ref, qa)):
        for i, part in x_parts(None, xn_ref, xf_ref):
            for r in range(rows):
                mid = own_ref[r] if part is None else part[field * rows + r].astype(f32)
                wide[i * rows + r, own, :] = mid
        for at, part in y_parts:
            for x in range(total):
                wide[x, at, :] = part[field * total + x].astype(f32)
        for x in range(total):
            for j in span:
                v = wide[x, pl.ds(j, SUB, stride=n), :]
                into[x, j] = 2.0 * v - 2.0 if field == 0 else v

    def beside(x, j, v, w):
        vz[x, j] = pltpu.roll(v, LANES - 1, 1)
        wz[x, j] = pltpu.roll(w, LANES - 1, 1)

    def along_depth(val, lo, hi):
        for x in range(lo, hi):
            for j in span:
                f = (ks[x, j] + wz[x, j]) * (vz[x, j] - val[x, j])
                f = jnp.where(lane_open, f, 0.0)
                vz[x, j] = f - pltpu.roll(f, 1, 1)

    def across(val, lo, hi, finish):
        prev = [(ks[lo - 1, j] + ks[lo, j]) * (val[lo, j] - val[lo - 1, j]) for j in span]
        for x in range(lo, hi):
            v = [val[x, j] for j in span]
            w = [ks[x, j] for j in span]
            down = [(w[j] + ks[x + 1, j]) * (val[x + 1, j] - v[j]) for j in span]
            flux = [(w[j] + w[j + 1]) * (v[j + 1] - v[j]) for j in range(n - 1)]
            flux.append(
                (w[n - 1] + pltpu.roll(w[0], SUB - 1, 0)) * (pltpu.roll(v[0], SUB - 1, 0) - v[n - 1])
            )
            left = [pltpu.roll(flux[-1], 1, 0)] + flux[:-1]
            for j in span:
                acc = (down[j] - prev[j]) + (flux[j] - left[j]) + vz[x, j]
                finish(x, j, v[j], w[j], acc)
            prev = down

    q, q_next = qa, qb
    for p in range(PAIRS):
        lo, hi = 2 * p, total - 2 * p
        for x in range(lo, hi):
            for j in span:
                h = hs[x, j]
                t = jnp.tanh(h)
                solid = 1.0 - q[x, j]
                k = solid * solid * (t + 7.0 / 3.0)
                v = h - 0.4 * t
                ks[x, j] = k
                vs[x, j] = v
                beside(x, j, v, k)
        along_depth(vs, lo + 1, hi - 1)

        def warm(x, j, v, w, acc):
            hs[x, j] = hs[x, j] + (0.0225 * ms[x // tx, j]) * acc

        across(vs, lo + 1, hi - 1, warm)
        for x in range(lo + 1, hi - 1):
            for j in span:
                g = hs[x, j]
                rate = 1.0 + jnp.tanh(2.5 * g - jnp.tanh(g))
                ks[x, j] = rate
                beside(x, j, q[x, j], rate)
        along_depth(q, lo + 2, hi - 2)

        def fill(x, j, v, w, acc, q_next=q_next):
            q_next[x, j] = v + (0.0375 * ms[x // tx, j]) * (acc - 4.0 * w * v)

        across(q, lo + 2, hi - 2, fill)
        q, q_next = q_next, q

    for src, out, field in ((hs, heat_out, 0), (q, pore_out, 1)):
        for r in range(rows):
            for j in span:
                v = src[DEEP + r, j]
                wide[r, pl.ds(j, SUB, stride=n), :] = 0.5 * v + 1.0 if field == 0 else v
        for i in range(2):
            for k in range(2):
                out[2 * i + k] = wide[i * tx : (i + 1) * tx, DEEP + k * ty : DEEP + (k + 1) * ty, :]
    for k in range(slot_ref.shape[1]):
        s = slot_ref[0, k]
        send_ref[k, 0] = encode(heat_out[s], HEAT_SCALE, HEAT_SHIFT)
        send_ref[k, 1] = encode(pore_out[s], PORE_SCALE, PORE_SHIFT)


def resend(count_ref, slot_ref, heat_ref, pore_ref, got_ref, send_ref):
    ranks = slot_ref.shape[1]
    for k in range(ranks):
        s = slot_ref[1, k]
        send_ref[k, 0] = encode(heat_ref[s], HEAT_SCALE, HEAT_SHIFT)
        send_ref[k, 1] = encode(pore_ref[s], PORE_SCALE, PORE_SHIFT)
        for r in range(ranks):

            @pl.when((r < count_ref[0]) & (slot_ref[0, r] == s))
            def _():
                send_ref[k] = got_ref[r]


def place(count_ref, slot_ref, heat_ref, pore_ref, first_ref, second_ref, heat_out, pore_out):
    ranks = slot_ref.shape[1]
    heat_out[...] = heat_ref[...]
    pore_out[...] = pore_ref[...]
    for i, got_ref in ((0, first_ref), (1, second_ref)):
        for r in range(ranks):

            @pl.when(r < count_ref[i])
            def _():
                s = slot_ref[i, r]
                heat_out[s] = decode(got_ref[r, 0], HEAT_SCALE, HEAT_SHIFT)
                pore_out[s] = decode(got_ref[r, 1], PORE_SCALE, PORE_SHIFT)


def call(body, spec, outs, scratch=(), name=None, out_space=pltpu.VMEM):
    def run(*args):
        space = {"s": pltpu.SMEM, "v": pltpu.VMEM, "V": pltpu.VMEM}
        args = [
            pltpu.with_memory_space_constraint(a, pltpu.VMEM) if c == "V" else a
            for c, a in zip(spec, args)
        ]
        shapes = [
            pltpu.VMEM(s, d) if out_space is not None else jax.ShapeDtypeStruct(s, d)
            for s, d in outs
        ]
        return pl.pallas_call(
            body,
            in_specs=[pl.BlockSpec(memory_space=space[c]) for c in spec],
            out_specs=[pl.BlockSpec(memory_space=pltpu.VMEM) for _ in outs],
            out_shape=shapes,
            scratch_shapes=list(scratch),
            compiler_params=pltpu.CompilerParams(vmem_limit_bytes=VMEM_LIMIT),
            name=name,
        )(*args)

    return run


def exchange(near, far, axis):
    n = lax.axis_size(axis)
    near_pairs = [(i, i ^ 1) for i in range(n) if i ^ 1 < n]
    far_pairs = [(i, ((i + 1) ^ 1) - 1) for i in range(1, n) if ((i + 1) ^ 1) - 1 < n]
    far = lax.ppermute(far, axis, far_pairs)
    near = lax.ppermute(near, axis, near_pairs)
    return near, far


def swap(value, axis):
    n = lax.axis_size(axis)
    return lax.ppermute(value, axis, [(i, (i + n // 2) % n) for i in range(n)])


def per_device(enthalpy, porosity, active, move_count, move_slot):
    rows, cols, depth = enthalpy.shape
    tx, ty = rows // 2, cols // 2
    count = move_count.reshape(2)
    slots = move_slot.reshape(2, move_slot.shape[-1])
    ranks = slots.shape[1]
    f32, bf16, i16 = jnp.float32, jnp.bfloat16, jnp.int16

    block = ((rows, cols, depth), f32)
    own, enthalpy, porosity = call(
        pack_x, "svv", [((2 * rows + 1, cols, depth), bf16), block, block], name="pack_x"
    )(active, enthalpy, porosity)
    x_near, x_far = exchange(own, own, "gx")
    side = ((6 * rows + 3, DEEP, depth), bf16)
    near, far = call(pack_y, "VVV", [side, side], name="pack_y")(own, x_near, x_far)
    y_near, y_far = exchange(near, far, "gy")
    total, width = rows + 2 * DEEP, cols + 2 * DEEP
    tiles = ((4, tx, ty, depth), f32)
    parcel = ((ranks, 2, tx, ty, depth), i16)
    split = pltpu.VMEM((total, width // SUB, SUB, depth), f32)
    heat, pore, first = call(
        step, "ssVVVVVV", [tiles, tiles, parcel],
        [pltpu.VMEM((total, width, depth), f32)]
        + [split] * 7
        + [pltpu.VMEM((total // tx, width // SUB, SUB, depth), f32)],
        name="step",
    )(active, slots, enthalpy, porosity, x_near, x_far, y_near, y_far)
    first = swap(first, "gx")
    (second,) = call(resend, "ssVVV", [parcel], name="resend")(count, slots, heat, pore, first)
    second = swap(second, "gy")
    heat, pore = call(place, "ssVVVV", [tiles, tiles], name="place", out_space=None)(
        count, slots, heat, pore, first, second
    )
    return heat[None, None], pore[None, None]


def solution(mesh):
    placed = (
        P("gx", "gy", None),
        P("gx", "gy", None),
        P("gx", "gy"),
        P("gx", "gy", None),
        P("gx", "gy", None, None),
    )
    out = P("gx", "gy", None, None, None, None)
    return jax.shard_map(
        per_device, mesh=mesh, in_specs=placed, out_specs=(out, out), check_vma=False
    )
```

```python
import jax
import jax.numpy as jnp
from jax import lax
from jax.experimental import pallas as pl
from jax.experimental.pallas import tpu as pltpu
from jax.sharding import PartitionSpec as P


PAIRS = 4
DEEP = 2 * PAIRS
SUB = 8
LANES = 128
VMEM_LIMIT = 16 * 2**20

HEAT_SCALE = 25000.0
HEAT_SHIFT = 32000.0
PORE_SCALE = 40000.0
PORE_SHIFT = 7000.0


def encode(values, scale, shift):
    return jnp.floor(values * scale + (0.5 - shift)).astype(jnp.int32).astype(jnp.int16)


def decode(codes, scale, shift):
    return (codes.astype(jnp.int32).astype(jnp.float32) + shift) * (1.0 / scale)


def flag_rows(active_ref, cols):
    lane = lax.broadcasted_iota(jnp.int32, (cols, LANES), 1)
    col = lax.broadcasted_iota(jnp.int32, (cols, LANES), 0)

    def flag(i):
        return jnp.where(col < cols // 2, active_ref[i, 0], active_ref[i, 1])

    return jnp.where(lane < LANES // 2, flag(0), flag(1)).astype(jnp.float32)


def mask_at(ranks):
    choose = lambda i, k, s: (i * ranks + k) * 4 + s
    taken = lambda i, r, s: 8 * ranks + (i * ranks + r) * 4 + s
    again = lambda k, r: 16 * ranks + k * ranks + r
    return choose, taken, again, 16 * ranks + ranks * ranks


def pack_x(
    active_ref, count_ref, slot_ref, heat_ref, pore_ref, out_ref, heat_out, pore_out, mask_ref
):
    rows, cols = heat_ref.shape[0], heat_ref.shape[1]
    ranks = slot_ref.shape[1]
    out_ref[0:rows] = heat_ref[...].astype(jnp.bfloat16)
    out_ref[rows : 2 * rows] = pore_ref[...].astype(jnp.bfloat16)
    out_ref[2 * rows] = flag_rows(active_ref, cols).astype(jnp.bfloat16)
    heat_out[...] = heat_ref[...]
    pore_out[...] = pore_ref[...]
    choose, taken, again, _ = mask_at(ranks)

    def put(row, holds):
        mask_ref[row] = jnp.full((SUB, LANES), jnp.where(holds, 1.0, 0.0), jnp.float32)

    for i in range(2):
        for k in range(ranks):
            for s in range(4):
                here = slot_ref[i, k] == s
                put(choose(i, k, s), here)
                put(taken(i, k, s), here & (k < count_ref[i]))
    for k in range(ranks):
        for r in range(ranks):
            put(again(k, r), (slot_ref[1, k] == slot_ref[0, r]) & (r < count_ref[0]))


def inner(axis):
    at = lax.axis_index(axis)
    return jnp.where((at > 0) & (at < lax.axis_size(axis) - 1), 1.0, 0.0).astype(jnp.float32)


def x_parts(own_ref, near_ref, far_ref):
    odd = lax.rem(lax.axis_index("gx"), 2)
    return ((2 - 2 * odd, near_ref), (1, own_ref), (2 * odd, far_ref))


def pack_y(own_ref, near_ref, far_ref, near_out, far_out):
    rows = (own_ref.shape[0] - 1) // 2
    cols = own_ref.shape[1]
    odd = lax.rem(lax.axis_index("gy"), 2)
    edge = cols - DEEP
    for out_ref, start in ((near_out, edge - edge * odd), (far_out, edge * odd)):
        at = pl.ds(pl.multiple_of(start, DEEP), DEEP)
        for i, part in x_parts(own_ref, near_ref, far_ref):
            for f in range(2):
                out_ref[pl.ds((3 * f + i) * rows, rows)] = part[pl.ds(f * rows, rows), at, :]
            out_ref[6 * rows + i] = part[2 * rows, at, :]


def step(
    own_ref, mask_ref, heat_ref, pore_ref, xn_ref, xf_ref, yn_ref, yf_ref,
    heat_out, pore_out, send_ref, later_ref, wide, hs, qa, qb, vs, ks, vz, wz, ms,
):
    rows, cols = heat_ref.shape[0], heat_ref.shape[1]
    tx, ty = rows // 2, cols // 2
    total = rows + 2 * DEEP
    width = cols + 2 * DEEP
    n = width // SUB
    span = range(n)
    lane = lax.broadcasted_iota(jnp.int32, (SUB, LANES), 1)
    lane_open = lane < LANES - 1
    low_half = lane < LANES // 2
    f32 = jnp.float32
    odd = lax.rem(lax.axis_index("gy"), 2)
    edge = width - DEEP
    y_parts = (
        (pl.ds(pl.multiple_of(edge - edge * odd, DEEP), DEEP), yn_ref, None),
        (pl.ds(pl.multiple_of(edge * odd, DEEP), DEEP), yf_ref, inner("gy")),
    )
    own = pl.ds(DEEP, cols)
    x_open = inner("gx")
    odd_x = lax.rem(lax.axis_index("gx"), 2)
    row_open = (
        jnp.where(odd_x == 0, x_open, 1.0),
        None,
        jnp.where(odd_x == 1, x_open, 1.0),
    )

    def scaled(v, *by):
        for s in by:
            v = v if s is None else v * s
        return v

    for (i, part), far in zip(x_parts(own_ref, xn_ref, xf_ref), (None, None, x_open)):
        wide[i, own, :] = scaled(part[2 * rows].astype(f32), far)
    for at, part, far in y_parts:
        for i in range(3):
            wide[i, at, :] = scaled(part[6 * rows + i].astype(f32), far, row_open[i])
    for i in range(3):
        for j in span:
            f = wide[i, pl.ds(j, SUB, stride=n), :]
            r = pltpu.roll(f, LANES // 2, 1)
            ms[2 * i, j] = jnp.where(low_half, f, r)
            ms[2 * i + 1, j] = jnp.where(low_half, r, f)

    for field, home_ref, into in ((0, heat_ref, hs), (1, pore_ref, qa)):
        for (i, part), far in zip(x_parts(None, xn_ref, xf_ref), (None, None, x_open)):
            for r in range(rows):
                if part is None:
                    mid = home_ref[r]
                else:
                    mid = scaled(part[field * rows + r].astype(f32), far)
                wide[i * rows + r, own, :] = mid
        for at, part, far in y_parts:
            for x in range(total):
                v = part[field * total + x].astype(f32)
                wide[x, at, :] = scaled(v, far, row_open[x // rows])
        for x in range(total):
            for j in span:
                v = wide[x, pl.ds(j, SUB, stride=n), :]
                into[x, j] = 2.0 * v - 2.0 if field == 0 else v

    def beside(x, j, v, w):
        vz[x, j] = pltpu.roll(v, LANES - 1, 1)
        wz[x, j] = pltpu.roll(w, LANES - 1, 1)

    def along_depth(val, lo, hi):
        for x in range(lo, hi):
            for j in span:
                f = (ks[x, j] + wz[x, j]) * (vz[x, j] - val[x, j])
                f = jnp.where(lane_open, f, 0.0)
                vz[x, j] = f - pltpu.roll(f, 1, 1)

    def across(val, lo, hi, finish):
        prev = [(ks[lo - 1, j] + ks[lo, j]) * (val[lo, j] - val[lo - 1, j]) for j in span]
        for x in range(lo, hi):
            v = [val[x, j] for j in span]
            w = [ks[x, j] for j in span]
            down = [(w[j] + ks[x + 1, j]) * (val[x + 1, j] - v[j]) for j in span]
            flux = [(w[j] + w[j + 1]) * (v[j + 1] - v[j]) for j in range(n - 1)]
            flux.append(
                (w[n - 1] + pltpu.roll(w[0], SUB - 1, 0)) * (pltpu.roll(v[0], SUB - 1, 0) - v[n - 1])
            )
            left = [pltpu.roll(flux[-1], 1, 0)] + flux[:-1]
            for j in span:
                acc = (down[j] - prev[j]) + (flux[j] - left[j]) + vz[x, j]
                finish(x, j, v[j], w[j], acc)
            prev = down

    q, q_next = qa, qb
    for p in range(PAIRS):
        lo, hi = 2 * p, total - 2 * p
        for x in range(lo, hi):
            for j in span:
                h = hs[x, j]
                t = jnp.tanh(h)
                solid = 1.0 - q[x, j]
                k = solid * solid * (t + 7.0 / 3.0)
                v = h - 0.4 * t
                ks[x, j] = k
                vs[x, j] = v
                beside(x, j, v, k)
        along_depth(vs, lo + 1, hi - 1)

        def warm(x, j, v, w, acc):
            hs[x, j] = hs[x, j] + (0.0225 * ms[x // tx, j]) * acc

        across(vs, lo + 1, hi - 1, warm)
        for x in range(lo + 1, hi - 1):
            for j in span:
                g = hs[x, j]
                rate = 1.0 + jnp.tanh(2.5 * g - jnp.tanh(g))
                ks[x, j] = rate
                beside(x, j, q[x, j], rate)
        along_depth(q, lo + 2, hi - 2)

        def fill(x, j, v, w, acc, q_next=q_next):
            q_next[x, j] = v + (0.0375 * ms[x // tx, j]) * (acc - 4.0 * w * v)

        across(q, lo + 2, hi - 2, fill)
        q, q_next = q_next, q

    for src, out, field in ((hs, heat_out, 0), (q, pore_out, 1)):
        for r in range(rows):
            for j in span:
                v = src[DEEP + r, j]
                wide[r, pl.ds(j, SUB, stride=n), :] = 0.5 * v + 1.0 if field == 0 else v
        for i in range(2):
            for k in range(2):
                out[2 * i + k] = wide[i * tx : (i + 1) * tx, DEEP + k * ty : DEEP + (k + 1) * ty, :]
    ranks = send_ref.shape[0]
    choose = mask_at(ranks)[0]
    shape = (tx, ty, LANES)
    for field, src, scale, shift in (
        (0, heat_out, HEAT_SCALE, HEAT_SHIFT),
        (1, pore_out, PORE_SCALE, PORE_SHIFT),
    ):
        for i, out in ((0, send_ref), (1, later_ref)):
            for k in range(ranks):
                v = src[0]
                for s in range(1, 4):
                    v = jnp.where(held(mask_ref, choose(i, k, s), shape), src[s], v)
                out[k, field] = encode(v, scale, shift)


def held(mask_ref, row, shape):
    m = mask_ref[row]
    m = jnp.concatenate([m] * (shape[1] // SUB), axis=0)
    return jnp.broadcast_to(m[None], shape) > 0.5


def resend(mask_ref, got_ref, local_ref, send_ref):
    ranks = got_ref.shape[0]
    shape = got_ref.shape[2:]
    again = mask_at(ranks)[2]
    for k in range(ranks):
        for f in range(2):
            v = local_ref[k, f].astype(jnp.int32)
            for r in range(ranks):
                v = jnp.where(
                    held(mask_ref, again(k, r), shape), got_ref[r, f].astype(jnp.int32), v
                )
            send_ref[k, f] = v.astype(jnp.int16)


def place(mask_ref, heat_ref, pore_ref, first_ref, second_ref, heat_out, pore_out):
    ranks = first_ref.shape[0]
    shape = first_ref.shape[2:]
    taken = mask_at(ranks)[1]
    for field, src, out, scale, shift in (
        (0, heat_ref, heat_out, HEAT_SCALE, HEAT_SHIFT),
        (1, pore_ref, pore_out, PORE_SCALE, PORE_SHIFT),
    ):
        came = [
            (i, r, decode(got[r, field], scale, shift))
            for i, got in ((0, first_ref), (1, second_ref))
            for r in range(ranks)
        ]
        for s in range(4):
            v = src[s]
            for i, r, tile in came:
                v = jnp.where(held(mask_ref, taken(i, r, s), shape), tile, v)
            out[s] = v


def call(body, spec, outs, scratch=(), out_space=pltpu.VMEM):
    def run(*args):
        space = {"s": pltpu.SMEM, "v": pltpu.VMEM, "V": pltpu.VMEM}
        args = [
            pltpu.with_memory_space_constraint(a, pltpu.VMEM if c == "V" else pltpu.HBM)
            for c, a in zip(spec, args)
        ]
        shapes = [
            pltpu.VMEM(s, d) if out_space is not None else jax.ShapeDtypeStruct(s, d)
            for s, d in outs
        ]
        return pl.pallas_call(
            body,
            in_specs=[pl.BlockSpec(memory_space=space[c]) for c in spec],
            out_specs=[pl.BlockSpec(memory_space=pltpu.VMEM) for _ in outs],
            out_shape=shapes,
            scratch_shapes=list(scratch),
            compiler_params=pltpu.CompilerParams(vmem_limit_bytes=VMEM_LIMIT),
        )(*args)

    return run


def exchange(near, far, axis):
    n = lax.axis_size(axis)
    near_pairs = [(i, i ^ 1) for i in range(n)]
    far_pairs = [(0, 0), (n - 1, n - 1)] + [(i, ((i + 1) ^ 1) - 1) for i in range(1, n - 1)]
    near = lax.ppermute(near, axis, near_pairs)
    far = lax.ppermute(far, axis, far_pairs)
    return near, far


def swap(value, axis):
    n = lax.axis_size(axis)
    return lax.ppermute(value, axis, [(i, (i + n // 2) % n) for i in range(n)])


def per_device(enthalpy, porosity, active, move_count, move_slot):
    rows, cols, depth = enthalpy.shape
    tx, ty = rows // 2, cols // 2
    count = move_count.reshape(2)
    slots = move_slot.reshape(2, move_slot.shape[-1])
    ranks = slots.shape[1]
    f32, bf16, i16 = jnp.float32, jnp.bfloat16, jnp.int16

    block = ((rows, cols, depth), f32)
    masks = ((mask_at(ranks)[3], SUB, LANES), f32)
    own, enthalpy, porosity, masks = call(
        pack_x, "sssvv", [((2 * rows + 1, cols, depth), bf16), block, block, masks]
    )(active, count, slots, enthalpy, porosity)
    x_near, x_far = exchange(own, own, "gx")
    side = ((6 * rows + 3, DEEP, depth), bf16)
    near, far = call(pack_y, "VVV", [side, side])(own, x_near, x_far)
    y_near, y_far = exchange(near, far, "gy")
    total, width = rows + 2 * DEEP, cols + 2 * DEEP
    tiles = ((4, tx, ty, depth), f32)
    parcel = ((ranks, 2, tx, ty, depth), i16)
    split = pltpu.VMEM((total, width // SUB, SUB, depth), f32)
    heat, pore, first, later = call(
        step, "VVVVVVVV", [tiles, tiles, parcel, parcel],
        [pltpu.VMEM((total, width, depth), f32)]
        + [split] * 7
        + [pltpu.VMEM((total // tx, width // SUB, SUB, depth), f32)],
    )(own, masks, enthalpy, porosity, x_near, x_far, y_near, y_far)
    first = swap(first, "gx")
    (second,) = call(resend, "VVV", [parcel])(masks, first, later)
    second = swap(second, "gy")
    heat, pore = call(place, "VVVVV", [tiles, tiles], out_space=None)(
        masks, heat, pore, first, second
    )
    return heat[None, None], pore[None, None]


def solution(mesh):
    placed = (
        P("gx", "gy", None),
        P("gx", "gy", None),
        P("gx", "gy"),
        P("gx", "gy", None),
        P("gx", "gy", None, None),
    )
    out = P("gx", "gy", None, None, None, None)

    return jax.shard_map(
        per_device, mesh=mesh, in_specs=placed, out_specs=(out, out), check_vma=False
    )
```

```python
import jax
import jax.numpy as jnp
from jax import lax
from jax.experimental import pallas as pl
from jax.experimental.pallas import tpu as pltpu
from jax.sharding import PartitionSpec as P


PAIRS = 4
DEEP = 2 * PAIRS
SUB = 8
LANES = 128
VMEM_LIMIT = 16 * 2**20

HEAT_SCALE = 25000.0
HEAT_SHIFT = 32000.0
PORE_SCALE = 40000.0
PORE_SHIFT = 7000.0


def encode(values, scale, shift):
    return jnp.floor(values * scale + (0.5 - shift)).astype(jnp.int32).astype(jnp.int16)


def decode(codes, scale, shift):
    return (codes.astype(jnp.int32).astype(jnp.float32) + shift) * (1.0 / scale)


def flag_rows(active_ref, cols):
    lane = lax.broadcasted_iota(jnp.int32, (cols, LANES), 1)
    col = lax.broadcasted_iota(jnp.int32, (cols, LANES), 0)

    def flag(i):
        return jnp.where(col < cols // 2, active_ref[i, 0], active_ref[i, 1])

    return jnp.where(lane < LANES // 2, flag(0), flag(1)).astype(jnp.float32)


def mask_at(ranks):
    choose = lambda i, k, s: (i * ranks + k) * 4 + s
    taken = lambda i, r, s: 8 * ranks + (i * ranks + r) * 4 + s
    again = lambda k, r: 16 * ranks + k * ranks + r
    return choose, taken, again, 16 * ranks + ranks * ranks


def pack_x(
    active_ref, count_ref, slot_ref, heat_ref, pore_ref, out_ref, heat_out, pore_out, mask_ref
):
    rows, cols = heat_ref.shape[0], heat_ref.shape[1]
    ranks = slot_ref.shape[1]
    out_ref[0:rows] = heat_ref[...].astype(jnp.bfloat16)
    out_ref[rows : 2 * rows] = pore_ref[...].astype(jnp.bfloat16)
    out_ref[2 * rows] = flag_rows(active_ref, cols).astype(jnp.bfloat16)
    heat_out[...] = heat_ref[...]
    pore_out[...] = pore_ref[...]
    choose, taken, again, _ = mask_at(ranks)

    def put(row, holds):
        mask_ref[row] = jnp.full((SUB, LANES), jnp.where(holds, 1.0, 0.0), jnp.float32)

    for i in range(2):
        for k in range(ranks):
            for s in range(4):
                here = slot_ref[i, k] == s
                put(choose(i, k, s), here)
                put(taken(i, k, s), here & (k < count_ref[i]))
    for k in range(ranks):
        for r in range(ranks):
            put(again(k, r), (slot_ref[1, k] == slot_ref[0, r]) & (r < count_ref[0]))


def inside(axis, below):
    at = lax.axis_index(axis)
    has = at < lax.axis_size(axis) - 1 if below else at > 0
    return jnp.where(has, 1.0, 0.0).astype(jnp.float32)


def x_parts(own_ref, first_ref, second_ref):
    odd = lax.rem(lax.axis_index("gx") + lax.axis_index("gy"), 2)
    return ((2 - 2 * odd, first_ref), (1, own_ref), (2 * odd, second_ref))


def pack_y(own_ref, first_ref, second_ref, near_out, far_out):
    rows = (own_ref.shape[0] - 1) // 2
    cols = own_ref.shape[1]
    odd = lax.rem(lax.axis_index("gy"), 2)
    edge = cols - DEEP
    for out_ref, start in ((near_out, edge - edge * odd), (far_out, edge * odd)):
        at = pl.ds(pl.multiple_of(start, DEEP), DEEP)
        for i, part in x_parts(own_ref, first_ref, second_ref):
            for f in range(2):
                out_ref[pl.ds((3 * f + i) * rows, rows)] = part[pl.ds(f * rows, rows), at, :]
            out_ref[6 * rows + i] = part[2 * rows, at, :]


def step(
    own_ref, mask_ref, heat_ref, pore_ref, xn_ref, xf_ref, yn_ref, yf_ref,
    heat_out, pore_out, send_ref, later_ref, wide, hs, qa, qb, vs, ks, vz, wz, ms,
):
    rows, cols = heat_ref.shape[0], heat_ref.shape[1]
    tx, ty = rows // 2, cols // 2
    total = rows + 2 * DEEP
    width = cols + 2 * DEEP
    n = width // SUB
    span = range(n)
    lane = lax.broadcasted_iota(jnp.int32, (SUB, LANES), 1)
    lane_open = lane < LANES - 1
    low_half = lane < LANES // 2
    f32 = jnp.float32
    odd = lax.rem(lax.axis_index("gy"), 2)
    edge = width - DEEP
    y_parts = (
        (pl.ds(pl.multiple_of(edge - edge * odd, DEEP), DEEP), yn_ref, None),
        (
            pl.ds(pl.multiple_of(edge * odd, DEEP), DEEP),
            yf_ref,
            jnp.where(odd == 1, inside("gy", True), inside("gy", False)),
        ),
    )
    own = pl.ds(DEEP, cols)
    row_open = (inside("gx", False), None, inside("gx", True))

    def scaled(v, by):
        return v if by is None else v * by

    for i, part in x_parts(own_ref, xn_ref, xf_ref):
        wide[i, own, :] = part[2 * rows].astype(f32)
    for at, part, far in y_parts:
        for i in range(3):
            wide[i, at, :] = scaled(part[6 * rows + i].astype(f32), far)
    for i in range(3):
        for j in span:
            f = scaled(wide[i, pl.ds(j, SUB, stride=n), :], row_open[i])
            r = pltpu.roll(f, LANES // 2, 1)
            ms[2 * i, j] = jnp.where(low_half, f, r)
            ms[2 * i + 1, j] = jnp.where(low_half, r, f)

    for field, home_ref, into in ((0, heat_ref, hs), (1, pore_ref, qa)):
        for i, part in x_parts(None, xn_ref, xf_ref):
            for r in range(rows):
                mid = home_ref[r] if part is None else part[field * rows + r].astype(f32)
                wide[i * rows + r, own, :] = mid
        for at, part, far in y_parts:
            for x in range(total):
                wide[x, at, :] = scaled(part[field * total + x].astype(f32), far)
        for x in range(total):
            for j in span:
                v = scaled(wide[x, pl.ds(j, SUB, stride=n), :], row_open[x // rows])
                into[x, j] = 2.0 * v - 2.0 if field == 0 else v

    def beside(x, j, v, w):
        vz[x, j] = pltpu.roll(v, LANES - 1, 1)
        wz[x, j] = pltpu.roll(w, LANES - 1, 1)

    def along_depth(val, lo, hi):
        for x in range(lo, hi):
            for j in span:
                f = (ks[x, j] + wz[x, j]) * (vz[x, j] - val[x, j])
                f = jnp.where(lane_open, f, 0.0)
                vz[x, j] = f - pltpu.roll(f, 1, 1)

    def across(val, lo, hi, finish):
        prev = [(ks[lo - 1, j] + ks[lo, j]) * (val[lo, j] - val[lo - 1, j]) for j in span]
        for x in range(lo, hi):
            v = [val[x, j] for j in span]
            w = [ks[x, j] for j in span]
            down = [(w[j] + ks[x + 1, j]) * (val[x + 1, j] - v[j]) for j in span]
            flux = [(w[j] + w[j + 1]) * (v[j + 1] - v[j]) for j in range(n - 1)]
            flux.append(
                (w[n - 1] + pltpu.roll(w[0], SUB - 1, 0)) * (pltpu.roll(v[0], SUB - 1, 0) - v[n - 1])
            )
            left = [pltpu.roll(flux[-1], 1, 0)] + flux[:-1]
            for j in span:
                acc = (down[j] - prev[j]) + (flux[j] - left[j]) + vz[x, j]
                finish(x, j, v[j], w[j], acc)
            prev = down

    q, q_next = qa, qb
    for p in range(PAIRS):
        lo, hi = 2 * p, total - 2 * p
        for x in range(lo, hi):
            for j in span:
                h = hs[x, j]
                t = jnp.tanh(h)
                solid = 1.0 - q[x, j]
                k = solid * solid * (t + 7.0 / 3.0)
                v = h - 0.4 * t
                ks[x, j] = k
                vs[x, j] = v
                beside(x, j, v, k)
        along_depth(vs, lo + 1, hi - 1)

        def warm(x, j, v, w, acc):
            hs[x, j] = hs[x, j] + (0.0225 * ms[x // tx, j]) * acc

        across(vs, lo + 1, hi - 1, warm)
        for x in range(lo + 1, hi - 1):
            for j in span:
                g = hs[x, j]
                rate = 1.0 + jnp.tanh(2.5 * g - jnp.tanh(g))
                ks[x, j] = rate
                beside(x, j, q[x, j], rate)
        along_depth(q, lo + 2, hi - 2)

        def fill(x, j, v, w, acc, q_next=q_next):
            q_next[x, j] = v + (0.0375 * ms[x // tx, j]) * (acc - 4.0 * w * v)

        across(q, lo + 2, hi - 2, fill)
        q, q_next = q_next, q

    for src, out, field in ((hs, heat_out, 0), (q, pore_out, 1)):
        for r in range(rows):
            for j in span:
                v = src[DEEP + r, j]
                wide[r, pl.ds(j, SUB, stride=n), :] = 0.5 * v + 1.0 if field == 0 else v
        for i in range(2):
            for k in range(2):
                out[2 * i + k] = wide[i * tx : (i + 1) * tx, DEEP + k * ty : DEEP + (k + 1) * ty, :]
    ranks = send_ref.shape[0]
    choose = mask_at(ranks)[0]
    shape = (tx, ty, LANES)
    for field, src, scale, shift in (
        (0, heat_out, HEAT_SCALE, HEAT_SHIFT),
        (1, pore_out, PORE_SCALE, PORE_SHIFT),
    ):
        for i, out in ((0, send_ref), (1, later_ref)):
            for k in range(ranks):
                v = src[0]
                for s in range(1, 4):
                    v = jnp.where(held(mask_ref, choose(i, k, s), shape), src[s], v)
                out[k, field] = encode(v, scale, shift)


def held(mask_ref, row, shape):
    m = mask_ref[row]
    m = jnp.concatenate([m] * (shape[1] // SUB), axis=0)
    return jnp.broadcast_to(m[None], shape) > 0.5


def resend(mask_ref, got_ref, local_ref, send_ref):
    ranks = got_ref.shape[0]
    shape = got_ref.shape[2:]
    again = mask_at(ranks)[2]
    for k in range(ranks):
        for f in range(2):
            v = local_ref[k, f].astype(jnp.int32)
            for r in range(ranks):
                v = jnp.where(
                    held(mask_ref, again(k, r), shape), got_ref[r, f].astype(jnp.int32), v
                )
            send_ref[k, f] = v.astype(jnp.int16)


def place(mask_ref, heat_ref, pore_ref, first_ref, second_ref, heat_out, pore_out):
    ranks = first_ref.shape[0]
    shape = first_ref.shape[2:]
    taken = mask_at(ranks)[1]
    for field, src, out, scale, shift in (
        (0, heat_ref, heat_out, HEAT_SCALE, HEAT_SHIFT),
        (1, pore_ref, pore_out, PORE_SCALE, PORE_SHIFT),
    ):
        came = [
            (i, r, decode(got[r, field], scale, shift))
            for i, got in ((0, first_ref), (1, second_ref))
            for r in range(ranks)
        ]
        for s in range(4):
            v = src[s]
            for i, r, tile in came:
                v = jnp.where(held(mask_ref, taken(i, r, s), shape), tile, v)
            out[s] = v


def call(body, spec, outs, scratch=(), out_space=pltpu.VMEM):
    def run(*args):
        space = {"s": pltpu.SMEM, "v": pltpu.VMEM, "V": pltpu.VMEM}
        args = [
            pltpu.with_memory_space_constraint(a, pltpu.VMEM if c == "V" else pltpu.HBM)
            for c, a in zip(spec, args)
        ]
        shapes = [
            pltpu.VMEM(s, d) if out_space is not None else jax.ShapeDtypeStruct(s, d)
            for s, d in outs
        ]
        return pl.pallas_call(
            body,
            in_specs=[pl.BlockSpec(memory_space=space[c]) for c in spec],
            out_specs=[pl.BlockSpec(memory_space=pltpu.VMEM) for _ in outs],
            out_shape=shapes,
            scratch_shapes=list(scratch),
            compiler_params=pltpu.CompilerParams(vmem_limit_bytes=VMEM_LIMIT),
        )(*args)

    return run


def permute(value, partner):
    nx, ny = lax.axis_size("gx"), lax.axis_size("gy")
    pairs = []
    for x in range(nx):
        for y in range(ny):
            u, v = partner(x, y)
            pairs.append((x * ny + y, u * ny + v))
    return lax.ppermute(value, ("gx", "gy"), pairs)


def exchange_x(value):
    nx, ny = lax.axis_size("gx"), lax.axis_size("gy")

    def partner(x, y, near):
        if near:
            return x ^ 1, y
        if 0 < x < nx - 1:
            return ((x + 1) ^ 1) - 1, y
        return (x, y ^ 2) if ny % 4 == 0 else (x, y)

    first = permute(value, lambda x, y: partner(x, y, y % 2 == 0))
    second = permute(value, lambda x, y: partner(x, y, y % 2 == 1))
    return first, second


def exchange_y(near, far):
    ny = lax.axis_size("gy")

    def partner(x, y):
        if 0 < y < ny - 1:
            return x, ((y + 1) ^ 1) - 1
        return x ^ 1, y

    far = permute(far, partner)
    near = permute(near, lambda x, y: (x, y ^ 1))
    return near, far


def swap(value, axis):
    n = lax.axis_size(axis)
    return lax.ppermute(value, axis, [(i, (i + n // 2) % n) for i in range(n)])


def per_device(enthalpy, porosity, active, move_count, move_slot):
    rows, cols, depth = enthalpy.shape
    tx, ty = rows // 2, cols // 2
    count = move_count.reshape(2)
    slots = move_slot.reshape(2, move_slot.shape[-1])
    ranks = slots.shape[1]
    f32, bf16, i16 = jnp.float32, jnp.bfloat16, jnp.int16

    block = ((rows, cols, depth), f32)
    masks = ((mask_at(ranks)[3], SUB, LANES), f32)
    own, enthalpy, porosity, masks = call(
        pack_x, "sssvv", [((2 * rows + 1, cols, depth), bf16), block, block, masks]
    )(active, count, slots, enthalpy, porosity)
    x_near, x_far = exchange_x(own)
    side = ((6 * rows + 3, DEEP, depth), bf16)
    near, far = call(pack_y, "VVV", [side, side])(own, x_near, x_far)
    y_near, y_far = exchange_y(near, far)
    total, width = rows + 2 * DEEP, cols + 2 * DEEP
    tiles = ((4, tx, ty, depth), f32)
    parcel = ((ranks, 2, tx, ty, depth), i16)
    split = pltpu.VMEM((total, width // SUB, SUB, depth), f32)
    heat, pore, first, later = call(
        step, "VVVVVVVV", [tiles, tiles, parcel, parcel],
        [pltpu.VMEM((total, width, depth), f32)]
        + [split] * 7
        + [pltpu.VMEM((total // tx, width // SUB, SUB, depth), f32)],
    )(own, masks, enthalpy, porosity, x_near, x_far, y_near, y_far)
    first = swap(first, "gx")
    (second,) = call(resend, "VVV", [parcel])(masks, first, later)
    second = swap(second, "gy")
    heat, pore = call(place, "VVVVV", [tiles, tiles], out_space=None)(
        masks, heat, pore, first, second
    )
    return heat[None, None], pore[None, None]


def solution(mesh):
    placed = (
        P("gx", "gy", None),
        P("gx", "gy", None),
        P("gx", "gy"),
        P("gx", "gy", None),
        P("gx", "gy", None, None),
    )
    out = P("gx", "gy", None, None, None, None)

    return jax.shard_map(
        per_device, mesh=mesh, in_specs=placed, out_specs=(out, out), check_vma=False
    )
```

```python
import jax
import jax.numpy as jnp
from jax import lax
from jax.experimental import pallas as pl
from jax.experimental.pallas import tpu as pltpu
from jax.sharding import PartitionSpec as P


PAIRS = 4
DEEP = 2 * PAIRS
SUB = 8
LANES = 128
VMEM_LIMIT = 16 * 2**20

HEAT_SCALE = 25000.0
HEAT_SHIFT = 32000.0
PORE_SCALE = 40000.0
PORE_SHIFT = 7000.0


def encode(values, scale, shift):
    return jnp.floor(values * scale + (0.5 - shift)).astype(jnp.int32).astype(jnp.int16)


def decode(codes, scale, shift):
    return (codes.astype(jnp.int32).astype(jnp.float32) + shift) * (1.0 / scale)


def flag_rows(active_ref, cols):
    lane = lax.broadcasted_iota(jnp.int32, (cols, LANES), 1)
    col = lax.broadcasted_iota(jnp.int32, (cols, LANES), 0)

    def flag(i):
        return jnp.where(col < cols // 2, active_ref[i, 0], active_ref[i, 1])

    return jnp.where(lane < LANES // 2, flag(0), flag(1)).astype(jnp.float32)


def mask_at(ranks):
    choose = lambda i, k, s: (i * ranks + k) * 4 + s
    taken = lambda i, r, s: 8 * ranks + (i * ranks + r) * 4 + s
    again = lambda k, r: 16 * ranks + k * ranks + r
    return choose, taken, again, 16 * ranks + ranks * ranks


def pack_x(
    active_ref, count_ref, slot_ref, heat_ref, pore_ref, out_ref, heat_out, pore_out, mask_ref
):
    rows, cols = heat_ref.shape[0], heat_ref.shape[1]
    ranks = slot_ref.shape[1]
    out_ref[0:rows] = heat_ref[...].astype(jnp.bfloat16)
    out_ref[rows : 2 * rows] = pore_ref[...].astype(jnp.bfloat16)
    out_ref[2 * rows] = flag_rows(active_ref, cols).astype(jnp.bfloat16)
    heat_out[...] = heat_ref[...]
    pore_out[...] = pore_ref[...]
    choose, taken, again, _ = mask_at(ranks)

    def put(row, holds):
        mask_ref[row] = jnp.full((SUB, LANES), jnp.where(holds, 1.0, 0.0), jnp.float32)

    for i in range(2):
        for k in range(ranks):
            for s in range(4):
                here = slot_ref[i, k] == s
                put(choose(i, k, s), here)
                put(taken(i, k, s), here & (k < count_ref[i]))
    for k in range(ranks):
        for r in range(ranks):
            put(again(k, r), (slot_ref[1, k] == slot_ref[0, r]) & (r < count_ref[0]))


def inside(axis, below):
    at = lax.axis_index(axis)
    has = at < lax.axis_size(axis) - 1 if below else at > 0
    return jnp.where(has, 1.0, 0.0).astype(jnp.float32)


def x_parts(own_ref, first_ref, second_ref):
    odd = lax.rem(lax.axis_index("gx") + lax.axis_index("gy"), 2)
    return ((2 - 2 * odd, first_ref), (1, own_ref), (2 * odd, second_ref))


def pack_y(own_ref, first_ref, second_ref, near_out, far_out):
    rows = (own_ref.shape[0] - 1) // 2
    cols = own_ref.shape[1]
    side = 2 * rows
    odd = lax.rem(lax.axis_index("gy"), 2)
    edge = cols - DEEP
    sub = lax.broadcasted_iota(jnp.int32, (DEEP, LANES), 0)
    sides = ((near_out, edge - edge * odd, odd == 0), (far_out, edge * odd, odd == 1))
    for out_ref, start, right in sides:
        at = pl.ds(pl.multiple_of(start, DEEP), DEEP)
        flags = jnp.zeros((DEEP, LANES), jnp.float32)
        for i, part in x_parts(own_ref, first_ref, second_ref):
            flags = jnp.where(sub == i, part[2 * rows, at, :].astype(jnp.float32), flags)
            for f in range(2):
                if part is own_ref:
                    out_ref[pl.ds(f * side, rows)] = part[pl.ds(f * rows, rows), at, :]
                    continue
                for d in range(1, rows // 2 + 1):
                    a, b = (
                        part[f * rows + jnp.where(i == 0, rows - e, e - 1), at, :].astype(jnp.float32)
                        for e in (d, rows - d)
                    )
                    if d < rows - d:
                        a = jnp.where(
                            right,
                            jnp.where(sub >= d, a, pltpu.roll(b, d, 0)),
                            jnp.where(sub < DEEP - d, a, pltpu.roll(b, DEEP - d, 0)),
                        )
                    out_ref[f * side + rows + (i // 2) * (rows // 2) + d - 1] = a.astype(jnp.bfloat16)
        out_ref[2 * side] = flags.astype(jnp.bfloat16)


def edge_row(part, field, x, rows, right):
    side = 2 * rows
    if rows <= x < 2 * rows:
        return part[field * side + x - rows].astype(jnp.float32)
    d = rows - x if x < rows else x - 2 * rows + 1
    at = field * side + rows + (0 if x < rows else rows // 2) - 1
    if d <= rows // 2:
        return part[at + d].astype(jnp.float32)
    if d == rows:
        return part[at + rows // 2].astype(jnp.float32)
    v = part[at + rows - d].astype(jnp.float32)
    return jnp.where(right, pltpu.roll(v, d, 0), pltpu.roll(v, DEEP - d, 0))


def step(
    own_ref, mask_ref, heat_ref, pore_ref, xn_ref, xf_ref, yn_ref, yf_ref,
    heat_out, pore_out, send_ref, later_ref, wide, hs, qa, qb, vs, ks, vz, wz, ms,
):
    rows, cols = heat_ref.shape[0], heat_ref.shape[1]
    tx, ty = rows // 2, cols // 2
    total = rows + 2 * DEEP
    width = cols + 2 * DEEP
    n = width // SUB
    span = range(n)
    lane = lax.broadcasted_iota(jnp.int32, (SUB, LANES), 1)
    lane_open = lane < LANES - 1
    low_half = lane < LANES // 2
    f32 = jnp.float32
    odd = lax.rem(lax.axis_index("gy"), 2)
    edge = width - DEEP
    y_parts = (
        (pl.ds(pl.multiple_of(edge - edge * odd, DEEP), DEEP), yn_ref, None, odd == 1),
        (
            pl.ds(pl.multiple_of(edge * odd, DEEP), DEEP),
            yf_ref,
            jnp.where(odd == 1, inside("gy", True), inside("gy", False)),
            odd == 0,
        ),
    )
    own = pl.ds(DEEP, cols)
    row_open = (inside("gx", False), None, inside("gx", True))

    def scaled(v, by):
        return v if by is None else v * by

    for i, part in x_parts(own_ref, xn_ref, xf_ref):
        wide[i, own, :] = part[2 * rows].astype(f32)
    for at, part, far, _ in y_parts:
        marks = scaled(part[4 * rows].astype(f32), far)
        for i in range(3):
            wide[i, at, :] = jnp.broadcast_to(marks[i : i + 1], (DEEP, LANES))
    for i in range(3):
        for j in span:
            f = scaled(wide[i, pl.ds(j, SUB, stride=n), :], row_open[i])
            r = pltpu.roll(f, LANES // 2, 1)
            ms[2 * i, j] = jnp.where(low_half, f, r)
            ms[2 * i + 1, j] = jnp.where(low_half, r, f)

    for field, home_ref, into in ((0, heat_ref, hs), (1, pore_ref, qa)):
        for i, part in x_parts(None, xn_ref, xf_ref):
            for r in range(rows):
                mid = home_ref[r] if part is None else part[field * rows + r].astype(f32)
                wide[i * rows + r, own, :] = mid
        for at, part, far, right in y_parts:
            for x in range(total):
                wide[x, at, :] = scaled(edge_row(part, field, x, rows, right), far)
        for x in range(total):
            for j in span:
                v = scaled(wide[x, pl.ds(j, SUB, stride=n), :], row_open[x // rows])
                into[x, j] = 2.0 * v - 2.0 if field == 0 else v

    def beside(x, j, v, w):
        vz[x, j] = pltpu.roll(v, LANES - 1, 1)
        wz[x, j] = pltpu.roll(w, LANES - 1, 1)

    def along_depth(val, lo, hi):
        for x in range(lo, hi):
            for j in span:
                f = (ks[x, j] + wz[x, j]) * (vz[x, j] - val[x, j])
                f = jnp.where(lane_open, f, 0.0)
                vz[x, j] = f - pltpu.roll(f, 1, 1)

    def across(val, lo, hi, finish):
        prev = [(ks[lo - 1, j] + ks[lo, j]) * (val[lo, j] - val[lo - 1, j]) for j in span]
        for x in range(lo, hi):
            v = [val[x, j] for j in span]
            w = [ks[x, j] for j in span]
            down = [(w[j] + ks[x + 1, j]) * (val[x + 1, j] - v[j]) for j in span]
            flux = [(w[j] + w[j + 1]) * (v[j + 1] - v[j]) for j in range(n - 1)]
            flux.append(
                (w[n - 1] + pltpu.roll(w[0], SUB - 1, 0)) * (pltpu.roll(v[0], SUB - 1, 0) - v[n - 1])
            )
            left = [pltpu.roll(flux[-1], 1, 0)] + flux[:-1]
            for j in span:
                acc = (down[j] - prev[j]) + (flux[j] - left[j]) + vz[x, j]
                finish(x, j, v[j], w[j], acc)
            prev = down

    q, q_next = qa, qb
    for p in range(PAIRS):
        lo, hi = 2 * p, total - 2 * p
        for x in range(lo, hi):
            for j in span:
                h = hs[x, j]
                t = jnp.tanh(h)
                solid = 1.0 - q[x, j]
                k = solid * solid * (t + 7.0 / 3.0)
                v = h - 0.4 * t
                ks[x, j] = k
                vs[x, j] = v
                if lo < x < hi - 1:
                    beside(x, j, v, k)
        along_depth(vs, lo + 1, hi - 1)

        def warm(x, j, v, w, acc):
            hs[x, j] = hs[x, j] + (0.0225 * ms[x // tx, j]) * acc

        across(vs, lo + 1, hi - 1, warm)
        for x in range(lo + 1, hi - 1):
            for j in span:
                g = hs[x, j]
                rate = 1.0 + jnp.tanh(2.5 * g - jnp.tanh(g))
                ks[x, j] = rate
                if lo + 1 < x < hi - 2:
                    beside(x, j, q[x, j], rate)
        along_depth(q, lo + 2, hi - 2)

        def fill(x, j, v, w, acc, q_next=q_next):
            q_next[x, j] = v + (0.0375 * ms[x // tx, j]) * (acc - 4.0 * w * v)

        across(q, lo + 2, hi - 2, fill)
        q, q_next = q_next, q

    for src, out, field in ((hs, heat_out, 0), (q, pore_out, 1)):
        for r in range(rows):
            for j in span:
                v = src[DEEP + r, j]
                wide[r, pl.ds(j, SUB, stride=n), :] = 0.5 * v + 1.0 if field == 0 else v
        for i in range(2):
            for k in range(2):
                out[2 * i + k] = wide[i * tx : (i + 1) * tx, DEEP + k * ty : DEEP + (k + 1) * ty, :]
    ranks = send_ref.shape[0]
    choose = mask_at(ranks)[0]
    shape = (tx, ty, LANES)
    for field, src, scale, shift in (
        (0, heat_out, HEAT_SCALE, HEAT_SHIFT),
        (1, pore_out, PORE_SCALE, PORE_SHIFT),
    ):
        for i, out in ((0, send_ref), (1, later_ref)):
            for k in range(ranks):
                v = src[0]
                for s in range(1, 4):
                    v = jnp.where(held(mask_ref, choose(i, k, s), shape), src[s], v)
                out[k, field] = encode(v, scale, shift)


def held(mask_ref, row, shape):
    m = mask_ref[row]
    m = jnp.concatenate([m] * (shape[1] // SUB), axis=0)
    return jnp.broadcast_to(m[None], shape) > 0.5


def resend(mask_ref, got_ref, local_ref, send_ref):
    ranks = got_ref.shape[0]
    shape = got_ref.shape[2:]
    again = mask_at(ranks)[2]
    for k in range(ranks):
        for f in range(2):
            v = local_ref[k, f].astype(jnp.int32)
            for r in range(ranks):
                v = jnp.where(
                    held(mask_ref, again(k, r), shape), got_ref[r, f].astype(jnp.int32), v
                )
            send_ref[k, f] = v.astype(jnp.int16)


def place(mask_ref, heat_ref, pore_ref, first_ref, second_ref, heat_out, pore_out):
    ranks = first_ref.shape[0]
    shape = first_ref.shape[2:]
    taken = mask_at(ranks)[1]
    for field, src, out, scale, shift in (
        (0, heat_ref, heat_out, HEAT_SCALE, HEAT_SHIFT),
        (1, pore_ref, pore_out, PORE_SCALE, PORE_SHIFT),
    ):
        came = [
            (i, r, decode(got[r, field], scale, shift))
            for i, got in ((0, first_ref), (1, second_ref))
            for r in range(ranks)
        ]
        for s in range(4):
            v = src[s]
            for i, r, tile in came:
                v = jnp.where(held(mask_ref, taken(i, r, s), shape), tile, v)
            out[s] = v


def call(body, spec, outs, scratch=(), out_space=pltpu.VMEM):
    def run(*args):
        space = {"s": pltpu.SMEM, "v": pltpu.VMEM, "V": pltpu.VMEM}
        args = [
            pltpu.with_memory_space_constraint(a, pltpu.VMEM if c == "V" else pltpu.HBM)
            for c, a in zip(spec, args)
        ]
        shapes = [
            pltpu.VMEM(s, d) if out_space is not None else jax.ShapeDtypeStruct(s, d)
            for s, d in outs
        ]
        return pl.pallas_call(
            body,
            in_specs=[pl.BlockSpec(memory_space=space[c]) for c in spec],
            out_specs=[pl.BlockSpec(memory_space=pltpu.VMEM) for _ in outs],
            out_shape=shapes,
            scratch_shapes=list(scratch),
            compiler_params=pltpu.CompilerParams(vmem_limit_bytes=VMEM_LIMIT),
        )(*args)

    return run


def permute(value, partner):
    nx, ny = lax.axis_size("gx"), lax.axis_size("gy")
    pairs = []
    for x in range(nx):
        for y in range(ny):
            u, v = partner(x, y)
            pairs.append((x * ny + y, u * ny + v))
    return lax.ppermute(value, ("gx", "gy"), pairs)


def exchange_x(value):
    nx, ny = lax.axis_size("gx"), lax.axis_size("gy")

    def partner(x, y, near):
        if near:
            return x ^ 1, y
        if 0 < x < nx - 1:
            return ((x + 1) ^ 1) - 1, y
        return (x, y ^ 2) if ny % 4 == 0 else (x, y)

    first = permute(value, lambda x, y: partner(x, y, y % 2 == 0))
    second = permute(value, lambda x, y: partner(x, y, y % 2 == 1))
    return first, second


def exchange_y(near, far):
    ny = lax.axis_size("gy")

    def partner(x, y):
        if 0 < y < ny - 1:
            return x, ((y + 1) ^ 1) - 1
        return x ^ 1, y

    far = permute(far, partner)
    near = permute(near, lambda x, y: (x, y ^ 1))
    return near, far


def swap(value, axis):
    n = lax.axis_size(axis)
    return lax.ppermute(value, axis, [(i, (i + n // 2) % n) for i in range(n)])


def per_device(enthalpy, porosity, active, move_count, move_slot):
    rows, cols, depth = enthalpy.shape
    tx, ty = rows // 2, cols // 2
    count = move_count.reshape(2)
    slots = move_slot.reshape(2, move_slot.shape[-1])
    ranks = slots.shape[1]
    f32, bf16, i16 = jnp.float32, jnp.bfloat16, jnp.int16

    block = ((rows, cols, depth), f32)
    masks = ((mask_at(ranks)[3], SUB, LANES), f32)
    own, enthalpy, porosity, masks = call(
        pack_x, "sssvv", [((2 * rows + 1, cols, depth), bf16), block, block, masks]
    )(active, count, slots, enthalpy, porosity)
    x_near, x_far = exchange_x(own)
    side = ((4 * rows + 1, DEEP, depth), bf16)
    near, far = call(pack_y, "VVV", [side, side])(own, x_near, x_far)
    y_near, y_far = exchange_y(near, far)
    total, width = rows + 2 * DEEP, cols + 2 * DEEP
    tiles = ((4, tx, ty, depth), f32)
    parcel = ((ranks, 2, tx, ty, depth), i16)
    split = pltpu.VMEM((total, width // SUB, SUB, depth), f32)
    heat, pore, first, later = call(
        step, "VVVVVVVV", [tiles, tiles, parcel, parcel],
        [pltpu.VMEM((total, width, depth), f32)]
        + [split] * 7
        + [pltpu.VMEM((total // tx, width // SUB, SUB, depth), f32)],
    )(own, masks, enthalpy, porosity, x_near, x_far, y_near, y_far)
    first = swap(first, "gx")
    (second,) = call(resend, "VVV", [parcel])(masks, first, later)
    second = swap(second, "gy")
    heat, pore = call(place, "VVVVV", [tiles, tiles], out_space=None)(
        masks, heat, pore, first, second
    )
    return heat[None, None], pore[None, None]


def solution(mesh):
    placed = (
        P("gx", "gy", None),
        P("gx", "gy", None),
        P("gx", "gy"),
        P("gx", "gy", None),
        P("gx", "gy", None, None),
    )
    out = P("gx", "gy", None, None, None, None)

    return jax.shard_map(
        per_device, mesh=mesh, in_specs=placed, out_specs=(out, out), check_vma=False
    )
```

```python
import jax
import jax.numpy as jnp
from jax import lax
from jax.experimental import pallas as pl
from jax.experimental.pallas import tpu as pltpu
from jax.sharding import PartitionSpec as P


PAIRS = 4
DEEP = 2 * PAIRS
SUB = 8
LANES = 128
VMEM_LIMIT = 16 * 2**20

HEAT_SCALE = 25000.0
HEAT_SHIFT = 32000.0
PORE_SCALE = 40000.0
PORE_SHIFT = 7000.0


def encode(values, scale, shift):
    return jnp.floor(values * scale + (0.5 - shift)).astype(jnp.int32).astype(jnp.int16)


def decode(codes, scale, shift):
    return (codes.astype(jnp.int32).astype(jnp.float32) + shift) * (1.0 / scale)


def flag_rows(active_ref, cols):
    lane = lax.broadcasted_iota(jnp.int32, (cols, LANES), 1)
    col = lax.broadcasted_iota(jnp.int32, (cols, LANES), 0)

    def flag(i):
        return jnp.where(col < cols // 2, active_ref[i, 0], active_ref[i, 1])

    return jnp.where(lane < LANES // 2, flag(0), flag(1)).astype(jnp.float32)


def mask_at(ranks):
    choose = lambda i, k, s: (i * ranks + k) * 4 + s
    taken = lambda i, r, s: 8 * ranks + (i * ranks + r) * 4 + s
    again = lambda k, r: 16 * ranks + k * ranks + r
    return choose, taken, again, 16 * ranks + ranks * ranks


def pack_x(
    active_ref, count_ref, slot_ref, heat_ref, pore_ref, out_ref, heat_out, pore_out, mask_ref
):
    rows, cols = heat_ref.shape[0], heat_ref.shape[1]
    ranks = slot_ref.shape[1]
    out_ref[0:rows] = heat_ref[...].astype(jnp.bfloat16)
    out_ref[rows : 2 * rows] = pore_ref[...].astype(jnp.bfloat16)
    out_ref[2 * rows] = flag_rows(active_ref, cols).astype(jnp.bfloat16)
    heat_out[...] = heat_ref[...]
    pore_out[...] = pore_ref[...]
    choose, taken, again, _ = mask_at(ranks)

    def put(row, holds):
        mask_ref[row] = jnp.full((SUB, LANES), jnp.where(holds, 1.0, 0.0), jnp.float32)

    for i in range(2):
        for k in range(ranks):
            for s in range(4):
                here = slot_ref[i, k] == s
                put(choose(i, k, s), here)
                put(taken(i, k, s), here & (k < count_ref[i]))
    for k in range(ranks):
        for r in range(ranks):
            put(again(k, r), (slot_ref[1, k] == slot_ref[0, r]) & (r < count_ref[0]))


def inside(axis, below):
    at = lax.axis_index(axis)
    has = at < lax.axis_size(axis) - 1 if below else at > 0
    return jnp.where(has, 1.0, 0.0).astype(jnp.float32)


def x_parts(own_ref, first_ref, second_ref):
    odd = lax.rem(lax.axis_index("gx") + lax.axis_index("gy"), 2)
    return ((2 - 2 * odd, first_ref), (1, own_ref), (2 * odd, second_ref))


def pack_y(own_ref, first_ref, second_ref, near_out, far_out):
    rows = (own_ref.shape[0] - 1) // 2
    cols = own_ref.shape[1]
    side = 2 * rows
    odd = lax.rem(lax.axis_index("gy"), 2)
    edge = cols - DEEP
    sub = lax.broadcasted_iota(jnp.int32, (DEEP, LANES), 0)
    sides = ((near_out, edge - edge * odd, odd == 0), (far_out, edge * odd, odd == 1))
    for out_ref, start, right in sides:
        at = pl.ds(pl.multiple_of(start, DEEP), DEEP)
        flags = jnp.zeros((DEEP, LANES), jnp.float32)
        for i, part in x_parts(own_ref, first_ref, second_ref):
            flags = jnp.where(sub == i, part[2 * rows, at, :].astype(jnp.float32), flags)
            for f in range(2):
                if part is own_ref:
                    out_ref[pl.ds(f * side, rows)] = part[pl.ds(f * rows, rows), at, :]
                    continue
                for d in range(1, rows // 2 + 1):
                    a, b = (
                        part[f * rows + jnp.where(i == 0, rows - e, e - 1), at, :].astype(jnp.float32)
                        for e in (d, rows - d)
                    )
                    if d < rows - d:
                        a = jnp.where(
                            right,
                            jnp.where(sub >= d, a, pltpu.roll(b, d, 0)),
                            jnp.where(sub < DEEP - d, a, pltpu.roll(b, DEEP - d, 0)),
                        )
                    out_ref[f * side + rows + (i // 2) * (rows // 2) + d - 1] = a.astype(jnp.bfloat16)
        out_ref[2 * side] = flags.astype(jnp.bfloat16)


def edge_row(part, field, x, rows, right):
    side = 2 * rows
    if rows <= x < 2 * rows:
        return part[field * side + x - rows].astype(jnp.float32)
    d = rows - x if x < rows else x - 2 * rows + 1
    at = field * side + rows + (0 if x < rows else rows // 2) - 1
    if d <= rows // 2:
        return part[at + d].astype(jnp.float32)
    if d == rows:
        return part[at + rows // 2].astype(jnp.float32)
    v = part[at + rows - d].astype(jnp.float32)
    return jnp.where(right, pltpu.roll(v, d, 0), pltpu.roll(v, DEEP - d, 0))


def along_depth(v, w, lane_open):
    f = (w + pltpu.roll(w, LANES - 1, 1)) * (pltpu.roll(v, LANES - 1, 1) - v)
    f = jnp.where(lane_open, f, 0.0)
    return f - pltpu.roll(f, 1, 1)


def flux_sum(val, wgt, lo, hi):
    n = len(val[lo])
    span = range(n)
    lane_open = lax.broadcasted_iota(jnp.int32, (SUB, LANES), 1) < LANES - 1
    depth = {c: [along_depth(val[c][j], wgt[c][j], lane_open) for j in span] for c in range(lo, hi)}

    def toward(c):
        return [(wgt[c][j] + wgt[c + 1][j]) * (val[c + 1][j] - val[c][j]) for j in span]

    out = {}
    last = toward(lo - 1)
    for c in range(lo, hi):
        v, w = val[c], wgt[c]
        ahead = toward(c)
        down = [(w[j] + w[j + 1]) * (v[j + 1] - v[j]) for j in range(n - 1)]
        down.append(
            (w[n - 1] + pltpu.roll(w[0], SUB - 1, 0)) * (pltpu.roll(v[0], SUB - 1, 0) - v[n - 1])
        )
        up = [pltpu.roll(down[-1], 1, 0)] + down[:-1]
        out[c] = [(ahead[j] - last[j]) + (down[j] - up[j]) + depth[c][j] for j in span]
        last = ahead
    return out


def conduct(h, q, mask, lo, hi):
    temp, cond = {}, {}
    for c in range(lo - 1, hi + 1):
        t = [jnp.tanh(v) for v in h[c]]
        temp[c] = [v - 0.4 * u for v, u in zip(h[c], t)]
        cond[c] = [(1.0 - v) * (1.0 - v) * (u + 7.0 / 3.0) for v, u in zip(q[c], t)]
    acc = flux_sum(temp, cond, lo, hi)
    return {
        c: [v + m * a for v, m, a in zip(h[c], mask(c, 0), acc[c])] for c in range(lo, hi)
    }


def consolidate(h, q, mask, lo, hi):
    rate = {
        c: [1.0 + jnp.tanh(2.5 * v - jnp.tanh(v)) for v in h[c]] for c in range(lo - 1, hi + 1)
    }
    acc = flux_sum(q, rate, lo, hi)
    return {
        c: [
            v + m * (a - 4.0 * r * v)
            for v, m, a, r in zip(q[c], mask(c, 1), acc[c], rate[c])
        ]
        for c in range(lo, hi)
    }


def tile_rows(marks, i, tx, n, out):
    low = lax.broadcasted_iota(jnp.int32, (SUB, LANES), 1) < LANES // 2
    sub = lax.broadcasted_iota(jnp.int32, (SUB, LANES), 0)
    other = pltpu.roll(marks, LANES // 2, 1)
    for h, flag in ((0, jnp.where(low, marks, other)), (1, jnp.where(low, other, marks))):
        first = (2 * i + h) * tx
        for j in range(n):
            x = sub * n + j
            out[j] = jnp.where((x >= first) & (x < first + tx), flag, out[j])
    return out


def scalings(flags):
    return ([0.0225 * f for f in flags], [0.0375 * f for f in flags])


def inner(
    own_ref, heat_ref, pore_ref, xa_ref, xb_ref,
    heat_edge, pore_edge, heat_save, pore_save, heat_mid, pore_mid, flag_out, wide,
):
    rows, cols = heat_ref.shape[0], heat_ref.shape[1]
    total = rows + 2 * DEEP
    width = cols + 2 * DEEP
    n = total // SUB
    tx, ty = rows // 2, cols // 2
    f32 = jnp.float32
    opens = []
    parts = x_parts(own_ref, xa_ref, xb_ref)
    for i, part in parts:
        opens.append(jnp.where(i == 0, inside("gx", False), inside("gx", True)))

    flags = []
    for k in range(2):
        f = [jnp.zeros((SUB, LANES), f32) for _ in range(n)]
        for (i, part), has in zip(parts, opens):
            marks = part[2 * rows, pl.ds(k * ty, SUB), :].astype(f32)
            f = tile_rows(marks if part is own_ref else marks * has, i, tx, n, f)
        for j in range(n):
            flag_out[k, j] = f[j]
        flags.append(scalings(f))

    def mask(c, kind):
        return flags[0 if c < DEEP + ty else 1][kind]

    h, q = {}, {}
    for field, home, state in ((0, heat_ref, h), (1, pore_ref, q)):
        for (i, part), has in zip(parts, opens):
            for r in range(rows):
                if part is own_ref:
                    v = home[r]
                else:
                    v = part[field * rows + r].astype(f32) * has
                at = pl.multiple_of((i * rows + r) * cols, SUB)
                wide[field, pl.ds(at, cols), :] = 2.0 * v - 2.0 if field == 0 else v
        for c in range(cols):
            state[DEEP + c] = [
                wide[field, pl.ds(j * cols + c, SUB, stride=n * cols), :] for j in range(n)
            ]

    for p in range(PAIRS):
        lo, hi = DEEP + 2 * p + 1, width - DEEP - 2 * p - 1
        for side, c in ((0, lo), (1, hi - 1)):
            for j in range(n):
                heat_save[p, side, j] = h[c][j]
        h.update(conduct(h, q, mask, lo, hi))
        lo, hi = lo + 1, hi - 1
        for side, c in ((0, lo), (1, hi - 1)):
            for j in range(n):
                pore_save[p, side, j] = q[c][j]
        q.update(consolidate(h, q, mask, lo, hi))

    for field, state, edge, mid in ((0, h, heat_edge, heat_mid), (1, q, pore_edge, pore_mid)):
        for c in range(DEEP + 1):
            for j in range(n):
                edge[0, c, j] = state[DEEP + c][j]
                edge[1, c, j] = state[width - DEEP - 1 - c][j]
        for c in range(DEEP, cols - DEEP):
            for j in range(n):
                v = state[DEEP + c][j]
                wide[field, pl.ds(j * cols + c, SUB, stride=n * cols), :] = (
                    0.5 * v + 1.0 if field == 0 else v
                )
        for r in range(rows):
            mid[r] = wide[field, pl.ds((DEEP + r) * cols + DEEP, cols - 2 * DEEP), :]


def edges(
    mask_ref, heat_edge, pore_edge, heat_save, pore_save, heat_mid, pore_mid, flag_ref, yn_ref, yf_ref,
    heat_out, pore_out, send_ref, later_ref, wide, block,
):
    rows, cols = heat_mid.shape[0], heat_mid.shape[1] + 2 * DEEP
    total = rows + 2 * DEEP
    width = cols + 2 * DEEP
    n = total // SUB
    tx, ty = rows // 2, cols // 2
    f32 = jnp.float32
    odd = lax.rem(lax.axis_index("gy"), 2)
    row_open = (inside("gx", False), None, inside("gx", True))
    far_open = jnp.where(odd == 1, inside("gy", True), inside("gy", False))
    parts = ((1 - odd, yn_ref, None, odd == 1), (odd, yf_ref, far_open, odd == 0))

    def scaled(v, *by):
        for s in by:
            v = v if s is None else v * s
        return v

    halves = []
    for at, part, has, _ in parts:
        marks = scaled(part[4 * rows].astype(f32), has)
        f = [jnp.zeros((SUB, LANES), f32) for _ in range(n)]
        for i in range(3):
            f = tile_rows(
                jnp.broadcast_to(scaled(marks[i : i + 1], row_open[i]), (SUB, LANES)), i, tx, n, f
            )
        halves.append(f)
    near, far = halves
    left = [jnp.where(odd == 1, a, b) for a, b in zip(near, far)]
    right = [jnp.where(odd == 1, b, a) for a, b in zip(near, far)]
    flags = [
        scalings(f)
        for f in (left, *([flag_ref[k, j] for j in range(n)] for k in range(2)), right)
    ]

    def mask(c, kind):
        return flags[0 if c < DEEP else 1 if c < DEEP + ty else 2 if c < DEEP + cols else 3][kind]

    pair = 2 * DEEP
    h, q = {}, {}
    for field, edge, state in ((0, heat_edge, h), (1, pore_edge, q)):
        for at, part, has, right_end in parts:
            for x in range(total):
                v = scaled(edge_row(part, field, x, rows, right_end), has, row_open[x // rows])
                into = pl.multiple_of(x * pair + at * DEEP, SUB)
                wide[field, pl.ds(into, DEEP), :] = 2.0 * v - 2.0 if field == 0 else v
        for c in range(DEEP):
            for first, halo in ((0, c), (DEEP, width - DEEP + c)):
                state[halo] = [
                    wide[field, pl.ds(j * pair + first + c, SUB, stride=n * pair), :]
                    for j in range(n)
                ]
        for c in range(DEEP + 1):
            state[DEEP + c] = [edge[0, c, j] for j in range(n)]
            state[width - DEEP - 1 - c] = [edge[1, c, j] for j in range(n)]

    for p in range(PAIRS):
        lo = 2 * p + 1
        hi = width - lo
        new = {}
        for side, a, b, c in ((0, lo, lo + DEEP, lo + DEEP), (1, hi - DEEP, hi, hi - DEEP - 1)):
            then = dict(h)
            then[c] = [heat_save[p, side, j] for j in range(n)]
            new.update(conduct(then, q, mask, a, b))
        h.update(new)
        lo, hi = lo + 1, hi - 1
        new = {}
        for side, a, b, c in ((0, lo, lo + DEEP, lo + DEEP), (1, hi - DEEP, hi, hi - DEEP - 1)):
            then = dict(q)
            then[c] = [pore_save[p, side, j] for j in range(n)]
            new.update(consolidate(h, then, mask, a, b))
        q.update(new)

    for field, state, mid, out in ((0, h, heat_mid, heat_out), (1, q, pore_mid, pore_out)):
        for c in range(DEEP):
            for first, own in ((0, DEEP + c), (DEEP, width - pair + c)):
                for j in range(n):
                    v = state[own][j]
                    wide[field, pl.ds(j * pair + first + c, SUB, stride=n * pair), :] = (
                        0.5 * v + 1.0 if field == 0 else v
                    )
        for r in range(rows):
            row = (DEEP + r) * pair
            block[field, r, 0:DEEP] = wide[field, pl.ds(row, DEEP), :]
            block[field, r, DEEP : cols - DEEP] = mid[r]
            block[field, r, cols - DEEP :] = wide[field, pl.ds(row + DEEP, DEEP), :]
        for i in range(2):
            for k in range(2):
                out[2 * i + k] = block[field, i * tx : (i + 1) * tx, k * ty : (k + 1) * ty, :]
    ranks = send_ref.shape[0]
    choose = mask_at(ranks)[0]
    shape = (tx, ty, LANES)
    for field, src, scale, shift in (
        (0, heat_out, HEAT_SCALE, HEAT_SHIFT),
        (1, pore_out, PORE_SCALE, PORE_SHIFT),
    ):
        for i, out in ((0, send_ref), (1, later_ref)):
            for k in range(ranks):
                v = src[0]
                for s in range(1, 4):
                    v = jnp.where(held(mask_ref, choose(i, k, s), shape), src[s], v)
                out[k, field] = encode(v, scale, shift)


def held(mask_ref, row, shape):
    m = mask_ref[row]
    m = jnp.concatenate([m] * (shape[1] // SUB), axis=0)
    return jnp.broadcast_to(m[None], shape) > 0.5


def resend(mask_ref, got_ref, local_ref, send_ref):
    ranks = got_ref.shape[0]
    shape = got_ref.shape[2:]
    again = mask_at(ranks)[2]
    for k in range(ranks):
        for f in range(2):
            v = local_ref[k, f].astype(jnp.int32)
            for r in range(ranks):
                v = jnp.where(
                    held(mask_ref, again(k, r), shape), got_ref[r, f].astype(jnp.int32), v
                )
            send_ref[k, f] = v.astype(jnp.int16)


def place(mask_ref, heat_ref, pore_ref, first_ref, second_ref, heat_out, pore_out):
    ranks = first_ref.shape[0]
    shape = first_ref.shape[2:]
    taken = mask_at(ranks)[1]
    for field, src, out, scale, shift in (
        (0, heat_ref, heat_out, HEAT_SCALE, HEAT_SHIFT),
        (1, pore_ref, pore_out, PORE_SCALE, PORE_SHIFT),
    ):
        came = [
            (i, r, decode(got[r, field], scale, shift))
            for i, got in ((0, first_ref), (1, second_ref))
            for r in range(ranks)
        ]
        for s in range(4):
            v = src[s]
            for i, r, tile in came:
                v = jnp.where(held(mask_ref, taken(i, r, s), shape), tile, v)
            out[s] = v


def call(body, spec, outs, scratch=(), out_space=pltpu.VMEM):
    def run(*args):
        space = {"s": pltpu.SMEM, "v": pltpu.VMEM, "V": pltpu.VMEM}
        args = [
            pltpu.with_memory_space_constraint(a, pltpu.VMEM if c == "V" else pltpu.HBM)
            for c, a in zip(spec, args)
        ]
        shapes = [
            pltpu.VMEM(s, d) if out_space is not None else jax.ShapeDtypeStruct(s, d)
            for s, d in outs
        ]
        return pl.pallas_call(
            body,
            in_specs=[pl.BlockSpec(memory_space=space[c]) for c in spec],
            out_specs=[pl.BlockSpec(memory_space=pltpu.VMEM) for _ in outs],
            out_shape=shapes,
            scratch_shapes=list(scratch),
            compiler_params=pltpu.CompilerParams(vmem_limit_bytes=VMEM_LIMIT),
        )(*args)

    return run


def permute(value, partner):
    nx, ny = lax.axis_size("gx"), lax.axis_size("gy")
    pairs = []
    for x in range(nx):
        for y in range(ny):
            u, v = partner(x, y)
            pairs.append((x * ny + y, u * ny + v))
    return lax.ppermute(value, ("gx", "gy"), pairs)


def exchange_x(value):
    nx, ny = lax.axis_size("gx"), lax.axis_size("gy")

    def partner(x, y, near):
        if near:
            return x ^ 1, y
        if 0 < x < nx - 1:
            return ((x + 1) ^ 1) - 1, y
        return (x, y ^ 2) if ny % 4 == 0 else (x, y)

    first = permute(value, lambda x, y: partner(x, y, y % 2 == 0))
    second = permute(value, lambda x, y: partner(x, y, y % 2 == 1))
    return first, second


def exchange_y(near, far):
    ny = lax.axis_size("gy")

    def partner(x, y):
        if 0 < y < ny - 1:
            return x, ((y + 1) ^ 1) - 1
        return x ^ 1, y

    far = permute(far, partner)
    near = permute(near, lambda x, y: (x, y ^ 1))
    return near, far


def swap(value, axis):
    n = lax.axis_size(axis)
    return lax.ppermute(value, axis, [(i, (i + n // 2) % n) for i in range(n)])


def per_device(enthalpy, porosity, active, move_count, move_slot):
    rows, cols, depth = enthalpy.shape
    tx, ty = rows // 2, cols // 2
    count = move_count.reshape(2)
    slots = move_slot.reshape(2, move_slot.shape[-1])
    ranks = slots.shape[1]
    f32, bf16, i16 = jnp.float32, jnp.bfloat16, jnp.int16

    block = ((rows, cols, depth), f32)
    masks = ((mask_at(ranks)[3], SUB, LANES), f32)
    own, enthalpy, porosity, masks = call(
        pack_x, "sssvv", [((2 * rows + 1, cols, depth), bf16), block, block, masks]
    )(active, count, slots, enthalpy, porosity)
    x_near, x_far = exchange_x(own)
    side = ((4 * rows + 1, DEEP, depth), bf16)
    near, far = call(pack_y, "VVV", [side, side])(own, x_near, x_far)
    y_near, y_far = exchange_y(near, far)
    total = rows + 2 * DEEP
    n = total // SUB
    tiles = ((4, tx, ty, depth), f32)
    parcel = ((ranks, 2, tx, ty, depth), i16)
    edge = ((2, DEEP + 1, n, SUB, depth), f32)
    save = ((PAIRS, 2, n, SUB, depth), f32)
    mid = ((rows, cols - 2 * DEEP, depth), f32)
    flag = ((2, n, SUB, depth), f32)
    state = call(
        inner, "VVVVV", [edge, edge, save, save, mid, mid, flag],
        [pltpu.VMEM((2, total * cols, depth), f32)],
    )(own, enthalpy, porosity, x_near, x_far)
    heat, pore, first, later = call(
        edges, "V" * 10, [tiles, tiles, parcel, parcel],
        [
            pltpu.VMEM((2, total * 2 * DEEP, depth), f32),
            pltpu.VMEM((2, rows, cols, depth), f32),
        ],
    )(masks, *state, y_near, y_far)
    first = swap(first, "gx")
    (second,) = call(resend, "VVV", [parcel])(masks, first, later)
    second = swap(second, "gy")
    heat, pore = call(place, "VVVVV", [tiles, tiles], out_space=None)(
        masks, heat, pore, first, second
    )
    return heat[None, None], pore[None, None]


def solution(mesh):
    placed = (
        P("gx", "gy", None),
        P("gx", "gy", None),
        P("gx", "gy"),
        P("gx", "gy", None),
        P("gx", "gy", None, None),
    )
    out = P("gx", "gy", None, None, None, None)

    return jax.shard_map(
        per_device, mesh=mesh, in_specs=placed, out_specs=(out, out), check_vma=False
    )
```

```python
import jax
import jax.numpy as jnp
from jax import lax
from jax.experimental import pallas as pl
from jax.experimental.pallas import tpu as pltpu
from jax.sharding import PartitionSpec as P


PAIRS = 4
DEEP = 2 * PAIRS
SUB = 8
LANES = 128
VMEM_LIMIT = 16 * 2**20

HEAT_SCALE = 25000.0
HEAT_SHIFT = 32000.0
PORE_SCALE = 40000.0
PORE_SHIFT = 7000.0


def encode(values, scale, shift):
    return jnp.floor(values * scale + (0.5 - shift)).astype(jnp.int32).astype(jnp.int16)


def decode(codes, scale, shift):
    return (codes.astype(jnp.int32).astype(jnp.float32) + shift) * (1.0 / scale)


def flag_rows(active_ref, cols):
    lane = lax.broadcasted_iota(jnp.int32, (cols, LANES), 1)
    col = lax.broadcasted_iota(jnp.int32, (cols, LANES), 0)

    def flag(i):
        return jnp.where(col < cols // 2, active_ref[i, 0], active_ref[i, 1])

    return jnp.where(lane < LANES // 2, flag(0), flag(1)).astype(jnp.float32)


def mask_at(ranks):
    choose = lambda i, k, s: (i * ranks + k) * 4 + s
    taken = lambda i, r, s: 8 * ranks + (i * ranks + r) * 4 + s
    again = lambda k, r: 16 * ranks + k * ranks + r
    return choose, taken, again, 16 * ranks + ranks * ranks


def pack_x(
    active_ref, count_ref, slot_ref, heat_ref, pore_ref, out_ref, heat_out, pore_out, mask_ref
):
    rows, cols = heat_ref.shape[0], heat_ref.shape[1]
    ranks = slot_ref.shape[1]
    out_ref[0:rows] = heat_ref[...].astype(jnp.bfloat16)
    out_ref[rows : 2 * rows] = pore_ref[...].astype(jnp.bfloat16)
    out_ref[2 * rows] = flag_rows(active_ref, cols).astype(jnp.bfloat16)
    heat_out[...] = heat_ref[...]
    pore_out[...] = pore_ref[...]
    choose, taken, again, _ = mask_at(ranks)

    def put(row, holds):
        mask_ref[row] = jnp.full((SUB, LANES), jnp.where(holds, 1.0, 0.0), jnp.float32)

    for i in range(2):
        for k in range(ranks):
            for s in range(4):
                here = slot_ref[i, k] == s
                put(choose(i, k, s), here)
                put(taken(i, k, s), here & (k < count_ref[i]))
    for k in range(ranks):
        for r in range(ranks):
            put(again(k, r), (slot_ref[1, k] == slot_ref[0, r]) & (r < count_ref[0]))


def inside(axis, below):
    at = lax.axis_index(axis)
    has = at < lax.axis_size(axis) - 1 if below else at > 0
    return jnp.where(has, 1.0, 0.0).astype(jnp.float32)


def x_parts(own_ref, first_ref, second_ref):
    odd = lax.rem(lax.axis_index("gx") + lax.axis_index("gy"), 2)
    return ((2 - 2 * odd, first_ref), (1, own_ref), (2 * odd, second_ref))


def pack_y(own_ref, first_ref, second_ref, near_out, far_out):
    rows = (own_ref.shape[0] - 1) // 2
    cols = own_ref.shape[1]
    side = 2 * rows
    odd = lax.rem(lax.axis_index("gy"), 2)
    edge = cols - DEEP
    sub = lax.broadcasted_iota(jnp.int32, (DEEP, LANES), 0)
    sides = ((near_out, edge - edge * odd, odd == 0), (far_out, edge * odd, odd == 1))
    for out_ref, start, right in sides:
        at = pl.ds(pl.multiple_of(start, DEEP), DEEP)
        flags = jnp.zeros((DEEP, LANES), jnp.float32)
        for i, part in x_parts(own_ref, first_ref, second_ref):
            flags = jnp.where(sub == i, part[2 * rows, at, :].astype(jnp.float32), flags)
            for f in range(2):
                if part is own_ref:
                    out_ref[pl.ds(f * side, rows)] = part[pl.ds(f * rows, rows), at, :]
                    continue
                for d in range(1, rows // 2 + 1):
                    a, b = (
                        part[f * rows + jnp.where(i == 0, rows - e, e - 1), at, :].astype(jnp.float32)
                        for e in (d, rows - d)
                    )
                    if d < rows - d:
                        a = jnp.where(
                            right,
                            jnp.where(sub >= d, a, pltpu.roll(b, d, 0)),
                            jnp.where(sub < DEEP - d, a, pltpu.roll(b, DEEP - d, 0)),
                        )
                    out_ref[f * side + rows + (i // 2) * (rows // 2) + d - 1] = a.astype(jnp.bfloat16)
        out_ref[2 * side] = flags.astype(jnp.bfloat16)


def edge_row(part, field, x, rows, right):
    side = 2 * rows
    if rows <= x < 2 * rows:
        return part[field * side + x - rows].astype(jnp.float32)
    d = rows - x if x < rows else x - 2 * rows + 1
    at = field * side + rows + (0 if x < rows else rows // 2) - 1
    if d <= rows // 2:
        return part[at + d].astype(jnp.float32)
    if d == rows:
        return part[at + rows // 2].astype(jnp.float32)
    v = part[at + rows - d].astype(jnp.float32)
    return jnp.where(right, pltpu.roll(v, d, 0), pltpu.roll(v, DEEP - d, 0))


def flux_sum(val, wgt, lo, hi):
    n = len(val[lo])
    span = range(n)
    lane_open = lax.broadcasted_iota(jnp.int32, (SUB, LANES), 1) < LANES - 1
    each = [(c, j) for c in range(lo, hi) for j in span]
    deeper = [
        (pltpu.roll(val[c][j], LANES - 1, 1), pltpu.roll(wgt[c][j], LANES - 1, 1)) for c, j in each
    ]
    depth = {}
    for (c, j), (v, w) in zip(each, deeper):
        depth[c, j] = jnp.where(lane_open, (wgt[c][j] + w) * (v - val[c][j]), 0.0)
    for at in each:
        depth[at] = depth[at] - pltpu.roll(depth[at], 1, 1)

    def toward(c):
        return [(wgt[c][j] + wgt[c + 1][j]) * (val[c + 1][j] - val[c][j]) for j in span]

    out = {}
    last = toward(lo - 1)
    for c in range(lo, hi):
        v, w = val[c], wgt[c]
        ahead = toward(c)
        down = [(w[j] + w[j + 1]) * (v[j + 1] - v[j]) for j in range(n - 1)]
        down.append(
            (w[n - 1] + pltpu.roll(w[0], SUB - 1, 0)) * (pltpu.roll(v[0], SUB - 1, 0) - v[n - 1])
        )
        up = [pltpu.roll(down[-1], 1, 0)] + down[:-1]
        out[c] = [(ahead[j] - last[j]) + (down[j] - up[j]) + depth[c, j] for j in span]
        last = ahead
    return out


def conduct(h, q, mask, lo, hi):
    temp, cond = {}, {}
    for c in range(lo - 1, hi + 1):
        t = [jnp.tanh(v) for v in h[c]]
        temp[c] = [v - 0.4 * u for v, u in zip(h[c], t)]
        cond[c] = [(1.0 - v) * (1.0 - v) * (u + 7.0 / 3.0) for v, u in zip(q[c], t)]
    acc = flux_sum(temp, cond, lo, hi)
    return {
        c: [v + m * a for v, m, a in zip(h[c], mask(c, 0), acc[c])] for c in range(lo, hi)
    }


def consolidate(h, q, mask, lo, hi):
    rate = {
        c: [1.0 + jnp.tanh(2.5 * v - jnp.tanh(v)) for v in h[c]] for c in range(lo - 1, hi + 1)
    }
    acc = flux_sum(q, rate, lo, hi)
    return {
        c: [
            v + m * (a - 4.0 * r * v)
            for v, m, a, r in zip(q[c], mask(c, 1), acc[c], rate[c])
        ]
        for c in range(lo, hi)
    }


def tile_rows(marks, i, tx, n, out):
    low = lax.broadcasted_iota(jnp.int32, (SUB, LANES), 1) < LANES // 2
    sub = lax.broadcasted_iota(jnp.int32, (SUB, LANES), 0)
    other = pltpu.roll(marks, LANES // 2, 1)
    for h, flag in ((0, jnp.where(low, marks, other)), (1, jnp.where(low, other, marks))):
        first = (2 * i + h) * tx
        for j in range(n):
            x = sub * n + j
            out[j] = jnp.where((x >= first) & (x < first + tx), flag, out[j])
    return out


def scalings(flags):
    return ([0.0225 * f for f in flags], [0.0375 * f for f in flags])


def inner(
    own_ref, heat_ref, pore_ref, xa_ref, xb_ref,
    heat_edge, pore_edge, heat_save, pore_save, heat_mid, pore_mid, flag_out, wide,
):
    rows, cols = heat_ref.shape[0], heat_ref.shape[1]
    total = rows + 2 * DEEP
    width = cols + 2 * DEEP
    n = total // SUB
    tx, ty = rows // 2, cols // 2
    f32 = jnp.float32
    opens = []
    parts = x_parts(own_ref, xa_ref, xb_ref)
    for i, part in parts:
        opens.append(jnp.where(i == 0, inside("gx", False), inside("gx", True)))

    flags = []
    for k in range(2):
        f = [jnp.zeros((SUB, LANES), f32) for _ in range(n)]
        for (i, part), has in zip(parts, opens):
            marks = part[2 * rows, pl.ds(k * ty, SUB), :].astype(f32)
            f = tile_rows(marks if part is own_ref else marks * has, i, tx, n, f)
        for j in range(n):
            flag_out[k, j] = f[j]
        flags.append(scalings(f))

    def mask(c, kind):
        return flags[0 if c < DEEP + ty else 1][kind]

    h, q = {}, {}
    for field, home, state in ((0, heat_ref, h), (1, pore_ref, q)):
        for (i, part), has in zip(parts, opens):
            for r in range(rows):
                if part is own_ref:
                    v = home[r]
                else:
                    v = part[field * rows + r].astype(f32) * has
                at = pl.multiple_of((i * rows + r) * cols, SUB)
                wide[field, pl.ds(at, cols), :] = 2.0 * v - 2.0 if field == 0 else v
        for c in range(cols):
            state[DEEP + c] = [
                wide[field, pl.ds(j * cols + c, SUB, stride=n * cols), :] for j in range(n)
            ]

    for p in range(PAIRS):
        lo, hi = DEEP + 2 * p + 1, width - DEEP - 2 * p - 1
        for side, c in ((0, lo), (1, hi - 1)):
            for j in range(n):
                heat_save[p, side, j] = h[c][j]
        h.update(conduct(h, q, mask, lo, hi))
        lo, hi = lo + 1, hi - 1
        for side, c in ((0, lo), (1, hi - 1)):
            for j in range(n):
                pore_save[p, side, j] = q[c][j]
        q.update(consolidate(h, q, mask, lo, hi))

    for field, state, edge, mid in ((0, h, heat_edge, heat_mid), (1, q, pore_edge, pore_mid)):
        for c in range(DEEP + 1):
            for j in range(n):
                edge[0, c, j] = state[DEEP + c][j]
                edge[1, c, j] = state[width - DEEP - 1 - c][j]
        for c in range(DEEP, cols - DEEP):
            for j in range(n):
                v = state[DEEP + c][j]
                wide[field, pl.ds(j * cols + c, SUB, stride=n * cols), :] = (
                    0.5 * v + 1.0 if field == 0 else v
                )
        for r in range(rows):
            mid[r] = wide[field, pl.ds((DEEP + r) * cols + DEEP, cols - 2 * DEEP), :]


def edges(
    mask_ref, heat_edge, pore_edge, heat_save, pore_save, heat_mid, pore_mid, flag_ref, yn_ref, yf_ref,
    heat_out, pore_out, send_ref, later_ref, wide, block,
):
    rows, cols = heat_mid.shape[0], heat_mid.shape[1] + 2 * DEEP
    total = rows + 2 * DEEP
    width = cols + 2 * DEEP
    n = total // SUB
    tx, ty = rows // 2, cols // 2
    f32 = jnp.float32
    odd = lax.rem(lax.axis_index("gy"), 2)
    row_open = (inside("gx", False), None, inside("gx", True))
    far_open = jnp.where(odd == 1, inside("gy", True), inside("gy", False))
    parts = ((1 - odd, yn_ref, None, odd == 1), (odd, yf_ref, far_open, odd == 0))

    def scaled(v, *by):
        for s in by:
            v = v if s is None else v * s
        return v

    halves = []
    for at, part, has, _ in parts:
        marks = scaled(part[4 * rows].astype(f32), has)
        f = [jnp.zeros((SUB, LANES), f32) for _ in range(n)]
        for i in range(3):
            f = tile_rows(
                jnp.broadcast_to(scaled(marks[i : i + 1], row_open[i]), (SUB, LANES)), i, tx, n, f
            )
        halves.append(f)
    near, far = halves
    left = [jnp.where(odd == 1, a, b) for a, b in zip(near, far)]
    right = [jnp.where(odd == 1, b, a) for a, b in zip(near, far)]
    flags = [
        scalings(f)
        for f in (left, *([flag_ref[k, j] for j in range(n)] for k in range(2)), right)
    ]

    def mask(c, kind):
        return flags[0 if c < DEEP else 1 if c < DEEP + ty else 2 if c < DEEP + cols else 3][kind]

    pair = 2 * DEEP
    h, q = {}, {}
    for field, edge, state in ((0, heat_edge, h), (1, pore_edge, q)):
        for at, part, has, right_end in parts:
            for x in range(total):
                v = scaled(edge_row(part, field, x, rows, right_end), has, row_open[x // rows])
                into = pl.multiple_of(x * pair + at * DEEP, SUB)
                wide[field, pl.ds(into, DEEP), :] = 2.0 * v - 2.0 if field == 0 else v
        for c in range(DEEP):
            for first, halo in ((0, c), (DEEP, width - DEEP + c)):
                state[halo] = [
                    wide[field, pl.ds(j * pair + first + c, SUB, stride=n * pair), :]
                    for j in range(n)
                ]
        for c in range(DEEP + 1):
            state[DEEP + c] = [edge[0, c, j] for j in range(n)]
            state[width - DEEP - 1 - c] = [edge[1, c, j] for j in range(n)]

    for p in range(PAIRS):
        lo = 2 * p + 1
        hi = width - lo
        new = {}
        for side, a, b, c in ((0, lo, lo + DEEP, lo + DEEP), (1, hi - DEEP, hi, hi - DEEP - 1)):
            then = dict(h)
            then[c] = [heat_save[p, side, j] for j in range(n)]
            new.update(conduct(then, q, mask, a, b))
        h.update(new)
        lo, hi = lo + 1, hi - 1
        new = {}
        for side, a, b, c in ((0, lo, lo + DEEP, lo + DEEP), (1, hi - DEEP, hi, hi - DEEP - 1)):
            then = dict(q)
            then[c] = [pore_save[p, side, j] for j in range(n)]
            new.update(consolidate(h, then, mask, a, b))
        q.update(new)

    for field, state, mid, out in ((0, h, heat_mid, heat_out), (1, q, pore_mid, pore_out)):
        for c in range(DEEP):
            for first, own in ((0, DEEP + c), (DEEP, width - pair + c)):
                for j in range(n):
                    v = state[own][j]
                    wide[field, pl.ds(j * pair + first + c, SUB, stride=n * pair), :] = (
                        0.5 * v + 1.0 if field == 0 else v
                    )
        for r in range(rows):
            row = (DEEP + r) * pair
            block[field, r, 0:DEEP] = wide[field, pl.ds(row, DEEP), :]
            block[field, r, DEEP : cols - DEEP] = mid[r]
            block[field, r, cols - DEEP :] = wide[field, pl.ds(row + DEEP, DEEP), :]
        for i in range(2):
            for k in range(2):
                out[2 * i + k] = block[field, i * tx : (i + 1) * tx, k * ty : (k + 1) * ty, :]
    ranks = send_ref.shape[0]
    choose = mask_at(ranks)[0]
    shape = (tx, ty, LANES)
    for field, src, scale, shift in (
        (0, heat_out, HEAT_SCALE, HEAT_SHIFT),
        (1, pore_out, PORE_SCALE, PORE_SHIFT),
    ):
        for i, out in ((0, send_ref), (1, later_ref)):
            for k in range(ranks):
                v = src[0]
                for s in range(1, 4):
                    v = jnp.where(held(mask_ref, choose(i, k, s), shape), src[s], v)
                out[k, field] = encode(v, scale, shift)


def held(mask_ref, row, shape):
    m = mask_ref[row]
    m = jnp.concatenate([m] * (shape[1] // SUB), axis=0)
    return jnp.broadcast_to(m[None], shape) > 0.5


def resend(mask_ref, got_ref, local_ref, send_ref):
    ranks = got_ref.shape[0]
    shape = got_ref.shape[2:]
    again = mask_at(ranks)[2]
    for k in range(ranks):
        for f in range(2):
            v = local_ref[k, f].astype(jnp.int32)
            for r in range(ranks):
                v = jnp.where(
                    held(mask_ref, again(k, r), shape), got_ref[r, f].astype(jnp.int32), v
                )
            send_ref[k, f] = v.astype(jnp.int16)


def place(mask_ref, heat_ref, pore_ref, first_ref, second_ref, heat_out, pore_out):
    ranks = first_ref.shape[0]
    shape = first_ref.shape[2:]
    taken = mask_at(ranks)[1]
    for field, src, out, scale, shift in (
        (0, heat_ref, heat_out, HEAT_SCALE, HEAT_SHIFT),
        (1, pore_ref, pore_out, PORE_SCALE, PORE_SHIFT),
    ):
        came = [
            (i, r, decode(got[r, field], scale, shift))
            for i, got in ((0, first_ref), (1, second_ref))
            for r in range(ranks)
        ]
        for s in range(4):
            v = src[s]
            for i, r, tile in came:
                v = jnp.where(held(mask_ref, taken(i, r, s), shape), tile, v)
            out[s] = v


def call(body, spec, outs, scratch=(), out_space=pltpu.VMEM):
    def run(*args):
        space = {"s": pltpu.SMEM, "v": pltpu.VMEM, "V": pltpu.VMEM}
        args = [
            pltpu.with_memory_space_constraint(a, pltpu.VMEM if c == "V" else pltpu.HBM)
            for c, a in zip(spec, args)
        ]
        shapes = [
            pltpu.VMEM(s, d) if out_space is not None else jax.ShapeDtypeStruct(s, d)
            for s, d in outs
        ]
        return pl.pallas_call(
            body,
            in_specs=[pl.BlockSpec(memory_space=space[c]) for c in spec],
            out_specs=[pl.BlockSpec(memory_space=pltpu.VMEM) for _ in outs],
            out_shape=shapes,
            scratch_shapes=list(scratch),
            compiler_params=pltpu.CompilerParams(vmem_limit_bytes=VMEM_LIMIT),
        )(*args)

    return run


def permute(value, partner):
    nx, ny = lax.axis_size("gx"), lax.axis_size("gy")
    pairs = []
    for x in range(nx):
        for y in range(ny):
            u, v = partner(x, y)
            pairs.append((x * ny + y, u * ny + v))
    return lax.ppermute(value, ("gx", "gy"), pairs)


def exchange_x(value):
    nx, ny = lax.axis_size("gx"), lax.axis_size("gy")

    def partner(x, y, near):
        if near:
            return x ^ 1, y
        if 0 < x < nx - 1:
            return ((x + 1) ^ 1) - 1, y
        return (x, y ^ 2) if ny % 4 == 0 else (x, y)

    first = permute(value, lambda x, y: partner(x, y, y % 2 == 0))
    second = permute(value, lambda x, y: partner(x, y, y % 2 == 1))
    return first, second


def exchange_y(near, far):
    ny = lax.axis_size("gy")

    def partner(x, y):
        if 0 < y < ny - 1:
            return x, ((y + 1) ^ 1) - 1
        return x ^ 1, y

    far = permute(far, partner)
    near = permute(near, lambda x, y: (x, y ^ 1))
    return near, far


def swap(value, axis):
    n = lax.axis_size(axis)
    return lax.ppermute(value, axis, [(i, (i + n // 2) % n) for i in range(n)])


def per_device(enthalpy, porosity, active, move_count, move_slot):
    rows, cols, depth = enthalpy.shape
    tx, ty = rows // 2, cols // 2
    count = move_count.reshape(2)
    slots = move_slot.reshape(2, move_slot.shape[-1])
    ranks = slots.shape[1]
    f32, bf16, i16 = jnp.float32, jnp.bfloat16, jnp.int16

    block = ((rows, cols, depth), f32)
    masks = ((mask_at(ranks)[3], SUB, LANES), f32)
    own, enthalpy, porosity, masks = call(
        pack_x, "sssvv", [((2 * rows + 1, cols, depth), bf16), block, block, masks]
    )(active, count, slots, enthalpy, porosity)
    x_near, x_far = exchange_x(own)
    side = ((4 * rows + 1, DEEP, depth), bf16)
    near, far = call(pack_y, "VVV", [side, side])(own, x_near, x_far)
    y_near, y_far = exchange_y(near, far)
    total = rows + 2 * DEEP
    n = total // SUB
    tiles = ((4, tx, ty, depth), f32)
    parcel = ((ranks, 2, tx, ty, depth), i16)
    edge = ((2, DEEP + 1, n, SUB, depth), f32)
    save = ((PAIRS, 2, n, SUB, depth), f32)
    mid = ((rows, cols - 2 * DEEP, depth), f32)
    flag = ((2, n, SUB, depth), f32)
    state = call(
        inner, "VVVVV", [edge, edge, save, save, mid, mid, flag],
        [pltpu.VMEM((2, total * cols, depth), f32)],
    )(own, enthalpy, porosity, x_near, x_far)
    heat, pore, first, later = call(
        edges, "V" * 10, [tiles, tiles, parcel, parcel],
        [
            pltpu.VMEM((2, total * 2 * DEEP, depth), f32),
            pltpu.VMEM((2, rows, cols, depth), f32),
        ],
    )(masks, *state, y_near, y_far)
    first = swap(first, "gx")
    (second,) = call(resend, "VVV", [parcel])(masks, first, later)
    second = swap(second, "gy")
    heat, pore = call(place, "VVVVV", [tiles, tiles], out_space=None)(
        masks, heat, pore, first, second
    )
    return heat[None, None], pore[None, None]


def solution(mesh):
    placed = (
        P("gx", "gy", None),
        P("gx", "gy", None),
        P("gx", "gy"),
        P("gx", "gy", None),
        P("gx", "gy", None, None),
    )
    out = P("gx", "gy", None, None, None, None)

    return jax.shard_map(
        per_device, mesh=mesh, in_specs=placed, out_specs=(out, out), check_vma=False
    )
```

```python
import jax
import jax.numpy as jnp
from jax import lax
from jax.experimental import pallas as pl
from jax.experimental.pallas import tpu as pltpu
from jax.sharding import PartitionSpec as P


PAIRS = 4
DEEP = 2 * PAIRS
SUB = 8
LANES = 128
VMEM_LIMIT = 16 * 2**20

HEAT_SCALE = 25000.0
HEAT_SHIFT = 32000.0
PORE_SCALE = 40000.0
PORE_SHIFT = 7000.0


def encode(values, scale, shift):
    return jnp.floor(values * scale + (0.5 - shift)).astype(jnp.int32).astype(jnp.int16)


def decode(codes, scale, shift):
    return (codes.astype(jnp.int32).astype(jnp.float32) + shift) * (1.0 / scale)


def flag_rows(active_ref, cols):
    lane = lax.broadcasted_iota(jnp.int32, (cols, LANES), 1)
    col = lax.broadcasted_iota(jnp.int32, (cols, LANES), 0)

    def flag(i):
        return jnp.where(col < cols // 2, active_ref[i, 0], active_ref[i, 1])

    return jnp.where(lane < LANES // 2, flag(0), flag(1)).astype(jnp.float32)


def mask_at(ranks):
    choose = lambda i, k, s: (i * ranks + k) * 4 + s
    taken = lambda i, r, s: 8 * ranks + (i * ranks + r) * 4 + s
    again = lambda k, r: 16 * ranks + k * ranks + r
    return choose, taken, again, 16 * ranks + ranks * ranks


def pack_x(
    active_ref, count_ref, slot_ref, heat_ref, pore_ref, out_ref, heat_out, pore_out, mask_ref
):
    rows, cols = heat_ref.shape[0], heat_ref.shape[1]
    ranks = slot_ref.shape[1]
    out_ref[0:rows] = heat_ref[...].astype(jnp.bfloat16)
    out_ref[rows : 2 * rows] = pore_ref[...].astype(jnp.bfloat16)
    out_ref[2 * rows] = flag_rows(active_ref, cols).astype(jnp.bfloat16)
    heat_out[...] = heat_ref[...]
    pore_out[...] = pore_ref[...]
    choose, taken, again, _ = mask_at(ranks)

    def put(row, holds):
        mask_ref[row] = jnp.full((SUB, LANES), jnp.where(holds, 1.0, 0.0), jnp.float32)

    for i in range(2):
        for k in range(ranks):
            for s in range(4):
                here = slot_ref[i, k] == s
                put(choose(i, k, s), here)
                put(taken(i, k, s), here & (k < count_ref[i]))
    for k in range(ranks):
        for r in range(ranks):
            put(again(k, r), (slot_ref[1, k] == slot_ref[0, r]) & (r < count_ref[0]))


def inside(axis, below):
    at = lax.axis_index(axis)
    has = at < lax.axis_size(axis) - 1 if below else at > 0
    return jnp.where(has, 1.0, 0.0).astype(jnp.float32)


def x_parts(own_ref, first_ref, second_ref):
    odd = lax.rem(lax.axis_index("gx") + lax.axis_index("gy"), 2)
    return ((2 - 2 * odd, first_ref), (1, own_ref), (2 * odd, second_ref))


def pack_y(own_ref, first_ref, second_ref, near_out, far_out):
    rows = (own_ref.shape[0] - 1) // 2
    cols = own_ref.shape[1]
    side = 2 * rows
    odd = lax.rem(lax.axis_index("gy"), 2)
    edge = cols - DEEP
    sub = lax.broadcasted_iota(jnp.int32, (DEEP, LANES), 0)
    sides = ((near_out, edge - edge * odd, odd == 0), (far_out, edge * odd, odd == 1))
    for out_ref, start, right in sides:
        at = pl.ds(pl.multiple_of(start, DEEP), DEEP)
        flags = jnp.zeros((DEEP, LANES), jnp.float32)
        for i, part in x_parts(own_ref, first_ref, second_ref):
            flags = jnp.where(sub == i, part[2 * rows, at, :].astype(jnp.float32), flags)
            for f in range(2):
                if part is own_ref:
                    out_ref[pl.ds(f * side, rows)] = part[pl.ds(f * rows, rows), at, :]
                    continue
                for d in range(1, rows // 2 + 1):
                    a, b = (
                        part[f * rows + jnp.where(i == 0, rows - e, e - 1), at, :].astype(jnp.float32)
                        for e in (d, rows - d)
                    )
                    if d < rows - d:
                        a = jnp.where(
                            right,
                            jnp.where(sub >= d, a, pltpu.roll(b, d, 0)),
                            jnp.where(sub < DEEP - d, a, pltpu.roll(b, DEEP - d, 0)),
                        )
                    out_ref[f * side + rows + (i // 2) * (rows // 2) + d - 1] = a.astype(jnp.bfloat16)
        out_ref[2 * side] = flags.astype(jnp.bfloat16)


def edge_row(part, field, x, rows, right):
    side = 2 * rows
    if rows <= x < 2 * rows:
        return part[field * side + x - rows].astype(jnp.float32)
    d = rows - x if x < rows else x - 2 * rows + 1
    at = field * side + rows + (0 if x < rows else rows // 2) - 1
    if d <= rows // 2:
        return part[at + d].astype(jnp.float32)
    if d == rows:
        return part[at + rows // 2].astype(jnp.float32)
    v = part[at + rows - d].astype(jnp.float32)
    return jnp.where(right, pltpu.roll(v, d, 0), pltpu.roll(v, DEEP - d, 0))


def flux_sums(parts):
    lane_open = lax.broadcasted_iota(jnp.int32, (SUB, LANES), 1) < LANES - 1
    depths = []
    for val, wgt, lo, hi in parts:
        depths.append(
            {
                (c, j): (pltpu.roll(v, LANES - 1, 1), pltpu.roll(w, LANES - 1, 1))
                for c in range(lo, hi)
                for j, (v, w) in enumerate(zip(val[c], wgt[c]))
            }
        )
    for (val, wgt, _, _), depth in zip(parts, depths):
        for (c, j), (v, w) in depth.items():
            depth[c, j] = jnp.where(lane_open, (wgt[c][j] + w) * (v - val[c][j]), 0.0)
    for depth in depths:
        for at, f in depth.items():
            depth[at] = f - pltpu.roll(f, 1, 1)

    sums = []
    for (val, wgt, lo, hi), depth in zip(parts, depths):
        n = len(val[lo])
        span = range(n)

        def toward(c):
            return [(wgt[c][j] + wgt[c + 1][j]) * (val[c + 1][j] - val[c][j]) for j in span]

        out = {}
        last = toward(lo - 1)
        for c in range(lo, hi):
            v, w = val[c], wgt[c]
            ahead = toward(c)
            down = [(w[j] + w[j + 1]) * (v[j + 1] - v[j]) for j in range(n - 1)]
            down.append(
                (w[n - 1] + pltpu.roll(w[0], SUB - 1, 0))
                * (pltpu.roll(v[0], SUB - 1, 0) - v[n - 1])
            )
            up = [pltpu.roll(down[-1], 1, 0)] + down[:-1]
            out[c] = [(ahead[j] - last[j]) + (down[j] - up[j]) + depth[c, j] for j in span]
            last = ahead
        sums.append(out)
    return sums


def conduct(parts, mask):
    fluxes = []
    for h, q, lo, hi in parts:
        temp, cond = {}, {}
        for c in range(lo - 1, hi + 1):
            t = [jnp.tanh(v) for v in h[c]]
            temp[c] = [2.5 * v - u for v, u in zip(h[c], t)]
            cond[c] = [(1.0 - v) * (1.0 - v) * (u + 7.0 / 3.0) for v, u in zip(q[c], t)]
        fluxes.append((temp, cond, lo, hi))
    new = {}
    for (h, q, lo, hi), acc in zip(parts, flux_sums(fluxes)):
        for c in range(lo, hi):
            new[c] = [v + m * a for v, m, a in zip(h[c], mask(c, 0), acc[c])]
    return new


def consolidate(parts, mask):
    fluxes = []
    for h, q, lo, hi in parts:
        rate = {
            c: [1.0 + jnp.tanh(2.5 * v - jnp.tanh(v)) for v in h[c]]
            for c in range(lo - 1, hi + 1)
        }
        fluxes.append((q, rate, lo, hi))
    new = {}
    for (q, rate, lo, hi), acc in zip(fluxes, flux_sums(fluxes)):
        for c in range(lo, hi):
            new[c] = [
                v + m * (a - 4.0 * r * v)
                for v, m, a, r in zip(q[c], mask(c, 1), acc[c], rate[c])
            ]
    return new


def tile_rows(marks, i, tx, n, out):
    low = lax.broadcasted_iota(jnp.int32, (SUB, LANES), 1) < LANES // 2
    sub = lax.broadcasted_iota(jnp.int32, (SUB, LANES), 0)
    other = pltpu.roll(marks, LANES // 2, 1)
    for h, flag in ((0, jnp.where(low, marks, other)), (1, jnp.where(low, other, marks))):
        first = (2 * i + h) * tx
        for j in range(n):
            x = sub * n + j
            out[j] = jnp.where((x >= first) & (x < first + tx), flag, out[j])
    return out


def scalings(flags):
    return ([0.009 * f for f in flags], [0.0375 * f for f in flags])


def back(columns, wide, turn, rows, total, heat):
    for c, column in enumerate(columns):
        n = len(column)
        for j, v in enumerate(column):
            wide[pl.ds(c * total + j, SUB, stride=n), :] = 0.5 * v + 1.0 if heat else v
    for c in range(len(columns)):
        turn[pl.ds(c * rows, rows), :] = wide[pl.ds(c * total + DEEP, rows), :]


def inner(
    own_ref, heat_ref, pore_ref, xa_ref, xb_ref,
    heat_edge, pore_edge, heat_save, pore_save, heat_mid, pore_mid, flag_out, wide, turn,
):
    rows, cols = heat_ref.shape[0], heat_ref.shape[1]
    total = rows + 2 * DEEP
    width = cols + 2 * DEEP
    n = total // SUB
    tx, ty = rows // 2, cols // 2
    f32 = jnp.float32
    opens = []
    parts = x_parts(own_ref, xa_ref, xb_ref)
    for i, part in parts:
        opens.append(jnp.where(i == 0, inside("gx", False), inside("gx", True)))

    flags = []
    for k in range(2):
        f = [jnp.zeros((SUB, LANES), f32) for _ in range(n)]
        for (i, part), has in zip(parts, opens):
            marks = part[2 * rows, pl.ds(k * ty, SUB), :].astype(f32)
            f = tile_rows(marks if part is own_ref else marks * has, i, tx, n, f)
        for j in range(n):
            flag_out[k, j] = f[j]
        flags.append(scalings(f))

    def mask(c, kind):
        return flags[0 if c < DEEP + ty else 1][kind]

    h, q = {}, {}
    for field, home, state in ((0, heat_ref, h), (1, pore_ref, q)):
        for (i, part), has in zip(parts, opens):
            for r in range(rows):
                if part is own_ref:
                    v = home[r]
                else:
                    v = part[field * rows + r].astype(f32) * has
                v = 2.0 * v - 2.0 if field == 0 else v
                for g in range(0, cols, SUB):
                    at = pl.multiple_of(g * total + (i * rows + r) * SUB, SUB)
                    wide[field, pl.ds(at, SUB), :] = v[g : g + SUB]
        for c in range(cols):
            at = c // SUB * SUB * total + c % SUB
            state[DEEP + c] = [
                wide[field, pl.ds(at + j * SUB, SUB, stride=n * SUB), :] for j in range(n)
            ]

    for p in range(PAIRS):
        lo, hi = DEEP + 2 * p + 1, width - DEEP - 2 * p - 1
        for side, c in ((0, lo), (1, hi - 1)):
            for j in range(n):
                heat_save[p, side, j] = h[c][j]
        h.update(conduct([(h, q, lo, hi)], mask))
        lo, hi = lo + 1, hi - 1
        for side, c in ((0, lo), (1, hi - 1)):
            for j in range(n):
                pore_save[p, side, j] = q[c][j]
        q.update(consolidate([(h, q, lo, hi)], mask))

    for field, state, edge, mid in ((0, h, heat_edge, heat_mid), (1, q, pore_edge, pore_mid)):
        for c in range(DEEP + 1):
            for j in range(n):
                edge[0, c, j] = state[DEEP + c][j]
                edge[1, c, j] = state[width - DEEP - 1 - c][j]
        back(
            [state[c] for c in range(2 * DEEP, width - 2 * DEEP)], wide.at[field], turn.at[field],
            rows, total, field == 0,
        )
        for r in range(rows):
            for g in range(0, cols - 2 * DEEP, SUB):
                mid[r, g : g + SUB] = turn[field, pl.ds(g * rows + r, SUB, stride=rows), :]


def edges(
    mask_ref, heat_edge, pore_edge, heat_save, pore_save, heat_mid, pore_mid, flag_ref, yn_ref, yf_ref,
    heat_out, pore_out, send_ref, later_ref, wide, turn, block,
):
    rows, cols = heat_mid.shape[0], heat_mid.shape[1] + 2 * DEEP
    total = rows + 2 * DEEP
    width = cols + 2 * DEEP
    n = total // SUB
    tx, ty = rows // 2, cols // 2
    f32 = jnp.float32
    odd = lax.rem(lax.axis_index("gy"), 2)
    row_open = (inside("gx", False), None, inside("gx", True))
    far_open = jnp.where(odd == 1, inside("gy", True), inside("gy", False))
    parts = ((1 - odd, yn_ref, None, odd == 1), (odd, yf_ref, far_open, odd == 0))

    def scaled(v, *by):
        for s in by:
            v = v if s is None else v * s
        return v

    halves = []
    for at, part, has, _ in parts:
        marks = scaled(part[4 * rows].astype(f32), has)
        f = [jnp.zeros((SUB, LANES), f32) for _ in range(n)]
        for i in range(3):
            f = tile_rows(
                jnp.broadcast_to(scaled(marks[i : i + 1], row_open[i]), (SUB, LANES)), i, tx, n, f
            )
        halves.append(f)
    near, far = halves
    left = [jnp.where(odd == 1, a, b) for a, b in zip(near, far)]
    right = [jnp.where(odd == 1, b, a) for a, b in zip(near, far)]
    flags = [
        scalings(f)
        for f in (left, *([flag_ref[k, j] for j in range(n)] for k in range(2)), right)
    ]

    def mask(c, kind):
        return flags[0 if c < DEEP else 1 if c < DEEP + ty else 2 if c < DEEP + cols else 3][kind]

    pair = 2 * DEEP
    h, q = {}, {}
    for field, edge, state in ((0, heat_edge, h), (1, pore_edge, q)):
        for at, part, has, right_end in parts:
            for x in range(total):
                v = scaled(edge_row(part, field, x, rows, right_end), has, row_open[x // rows])
                into = pl.multiple_of(at * DEEP * total + x * DEEP, SUB)
                wide[field, pl.ds(into, DEEP), :] = 2.0 * v - 2.0 if field == 0 else v
        for c in range(DEEP):
            for first, halo in ((0, c), (DEEP, width - DEEP + c)):
                state[halo] = [
                    wide[field, pl.ds(first * total + j * DEEP + c, SUB, stride=n * DEEP), :]
                    for j in range(n)
                ]
        for c in range(DEEP + 1):
            state[DEEP + c] = [edge[0, c, j] for j in range(n)]
            state[width - DEEP - 1 - c] = [edge[1, c, j] for j in range(n)]

    for p in range(PAIRS):
        lo = 2 * p + 1
        hi = width - lo
        parts = []
        for side, a, b, c in ((0, lo, lo + DEEP, lo + DEEP), (1, hi - DEEP, hi, hi - DEEP - 1)):
            then = dict(h)
            then[c] = [heat_save[p, side, j] for j in range(n)]
            parts.append((then, q, a, b))
        h.update(conduct(parts, mask))
        lo, hi = lo + 1, hi - 1
        parts = []
        for side, a, b, c in ((0, lo, lo + DEEP, lo + DEEP), (1, hi - DEEP, hi, hi - DEEP - 1)):
            then = dict(q)
            then[c] = [pore_save[p, side, j] for j in range(n)]
            parts.append((h, then, a, b))
        q.update(consolidate(parts, mask))

    for field, state, mid, out in ((0, h, heat_mid, heat_out), (1, q, pore_mid, pore_out)):
        ends = [*range(DEEP, pair), *range(width - pair, width - DEEP)]
        back([state[c] for c in ends], wide.at[field], turn.at[field], rows, total, field == 0)
        for r in range(rows):
            block[field, r, 0:DEEP] = turn[field, pl.ds(r, DEEP, stride=rows), :]
            block[field, r, DEEP : cols - DEEP] = mid[r]
            block[field, r, cols - DEEP :] = turn[
                field, pl.ds(DEEP * rows + r, DEEP, stride=rows), :
            ]
        for i in range(2):
            for k in range(2):
                out[2 * i + k] = block[field, i * tx : (i + 1) * tx, k * ty : (k + 1) * ty, :]
    ranks = send_ref.shape[0]
    choose = mask_at(ranks)[0]
    shape = (tx, ty, LANES)
    for field, src, scale, shift in (
        (0, heat_out, HEAT_SCALE, HEAT_SHIFT),
        (1, pore_out, PORE_SCALE, PORE_SHIFT),
    ):
        for i, out in ((0, send_ref), (1, later_ref)):
            for k in range(ranks):
                v = src[0]
                for s in range(1, 4):
                    v = jnp.where(held(mask_ref, choose(i, k, s), shape), src[s], v)
                out[k, field] = encode(v, scale, shift)


def held(mask_ref, row, shape):
    m = mask_ref[row]
    m = jnp.concatenate([m] * (shape[1] // SUB), axis=0)
    return jnp.broadcast_to(m[None], shape) > 0.5


def resend(mask_ref, got_ref, local_ref, send_ref):
    ranks = got_ref.shape[0]
    shape = got_ref.shape[2:]
    again = mask_at(ranks)[2]
    for k in range(ranks):
        for f in range(2):
            v = local_ref[k, f].astype(jnp.int32)
            for r in range(ranks):
                v = jnp.where(
                    held(mask_ref, again(k, r), shape), got_ref[r, f].astype(jnp.int32), v
                )
            send_ref[k, f] = v.astype(jnp.int16)


def place(mask_ref, heat_ref, pore_ref, first_ref, second_ref, heat_out, pore_out):
    ranks = first_ref.shape[0]
    shape = first_ref.shape[2:]
    taken = mask_at(ranks)[1]
    for field, src, out, scale, shift in (
        (0, heat_ref, heat_out, HEAT_SCALE, HEAT_SHIFT),
        (1, pore_ref, pore_out, PORE_SCALE, PORE_SHIFT),
    ):
        came = [
            (i, r, decode(got[r, field], scale, shift))
            for i, got in ((0, first_ref), (1, second_ref))
            for r in range(ranks)
        ]
        for s in range(4):
            v = src[s]
            for i, r, tile in came:
                v = jnp.where(held(mask_ref, taken(i, r, s), shape), tile, v)
            out[s] = v


def call(body, spec, outs, scratch=(), out_space=pltpu.VMEM):
    def run(*args):
        space = {"s": pltpu.SMEM, "v": pltpu.VMEM, "V": pltpu.VMEM}
        args = [
            pltpu.with_memory_space_constraint(a, pltpu.VMEM if c == "V" else pltpu.HBM)
            for c, a in zip(spec, args)
        ]
        shapes = [
            pltpu.VMEM(s, d) if out_space is not None else jax.ShapeDtypeStruct(s, d)
            for s, d in outs
        ]
        return pl.pallas_call(
            body,
            in_specs=[pl.BlockSpec(memory_space=space[c]) for c in spec],
            out_specs=[pl.BlockSpec(memory_space=pltpu.VMEM) for _ in outs],
            out_shape=shapes,
            scratch_shapes=list(scratch),
            compiler_params=pltpu.CompilerParams(vmem_limit_bytes=VMEM_LIMIT),
        )(*args)

    return run


def permute(value, partner):
    nx, ny = lax.axis_size("gx"), lax.axis_size("gy")
    pairs = []
    for x in range(nx):
        for y in range(ny):
            u, v = partner(x, y)
            pairs.append((x * ny + y, u * ny + v))
    return lax.ppermute(value, ("gx", "gy"), pairs)


def exchange_x(value):
    nx, ny = lax.axis_size("gx"), lax.axis_size("gy")

    def partner(x, y, near):
        if near:
            return x ^ 1, y
        if 0 < x < nx - 1:
            return ((x + 1) ^ 1) - 1, y
        return (x, y ^ 2) if ny % 4 == 0 else (x, y)

    first = permute(value, lambda x, y: partner(x, y, y % 2 == 0))
    second = permute(value, lambda x, y: partner(x, y, y % 2 == 1))
    return first, second


def exchange_y(near, far):
    ny = lax.axis_size("gy")

    def partner(x, y):
        if 0 < y < ny - 1:
            return x, ((y + 1) ^ 1) - 1
        return x ^ 1, y

    far = permute(far, partner)
    near = permute(near, lambda x, y: (x, y ^ 1))
    return near, far


def swap(value, axis):
    n = lax.axis_size(axis)
    return lax.ppermute(value, axis, [(i, (i + n // 2) % n) for i in range(n)])


def per_device(enthalpy, porosity, active, move_count, move_slot):
    rows, cols, depth = enthalpy.shape
    tx, ty = rows // 2, cols // 2
    count = move_count.reshape(2)
    slots = move_slot.reshape(2, move_slot.shape[-1])
    ranks = slots.shape[1]
    f32, bf16, i16 = jnp.float32, jnp.bfloat16, jnp.int16

    block = ((rows, cols, depth), f32)
    masks = ((mask_at(ranks)[3], SUB, LANES), f32)
    own, enthalpy, porosity, masks = call(
        pack_x, "sssvv", [((2 * rows + 1, cols, depth), bf16), block, block, masks]
    )(active, count, slots, enthalpy, porosity)
    x_near, x_far = exchange_x(own)
    side = ((4 * rows + 1, DEEP, depth), bf16)
    near, far = call(pack_y, "VVV", [side, side])(own, x_near, x_far)
    y_near, y_far = exchange_y(near, far)
    total = rows + 2 * DEEP
    n = total // SUB
    tiles = ((4, tx, ty, depth), f32)
    parcel = ((ranks, 2, tx, ty, depth), i16)
    edge = ((2, DEEP + 1, n, SUB, depth), f32)
    save = ((PAIRS, 2, n, SUB, depth), f32)
    mid = ((rows, cols - 2 * DEEP, depth), f32)
    flag = ((2, n, SUB, depth), f32)
    state = call(
        inner, "VVVVV", [edge, edge, save, save, mid, mid, flag],
        [
            pltpu.VMEM((2, total * cols, depth), f32),
            pltpu.VMEM((2, rows * (cols - 2 * DEEP), depth), f32),
        ],
    )(own, enthalpy, porosity, x_near, x_far)
    heat, pore, first, later = call(
        edges, "V" * 10, [tiles, tiles, parcel, parcel],
        [
            pltpu.VMEM((2, total * 2 * DEEP, depth), f32),
            pltpu.VMEM((2, rows * 2 * DEEP, depth), f32),
            pltpu.VMEM((2, rows, cols, depth), f32),
        ],
    )(masks, *state, y_near, y_far)
    first = swap(first, "gx")
    (second,) = call(resend, "VVV", [parcel])(masks, first, later)
    second = swap(second, "gy")
    heat, pore = call(place, "VVVVV", [tiles, tiles], out_space=None)(
        masks, heat, pore, first, second
    )
    return heat[None, None], pore[None, None]


def solution(mesh):
    placed = (
        P("gx", "gy", None),
        P("gx", "gy", None),
        P("gx", "gy"),
        P("gx", "gy", None),
        P("gx", "gy", None, None),
    )
    out = P("gx", "gy", None, None, None, None)

    return jax.shard_map(
        per_device, mesh=mesh, in_specs=placed, out_specs=(out, out), check_vma=False
    )
```

```python
import jax
import jax.numpy as jnp
from jax import lax
from jax.experimental import pallas as pl
from jax.experimental.pallas import tpu as pltpu
from jax.sharding import PartitionSpec as P


PAIRS = 4
DEEP = 2 * PAIRS
PARTS = 4
SUB = 8
LANES = 128
VMEM_LIMIT = 16 * 2**20

HEAT_SCALE = 25000.0
HEAT_SHIFT = 32000.0
PORE_SCALE = 40000.0
PORE_SHIFT = 7000.0


def encode(values, scale, shift):
    return jnp.floor(values * scale + (0.5 - shift)).astype(jnp.int32).astype(jnp.int16)


def decode(codes, scale, shift):
    return (codes.astype(jnp.int32).astype(jnp.float32) + shift) * (1.0 / scale)


def flag_rows(active_ref, cols):
    lane = lax.broadcasted_iota(jnp.int32, (cols, LANES), 1)
    col = lax.broadcasted_iota(jnp.int32, (cols, LANES), 0)

    def flag(i):
        return jnp.where(col < cols // 2, active_ref[i, 0], active_ref[i, 1])

    return jnp.where(lane < LANES // 2, flag(0), flag(1)).astype(jnp.float32)


def mask_at(ranks):
    choose = lambda i, k, s: (i * ranks + k) * 4 + s
    taken = lambda i, r, s: 8 * ranks + (i * ranks + r) * 4 + s
    again = lambda k, r: 16 * ranks + k * ranks + r
    return choose, taken, again, 16 * ranks + ranks * ranks


def pack_x(
    active_in, count_in, slot_in, heat_in, pore_in, out_ref, heat_ref, pore_ref, mask_ref,
    active_ref, count_ref, slot_ref, sems,
):
    rows, cols = heat_ref.shape[0], heat_ref.shape[1]
    ranks = slot_ref.shape[1]
    part = rows // PARTS
    copies = []

    def fetch(src, dst):
        copies.append(pltpu.make_async_copy(src, dst, sems.at[len(copies)]))
        copies[-1].start()

    for src, dst in ((heat_in, heat_ref), (pore_in, pore_ref)):
        for i in range(PARTS):
            at = pl.ds(i * part, part)
            fetch(src.at[at], dst.at[at])
    for src, dst in ((active_in, active_ref), (count_in, count_ref), (slot_in, slot_ref)):
        fetch(src, dst)
    for copy in copies:
        copy.wait()
    out_ref[0:rows] = heat_ref[...].astype(jnp.bfloat16)
    out_ref[rows : 2 * rows] = pore_ref[...].astype(jnp.bfloat16)
    out_ref[2 * rows] = flag_rows(active_ref, cols).astype(jnp.bfloat16)
    choose, taken, again, _ = mask_at(ranks)

    def put(row, holds):
        mask_ref[row] = jnp.full((SUB, LANES), jnp.where(holds, 1.0, 0.0), jnp.float32)

    for i in range(2):
        for k in range(ranks):
            for s in range(4):
                here = slot_ref[i, k] == s
                put(choose(i, k, s), here)
                put(taken(i, k, s), here & (k < count_ref[i]))
    for k in range(ranks):
        for r in range(ranks):
            put(again(k, r), (slot_ref[1, k] == slot_ref[0, r]) & (r < count_ref[0]))


def inside(axis, below):
    at = lax.axis_index(axis)
    has = at < lax.axis_size(axis) - 1 if below else at > 0
    return jnp.where(has, 1.0, 0.0).astype(jnp.float32)


def x_parts(own_ref, first_ref, second_ref):
    odd = lax.rem(lax.axis_index("gx") + lax.axis_index("gy"), 2)
    return ((2 - 2 * odd, first_ref), (1, own_ref), (2 * odd, second_ref))


def pack_y(own_ref, first_ref, second_ref, near_out, far_out):
    rows = (own_ref.shape[0] - 1) // 2
    cols = own_ref.shape[1]
    side = 2 * rows
    odd = lax.rem(lax.axis_index("gy"), 2)
    edge = cols - DEEP
    sub = lax.broadcasted_iota(jnp.int32, (DEEP, LANES), 0)
    sides = ((near_out, edge - edge * odd, odd == 0), (far_out, edge * odd, odd == 1))
    for out_ref, start, right in sides:
        at = pl.ds(pl.multiple_of(start, DEEP), DEEP)
        flags = jnp.zeros((DEEP, LANES), jnp.float32)
        for i, part in x_parts(own_ref, first_ref, second_ref):
            flags = jnp.where(sub == i, part[2 * rows, at, :].astype(jnp.float32), flags)
            for f in range(2):
                if part is own_ref:
                    out_ref[pl.ds(f * side, rows)] = part[pl.ds(f * rows, rows), at, :]
                    continue
                for d in range(1, rows // 2 + 1):
                    a, b = (
                        part[f * rows + jnp.where(i == 0, rows - e, e - 1), at, :].astype(jnp.float32)
                        for e in (d, rows - d)
                    )
                    if d < rows - d:
                        a = jnp.where(
                            right,
                            jnp.where(sub >= d, a, pltpu.roll(b, d, 0)),
                            jnp.where(sub < DEEP - d, a, pltpu.roll(b, DEEP - d, 0)),
                        )
                    out_ref[f * side + rows + (i // 2) * (rows // 2) + d - 1] = a.astype(jnp.bfloat16)
        out_ref[2 * side] = flags.astype(jnp.bfloat16)


def edge_row(part, field, x, rows, right):
    side = 2 * rows
    if rows <= x < 2 * rows:
        return part[field * side + x - rows].astype(jnp.float32)
    d = rows - x if x < rows else x - 2 * rows + 1
    at = field * side + rows + (0 if x < rows else rows // 2) - 1
    if d <= rows // 2:
        return part[at + d].astype(jnp.float32)
    if d == rows:
        return part[at + rows // 2].astype(jnp.float32)
    v = part[at + rows - d].astype(jnp.float32)
    return jnp.where(right, pltpu.roll(v, d, 0), pltpu.roll(v, DEEP - d, 0))


def flux_sums(parts):
    lane_open = lax.broadcasted_iota(jnp.int32, (SUB, LANES), 1) < LANES - 1
    depths = []
    for val, wgt, lo, hi in parts:
        depths.append(
            {
                (c, j): (pltpu.roll(v, LANES - 1, 1), pltpu.roll(w, LANES - 1, 1))
                for c in range(lo, hi)
                for j, (v, w) in enumerate(zip(val[c], wgt[c]))
            }
        )
    for (val, wgt, _, _), depth in zip(parts, depths):
        for (c, j), (v, w) in depth.items():
            depth[c, j] = jnp.where(lane_open, (wgt[c][j] + w) * (v - val[c][j]), 0.0)
    for depth in depths:
        for at, f in depth.items():
            depth[at] = f - pltpu.roll(f, 1, 1)

    sums = []
    for (val, wgt, lo, hi), depth in zip(parts, depths):
        n = len(val[lo])
        span = range(n)

        def toward(c):
            return [(wgt[c][j] + wgt[c + 1][j]) * (val[c + 1][j] - val[c][j]) for j in span]

        out = {}
        last = toward(lo - 1)
        for c in range(lo, hi):
            v, w = val[c], wgt[c]
            ahead = toward(c)
            down = [(w[j] + w[j + 1]) * (v[j + 1] - v[j]) for j in range(n - 1)]
            down.append(
                (w[n - 1] + pltpu.roll(w[0], SUB - 1, 0))
                * (pltpu.roll(v[0], SUB - 1, 0) - v[n - 1])
            )
            up = [pltpu.roll(down[-1], 1, 0)] + down[:-1]
            out[c] = [(ahead[j] - last[j]) + (down[j] - up[j]) + depth[c, j] for j in span]
            last = ahead
        sums.append(out)
    return sums


def conduct(parts, mask):
    fluxes = []
    for h, q, lo, hi in parts:
        temp, cond = {}, {}
        for c in range(lo - 1, hi + 1):
            t = [jnp.tanh(v) for v in h[c]]
            temp[c] = [2.5 * v - u for v, u in zip(h[c], t)]
            cond[c] = [(1.0 - v) * (1.0 - v) * (u + 7.0 / 3.0) for v, u in zip(q[c], t)]
        fluxes.append((temp, cond, lo, hi))
    new = {}
    for (h, q, lo, hi), acc in zip(parts, flux_sums(fluxes)):
        for c in range(lo, hi):
            new[c] = [v + m * a for v, m, a in zip(h[c], mask(c, 0), acc[c])]
    return new


def consolidate(parts, mask):
    fluxes = []
    for h, q, lo, hi in parts:
        rate = {
            c: [1.0 + jnp.tanh(2.5 * v - jnp.tanh(v)) for v in h[c]]
            for c in range(lo - 1, hi + 1)
        }
        fluxes.append((q, rate, lo, hi))
    new = {}
    for (q, rate, lo, hi), acc in zip(fluxes, flux_sums(fluxes)):
        for c in range(lo, hi):
            new[c] = [
                v + m * (a - 4.0 * r * v)
                for v, m, a, r in zip(q[c], mask(c, 1), acc[c], rate[c])
            ]
    return new


def tile_rows(marks, i, tx, n, out):
    low = lax.broadcasted_iota(jnp.int32, (SUB, LANES), 1) < LANES // 2
    sub = lax.broadcasted_iota(jnp.int32, (SUB, LANES), 0)
    other = pltpu.roll(marks, LANES // 2, 1)
    for h, flag in ((0, jnp.where(low, marks, other)), (1, jnp.where(low, other, marks))):
        first = (2 * i + h) * tx
        for j in range(n):
            x = sub * n + j
            out[j] = jnp.where((x >= first) & (x < first + tx), flag, out[j])
    return out


def scalings(flags):
    return ([0.009 * f for f in flags], [0.0375 * f for f in flags])


def back(columns, wide, turn, rows, total, heat):
    for c, column in enumerate(columns):
        n = len(column)
        for j, v in enumerate(column):
            wide[pl.ds(c * total + j, SUB, stride=n), :] = 0.5 * v + 1.0 if heat else v
    for c in range(len(columns)):
        turn[pl.ds(c * rows, rows), :] = wide[pl.ds(c * total + DEEP, rows), :]


def inner(
    own_ref, heat_ref, pore_ref, xa_ref, xb_ref,
    heat_edge, pore_edge, heat_save, pore_save, heat_mid, pore_mid, flag_out, wide, turn,
):
    rows, cols = heat_ref.shape[0], heat_ref.shape[1]
    total = rows + 2 * DEEP
    width = cols + 2 * DEEP
    n = total // SUB
    tx, ty = rows // 2, cols // 2
    f32 = jnp.float32
    opens = []
    parts = x_parts(own_ref, xa_ref, xb_ref)
    for i, part in parts:
        opens.append(jnp.where(i == 0, inside("gx", False), inside("gx", True)))

    flags = []
    for k in range(2):
        f = [jnp.zeros((SUB, LANES), f32) for _ in range(n)]
        for (i, part), has in zip(parts, opens):
            marks = part[2 * rows, pl.ds(k * ty, SUB), :].astype(f32)
            f = tile_rows(marks if part is own_ref else marks * has, i, tx, n, f)
        for j in range(n):
            flag_out[k, j] = f[j]
        flags.append(scalings(f))

    def mask(c, kind):
        return flags[0 if c < DEEP + ty else 1][kind]

    h, q = {}, {}
    for field, home, state in ((0, heat_ref, h), (1, pore_ref, q)):
        for (i, part), has in zip(parts, opens):
            for r in range(rows):
                if part is own_ref:
                    v = home[r]
                else:
                    v = part[field * rows + r].astype(f32) * has
                v = 2.0 * v - 2.0 if field == 0 else v
                for g in range(0, cols, SUB):
                    at = pl.multiple_of(g * total + (i * rows + r) * SUB, SUB)
                    wide[field, pl.ds(at, SUB), :] = v[g : g + SUB]
        for c in range(cols):
            at = c // SUB * SUB * total + c % SUB
            state[DEEP + c] = [
                wide[field, pl.ds(at + j * SUB, SUB, stride=n * SUB), :] for j in range(n)
            ]

    for p in range(PAIRS):
        lo, hi = DEEP + 2 * p + 1, width - DEEP - 2 * p - 1
        for side, c in ((0, lo), (1, hi - 1)):
            for j in range(n):
                heat_save[p, side, j] = h[c][j]
        h.update(conduct([(h, q, lo, hi)], mask))
        lo, hi = lo + 1, hi - 1
        for side, c in ((0, lo), (1, hi - 1)):
            for j in range(n):
                pore_save[p, side, j] = q[c][j]
        q.update(consolidate([(h, q, lo, hi)], mask))

    for field, state, edge, mid in ((0, h, heat_edge, heat_mid), (1, q, pore_edge, pore_mid)):
        for c in range(DEEP + 1):
            for j in range(n):
                edge[0, c, j] = state[DEEP + c][j]
                edge[1, c, j] = state[width - DEEP - 1 - c][j]
        back(
            [state[c] for c in range(2 * DEEP, width - 2 * DEEP)], wide.at[field], turn.at[field],
            rows, total, field == 0,
        )
        for r in range(rows):
            for g in range(0, cols - 2 * DEEP, SUB):
                mid[r, g : g + SUB] = turn[field, pl.ds(g * rows + r, SUB, stride=rows), :]


def edges(
    mask_ref, heat_edge, pore_edge, heat_save, pore_save, heat_mid, pore_mid, flag_ref, yn_ref, yf_ref,
    heat_out, pore_out, send_ref, later_ref, wide, turn, block,
):
    rows, cols = heat_mid.shape[0], heat_mid.shape[1] + 2 * DEEP
    total = rows + 2 * DEEP
    width = cols + 2 * DEEP
    n = total // SUB
    tx, ty = rows // 2, cols // 2
    f32 = jnp.float32
    odd = lax.rem(lax.axis_index("gy"), 2)
    row_open = (inside("gx", False), None, inside("gx", True))
    far_open = jnp.where(odd == 1, inside("gy", True), inside("gy", False))
    parts = ((1 - odd, yn_ref, None, odd == 1), (odd, yf_ref, far_open, odd == 0))

    def scaled(v, *by):
        for s in by:
            v = v if s is None else v * s
        return v

    halves = []
    for at, part, has, _ in parts:
        marks = scaled(part[4 * rows].astype(f32), has)
        f = [jnp.zeros((SUB, LANES), f32) for _ in range(n)]
        for i in range(3):
            f = tile_rows(
                jnp.broadcast_to(scaled(marks[i : i + 1], row_open[i]), (SUB, LANES)), i, tx, n, f
            )
        halves.append(f)
    near, far = halves
    left = [jnp.where(odd == 1, a, b) for a, b in zip(near, far)]
    right = [jnp.where(odd == 1, b, a) for a, b in zip(near, far)]
    flags = [
        scalings(f)
        for f in (left, *([flag_ref[k, j] for j in range(n)] for k in range(2)), right)
    ]

    def mask(c, kind):
        return flags[0 if c < DEEP else 1 if c < DEEP + ty else 2 if c < DEEP + cols else 3][kind]

    pair = 2 * DEEP
    h, q = {}, {}
    for field, edge, state in ((0, heat_edge, h), (1, pore_edge, q)):
        for at, part, has, right_end in parts:
            for x in range(total):
                v = scaled(edge_row(part, field, x, rows, right_end), has, row_open[x // rows])
                into = pl.multiple_of(at * DEEP * total + x * DEEP, SUB)
                wide[field, pl.ds(into, DEEP), :] = 2.0 * v - 2.0 if field == 0 else v
        for c in range(DEEP):
            for first, halo in ((0, c), (DEEP, width - DEEP + c)):
                state[halo] = [
                    wide[field, pl.ds(first * total + j * DEEP + c, SUB, stride=n * DEEP), :]
                    for j in range(n)
                ]
        for c in range(DEEP + 1):
            state[DEEP + c] = [edge[0, c, j] for j in range(n)]
            state[width - DEEP - 1 - c] = [edge[1, c, j] for j in range(n)]

    for p in range(PAIRS):
        lo = 2 * p + 1
        hi = width - lo
        parts = []
        for side, a, b, c in ((0, lo, lo + DEEP, lo + DEEP), (1, hi - DEEP, hi, hi - DEEP - 1)):
            then = dict(h)
            then[c] = [heat_save[p, side, j] for j in range(n)]
            parts.append((then, q, a, b))
        h.update(conduct(parts, mask))
        lo, hi = lo + 1, hi - 1
        parts = []
        for side, a, b, c in ((0, lo, lo + DEEP, lo + DEEP), (1, hi - DEEP, hi, hi - DEEP - 1)):
            then = dict(q)
            then[c] = [pore_save[p, side, j] for j in range(n)]
            parts.append((h, then, a, b))
        q.update(consolidate(parts, mask))

    for field, state, mid, out in ((0, h, heat_mid, heat_out), (1, q, pore_mid, pore_out)):
        ends = [*range(DEEP, pair), *range(width - pair, width - DEEP)]
        back([state[c] for c in ends], wide.at[field], turn.at[field], rows, total, field == 0)
        for r in range(rows):
            block[field, r, 0:DEEP] = turn[field, pl.ds(r, DEEP, stride=rows), :]
            block[field, r, DEEP : cols - DEEP] = mid[r]
            block[field, r, cols - DEEP :] = turn[
                field, pl.ds(DEEP * rows + r, DEEP, stride=rows), :
            ]
        for i in range(2):
            for k in range(2):
                out[2 * i + k] = block[field, i * tx : (i + 1) * tx, k * ty : (k + 1) * ty, :]
    ranks = send_ref.shape[0]
    choose = mask_at(ranks)[0]
    shape = (tx, ty, LANES)
    for field, src, scale, shift in (
        (0, heat_out, HEAT_SCALE, HEAT_SHIFT),
        (1, pore_out, PORE_SCALE, PORE_SHIFT),
    ):
        for i, out in ((0, send_ref), (1, later_ref)):
            for k in range(ranks):
                v = src[0]
                for s in range(1, 4):
                    v = jnp.where(held(mask_ref, choose(i, k, s), shape), src[s], v)
                out[k, field] = encode(v, scale, shift)


def held(mask_ref, row, shape):
    m = mask_ref[row]
    m = jnp.concatenate([m] * (shape[1] // SUB), axis=0)
    return jnp.broadcast_to(m[None], shape) > 0.5


def resend(mask_ref, got_ref, local_ref, send_ref):
    ranks = got_ref.shape[0]
    shape = got_ref.shape[2:]
    again = mask_at(ranks)[2]
    for k in range(ranks):
        for f in range(2):
            v = local_ref[k, f].astype(jnp.int32)
            for r in range(ranks):
                v = jnp.where(
                    held(mask_ref, again(k, r), shape), got_ref[r, f].astype(jnp.int32), v
                )
            send_ref[k, f] = v.astype(jnp.int16)


def place(mask_ref, heat_ref, pore_ref, first_ref, second_ref, heat_out, pore_out, tiles, sems):
    ranks = first_ref.shape[0]
    shape = first_ref.shape[2:]
    taken = mask_at(ranks)[1]
    copies = []
    for field, src, out, scale, shift in (
        (0, heat_ref, heat_out, HEAT_SCALE, HEAT_SHIFT),
        (1, pore_ref, pore_out, PORE_SCALE, PORE_SHIFT),
    ):
        came = [
            (i, r, decode(got[r, field], scale, shift))
            for i, got in ((0, first_ref), (1, second_ref))
            for r in range(ranks)
        ]
        for s in range(4):
            v = src[s]
            for i, r, tile in came:
                v = jnp.where(held(mask_ref, taken(i, r, s), shape), tile, v)
            tiles[field, s] = v
            copies.append(
                pltpu.make_async_copy(tiles.at[field, s], out.at[s], sems.at[2 * s + field])
            )
            copies[-1].start()
    for copy in copies:
        copy.wait()


def call(body, spec, outs, scratch=(), out_space=pltpu.VMEM):
    def run(*args):
        space = {"h": pltpu.HBM, "V": pltpu.VMEM}
        args = [
            pltpu.with_memory_space_constraint(a, pltpu.VMEM if c == "V" else pltpu.HBM)
            for c, a in zip(spec, args)
        ]
        shapes = [
            pltpu.VMEM(s, d) if out_space is pltpu.VMEM else jax.ShapeDtypeStruct(s, d)
            for s, d in outs
        ]
        return pl.pallas_call(
            body,
            in_specs=[pl.BlockSpec(memory_space=space[c]) for c in spec],
            out_specs=[pl.BlockSpec(memory_space=out_space) for _ in outs],
            out_shape=shapes,
            scratch_shapes=list(scratch),
            compiler_params=pltpu.CompilerParams(vmem_limit_bytes=VMEM_LIMIT),
        )(*args)

    return run


def permute(value, partner):
    nx, ny = lax.axis_size("gx"), lax.axis_size("gy")
    pairs = []
    for x in range(nx):
        for y in range(ny):
            u, v = partner(x, y)
            pairs.append((x * ny + y, u * ny + v))
    return lax.ppermute(value, ("gx", "gy"), pairs)


def exchange_x(value):
    nx, ny = lax.axis_size("gx"), lax.axis_size("gy")

    def partner(x, y, near):
        if near:
            return x ^ 1, y
        if 0 < x < nx - 1:
            return ((x + 1) ^ 1) - 1, y
        return (x, y ^ 2) if ny % 4 == 0 else (x, y)

    first = permute(value, lambda x, y: partner(x, y, y % 2 == 0))
    second = permute(value, lambda x, y: partner(x, y, y % 2 == 1))
    return first, second


def exchange_y(near, far):
    ny = lax.axis_size("gy")

    def partner(x, y):
        if 0 < y < ny - 1:
            return x, ((y + 1) ^ 1) - 1
        return x ^ 1, y

    far = permute(far, partner)
    near = permute(near, lambda x, y: (x, y ^ 1))
    return near, far


def swap(value, axis):
    n = lax.axis_size(axis)
    return lax.ppermute(value, axis, [(i, (i + n // 2) % n) for i in range(n)])


def per_device(enthalpy, porosity, active, move_count, move_slot):
    rows, cols, depth = enthalpy.shape
    tx, ty = rows // 2, cols // 2
    count = move_count.reshape(2)
    slots = move_slot.reshape(2, move_slot.shape[-1])
    ranks = slots.shape[1]
    f32, bf16, i16 = jnp.float32, jnp.bfloat16, jnp.int16

    block = ((rows, cols, depth), f32)
    masks = ((mask_at(ranks)[3], SUB, LANES), f32)
    own, enthalpy, porosity, masks = call(
        pack_x, "hhhhh", [((2 * rows + 1, cols, depth), bf16), block, block, masks],
        [
            pltpu.SMEM(active.shape, active.dtype),
            pltpu.SMEM(count.shape, count.dtype),
            pltpu.SMEM(slots.shape, slots.dtype),
            pltpu.SemaphoreType.DMA((2 * PARTS + 3,)),
        ],
    )(active, count, slots, enthalpy, porosity)
    x_near, x_far = exchange_x(own)
    side = ((4 * rows + 1, DEEP, depth), bf16)
    near, far = call(pack_y, "VVV", [side, side])(own, x_near, x_far)
    y_near, y_far = exchange_y(near, far)
    total = rows + 2 * DEEP
    n = total // SUB
    tiles = ((4, tx, ty, depth), f32)
    parcel = ((ranks, 2, tx, ty, depth), i16)
    edge = ((2, DEEP + 1, n, SUB, depth), f32)
    save = ((PAIRS, 2, n, SUB, depth), f32)
    mid = ((rows, cols - 2 * DEEP, depth), f32)
    flag = ((2, n, SUB, depth), f32)
    state = call(
        inner, "VVVVV", [edge, edge, save, save, mid, mid, flag],
        [
            pltpu.VMEM((2, total * cols, depth), f32),
            pltpu.VMEM((2, rows * (cols - 2 * DEEP), depth), f32),
        ],
    )(own, enthalpy, porosity, x_near, x_far)
    heat, pore, first, later = call(
        edges, "V" * 10, [tiles, tiles, parcel, parcel],
        [
            pltpu.VMEM((2, total * 2 * DEEP, depth), f32),
            pltpu.VMEM((2, rows * 2 * DEEP, depth), f32),
            pltpu.VMEM((2, rows, cols, depth), f32),
        ],
    )(masks, *state, y_near, y_far)
    first = swap(first, "gx")
    (second,) = call(resend, "VVV", [parcel])(masks, first, later)
    second = swap(second, "gy")
    heat, pore = call(
        place, "VVVVV", [tiles, tiles],
        [pltpu.VMEM((2, 4, tx, ty, depth), f32), pltpu.SemaphoreType.DMA((8,))],
        out_space=pltpu.HBM,
    )(
        masks, heat, pore, first, second
    )
    return heat[None, None], pore[None, None]


def solution(mesh):
    placed = (
        P("gx", "gy", None),
        P("gx", "gy", None),
        P("gx", "gy"),
        P("gx", "gy", None),
        P("gx", "gy", None, None),
    )
    out = P("gx", "gy", None, None, None, None)

    return jax.shard_map(
        per_device, mesh=mesh, in_specs=placed, out_specs=(out, out), check_vma=False
    )
```

```python
import jax
import jax.numpy as jnp
from jax import lax
from jax.experimental import pallas as pl
from jax.experimental.pallas import tpu as pltpu
from jax.sharding import PartitionSpec as P


PAIRS = 4
DEEP = 2 * PAIRS
EARLY = PAIRS // 2
SUB = 8
LANES = 128
VMEM_LIMIT = 16 * 2**20

HEAT_SCALE = 25000.0
HEAT_SHIFT = 32000.0
PORE_SCALE = 40000.0
PORE_SHIFT = 7000.0


def encode(values, scale, shift):
    return jnp.floor(values * scale + (0.5 - shift)).astype(jnp.int32).astype(jnp.int16)


def decode(codes, scale, shift):
    return (codes.astype(jnp.int32).astype(jnp.float32) + shift) * (1.0 / scale)


def flag_rows(active_ref, cols):
    lane = lax.broadcasted_iota(jnp.int32, (cols, LANES), 1)
    col = lax.broadcasted_iota(jnp.int32, (cols, LANES), 0)

    def flag(i):
        return jnp.where(col < cols // 2, active_ref[i, 0], active_ref[i, 1])

    return jnp.where(lane < LANES // 2, flag(0), flag(1)).astype(jnp.float32)


def mask_at(ranks):
    choose = lambda i, k, s: (i * ranks + k) * 4 + s
    taken = lambda i, r, s: 8 * ranks + (i * ranks + r) * 4 + s
    again = lambda k, r: 16 * ranks + k * ranks + r
    return choose, taken, again, 16 * ranks + ranks * ranks


def pack_x(
    active_ref, count_ref, slot_ref, heat_ref, pore_ref, out_ref, heat_out, pore_out, mask_ref
):
    rows, cols = heat_ref.shape[0], heat_ref.shape[1]
    ranks = slot_ref.shape[1]
    out_ref[0:rows] = heat_ref[...].astype(jnp.bfloat16)
    out_ref[rows : 2 * rows] = pore_ref[...].astype(jnp.bfloat16)
    out_ref[2 * rows] = flag_rows(active_ref, cols).astype(jnp.bfloat16)
    heat_out[...] = heat_ref[...]
    pore_out[...] = pore_ref[...]
    choose, taken, again, _ = mask_at(ranks)

    def put(row, holds):
        mask_ref[row] = jnp.full((SUB, LANES), jnp.where(holds, 1.0, 0.0), jnp.float32)

    for i in range(2):
        for k in range(ranks):
            for s in range(4):
                here = slot_ref[i, k] == s
                put(choose(i, k, s), here)
                put(taken(i, k, s), here & (k < count_ref[i]))
    for k in range(ranks):
        for r in range(ranks):
            put(again(k, r), (slot_ref[1, k] == slot_ref[0, r]) & (r < count_ref[0]))


def inside(axis, below):
    at = lax.axis_index(axis)
    has = at < lax.axis_size(axis) - 1 if below else at > 0
    return jnp.where(has, 1.0, 0.0).astype(jnp.float32)


def x_parts(own_ref, first_ref, second_ref):
    odd = lax.rem(lax.axis_index("gx") + lax.axis_index("gy"), 2)
    return ((2 - 2 * odd, first_ref), (1, own_ref), (2 * odd, second_ref))


def pack_y(own_ref, first_ref, second_ref, near_out, far_out):
    rows = (own_ref.shape[0] - 1) // 2
    cols = own_ref.shape[1]
    side = 2 * rows
    odd = lax.rem(lax.axis_index("gy"), 2)
    edge = cols - DEEP
    sub = lax.broadcasted_iota(jnp.int32, (DEEP, LANES), 0)
    sides = ((near_out, edge - edge * odd, odd == 0), (far_out, edge * odd, odd == 1))
    for out_ref, start, right in sides:
        at = pl.ds(pl.multiple_of(start, DEEP), DEEP)
        flags = jnp.zeros((DEEP, LANES), jnp.float32)
        for i, part in x_parts(own_ref, first_ref, second_ref):
            flags = jnp.where(sub == i, part[2 * rows, at, :].astype(jnp.float32), flags)
            for f in range(2):
                if part is own_ref:
                    out_ref[pl.ds(f * side, rows)] = part[pl.ds(f * rows, rows), at, :]
                    continue
                for d in range(1, rows // 2 + 1):
                    a, b = (
                        part[f * rows + jnp.where(i == 0, rows - e, e - 1), at, :].astype(jnp.float32)
                        for e in (d, rows - d)
                    )
                    if d < rows - d:
                        a = jnp.where(
                            right,
                            jnp.where(sub >= d, a, pltpu.roll(b, d, 0)),
                            jnp.where(sub < DEEP - d, a, pltpu.roll(b, DEEP - d, 0)),
                        )
                    out_ref[f * side + rows + (i // 2) * (rows // 2) + d - 1] = a.astype(jnp.bfloat16)
        out_ref[2 * side] = flags.astype(jnp.bfloat16)


def edge_row(part, field, x, rows, right):
    side = 2 * rows
    if rows <= x < 2 * rows:
        return part[field * side + x - rows].astype(jnp.float32)
    d = rows - x if x < rows else x - 2 * rows + 1
    at = field * side + rows + (0 if x < rows else rows // 2) - 1
    if d <= rows // 2:
        return part[at + d].astype(jnp.float32)
    if d == rows:
        return part[at + rows // 2].astype(jnp.float32)
    v = part[at + rows - d].astype(jnp.float32)
    return jnp.where(right, pltpu.roll(v, d, 0), pltpu.roll(v, DEEP - d, 0))


def flux_sums(parts, twice):
    lane = lax.broadcasted_iota(jnp.int32, (SUB, LANES), 1)
    depths = []
    for val, wgt, lo, hi in parts:
        depths.append(
            {
                (c, j): [
                    (pltpu.roll(v, by, 1), pltpu.roll(w, by, 1))
                    for by in ((LANES - 1,) if twice else (LANES - 1, 1))
                ]
                for c in range(lo, hi)
                for j, (v, w) in enumerate(zip(val[c], wgt[c]))
            }
        )
    for (val, wgt, _, _), depth in zip(parts, depths):
        for (c, j), shifted in depth.items():
            f = None
            for (v, w), ok in zip(shifted, (lane < LANES - 1, lane > 0)):
                g = jnp.where(ok, (wgt[c][j] + w) * (v - val[c][j]), 0.0)
                f = g if f is None else f + g
            depth[c, j] = f
    for depth in depths:
        for at, f in depth.items():
            depth[at] = f - pltpu.roll(f, 1, 1) if twice else f

    sums = []
    for (val, wgt, lo, hi), depth in zip(parts, depths):
        n = len(val[lo])
        span = range(n)

        def toward(c):
            return [(wgt[c][j] + wgt[c + 1][j]) * (val[c + 1][j] - val[c][j]) for j in span]

        out = {}
        last = toward(lo - 1)
        for c in range(lo, hi):
            v, w = val[c], wgt[c]
            ahead = toward(c)
            down = [(w[j] + w[j + 1]) * (v[j + 1] - v[j]) for j in range(n - 1)]
            down.append(
                (w[n - 1] + pltpu.roll(w[0], SUB - 1, 0))
                * (pltpu.roll(v[0], SUB - 1, 0) - v[n - 1])
            )
            up = [pltpu.roll(down[-1], 1, 0)] + down[:-1]
            out[c] = [(ahead[j] - last[j]) + (down[j] - up[j]) + depth[c, j] for j in span]
            last = ahead
        sums.append(out)
    return sums


def advance(*parts, twice=True):
    fluxes = []
    for pore, h, q, lo, hi, _ in parts:
        val, wgt = {}, {}
        for c in range(lo - 1, hi + 1):
            t = [jnp.tanh(v) for v in h[c]]
            temp = [2.5 * v - u for v, u in zip(h[c], t)]
            if pore:
                val[c] = q[c]
                wgt[c] = [1.0 + jnp.tanh(v) for v in temp]
            else:
                val[c] = temp
                wgt[c] = [(1.0 - v) * (1.0 - v) * (u + 7.0 / 3.0) for v, u in zip(q[c], t)]
        fluxes.append((val, wgt, lo, hi))
    results = []
    for (pore, h, q, lo, hi, mask), (val, wgt, _, _), acc in zip(parts, fluxes, flux_sums(fluxes, twice)):
        new = {}
        for c in range(lo, hi):
            if pore:
                new[c] = [
                    v + m * (a - 4.0 * r * v)
                    for v, m, a, r in zip(q[c], mask(c, 1), acc[c], wgt[c])
                ]
            else:
                new[c] = [v + m * a for v, m, a in zip(h[c], mask(c, 0), acc[c])]
        results.append(new)
    return results


def tile_rows(marks, i, tx, n, out):
    low = lax.broadcasted_iota(jnp.int32, (SUB, LANES), 1) < LANES // 2
    sub = lax.broadcasted_iota(jnp.int32, (SUB, LANES), 0)
    other = pltpu.roll(marks, LANES // 2, 1)
    for h, flag in ((0, jnp.where(low, marks, other)), (1, jnp.where(low, other, marks))):
        first = (2 * i + h) * tx
        for j in range(n):
            x = sub * n + j
            out[j] = jnp.where((x >= first) & (x < first + tx), flag, out[j])
    return out


def scalings(flags):
    return ([0.009 * f for f in flags], [0.0375 * f for f in flags])


def back(columns, wide, turn, rows, total, heat):
    for c, column in enumerate(columns):
        n = len(column)
        for j, v in enumerate(column):
            wide[pl.ds(c * total + j, SUB, stride=n), :] = 0.5 * v + 1.0 if heat else v
    for c in range(len(columns)):
        turn[pl.ds(c * rows, rows), :] = wide[pl.ds(c * total + DEEP, rows), :]


def inner(
    own_ref, heat_ref, pore_ref, xa_ref, xb_ref,
    heat_out, pore_out, heat_save, pore_save, flag_out, wide,
):
    rows, cols = heat_ref.shape[0], heat_ref.shape[1]
    total = rows + 2 * DEEP
    width = cols + 2 * DEEP
    n = total // SUB
    tx, ty = rows // 2, cols // 2
    f32 = jnp.float32
    opens = []
    parts = x_parts(own_ref, xa_ref, xb_ref)
    for i, part in parts:
        opens.append(jnp.where(i == 0, inside("gx", False), inside("gx", True)))

    flags = []
    for k in range(2):
        f = [jnp.zeros((SUB, LANES), f32) for _ in range(n)]
        for (i, part), has in zip(parts, opens):
            marks = part[2 * rows, pl.ds(k * ty, SUB), :].astype(f32)
            f = tile_rows(marks if part is own_ref else marks * has, i, tx, n, f)
        for j in range(n):
            flag_out[k, j] = f[j]
        flags.append(scalings(f))

    def mask(c, kind):
        return flags[0 if c < DEEP + ty else 1][kind]

    h, q = {}, {}
    for field, home, state in ((0, heat_ref, h), (1, pore_ref, q)):
        for (i, part), has in zip(parts, opens):
            for r in range(rows):
                if part is own_ref:
                    v = home[r]
                else:
                    v = part[field * rows + r].astype(f32) * has
                v = 2.0 * v - 2.0 if field == 0 else v
                for g in range(0, cols, SUB):
                    at = pl.multiple_of(g * total + (i * rows + r) * SUB, SUB)
                    wide[field, pl.ds(at, SUB), :] = v[g : g + SUB]
        for c in range(cols):
            at = c // SUB * SUB * total + c % SUB
            state[DEEP + c] = [
                wide[field, pl.ds(at + j * SUB, SUB, stride=n * SUB), :] for j in range(n)
            ]

    for p in range(EARLY):
        lo, hi = DEEP + 2 * p + 1, width - DEEP - 2 * p - 1
        for side, c in ((0, lo), (1, hi - 1)):
            for j in range(n):
                heat_save[p, side, j] = h[c][j]
        h.update(*advance((False, h, q, lo, hi, mask)))
        lo, hi = lo + 1, hi - 1
        for side, c in ((0, lo), (1, hi - 1)):
            for j in range(n):
                pore_save[p, side, j] = q[c][j]
        q.update(*advance((True, h, q, lo, hi, mask)))
    for state, out in ((h, heat_out), (q, pore_out)):
        for c in range(cols):
            for j in range(n):
                out[c, j] = state[DEEP + c][j]


def halo(near, flag_ref, got_ref, wide, rows, n):
    total = n * SUB
    tx = rows // 2
    f32 = jnp.float32
    odd = lax.rem(lax.axis_index("gy"), 2)
    side = 1 - odd if near else odd
    left = side == 0
    has = None if near else jnp.where(left, inside("gy", False), inside("gy", True))
    row_open = (inside("gx", False), None, inside("gx", True))

    def scaled(v, *by):
        for s in by:
            v = v if s is None else v * s
        return v

    marks = scaled(got_ref[4 * rows].astype(f32), has)
    beyond = [jnp.zeros((SUB, LANES), f32) for _ in range(n)]
    for i in range(3):
        row = jnp.broadcast_to(scaled(marks[i : i + 1], row_open[i]), (SUB, LANES))
        beyond = tile_rows(row, i, tx, n, beyond)
    flags = [scalings(beyond), scalings([flag_ref[side, j] for j in range(n)])]

    def mask(c, kind):
        return flags[0 if c < DEEP else 1][kind]

    states = ({}, {})
    for field, state in enumerate(states):
        for x in range(total):
            v = scaled(edge_row(got_ref, field, x, rows, left), has, row_open[x // rows])
            wide[field, x * DEEP : (x + 1) * DEEP, :] = 2.0 * v - 2.0 if field == 0 else v
        for c in range(DEEP):
            state[c] = [
                jnp.where(
                    left,
                    wide[field, pl.ds(j * DEEP + c, SUB, stride=n * DEEP), :],
                    wide[field, pl.ds(j * DEEP + DEEP - 1 - c, SUB, stride=n * DEEP), :],
                )
                for j in range(n)
            ]
    return side, left, states, mask


def strips(h, q, left, wide, turn, rows, n):
    total = n * SUB
    for field, state in ((0, h), (1, q)):
        for c in range(DEEP):
            for j, v in enumerate(state[DEEP + c]):
                wide[field, pl.ds(c * total + j, SUB, stride=n), :] = (
                    0.5 * v + 1.0 if field == 0 else v
                )
        for c in range(DEEP):
            at = pl.multiple_of(jnp.where(left, c, DEEP - 1 - c) * rows, SUB)
            turn[field, pl.ds(at, rows), :] = wide[field, pl.ds(c * total + DEEP, rows), :]


def middle(
    heat_in, pore_in, heat_save, pore_save, flag_ref, got_ref,
    heat_strip, pore_strip, heat_mid, pore_mid, heat_edge, pore_edge, heat_kept, pore_kept,
    wide, turn, wide_mid, turn_mid,
):
    rows, cols = heat_mid.shape[0], heat_in.shape[0]
    n = heat_in.shape[1]
    width = cols + 2 * DEEP
    total = n * SUB
    ty = cols // 2
    span = range(n)
    side, left, (hw, qw), mask_w = halo(True, flag_ref, got_ref, wide, rows, n)
    flags = [scalings([flag_ref[k, j] for j in span]) for k in range(2)]

    def mask(c, kind):
        return flags[0 if c < DEEP + ty else 1][kind]

    h = {DEEP + c: [heat_in[c, j] for j in span] for c in range(cols)}
    q = {DEEP + c: [pore_in[c, j] for j in span] for c in range(cols)}

    def pick(low, high):
        return [jnp.where(left, a, b) for a, b in zip(low, high)]

    def at(state, c):
        return pick(state[c], state[width - 1 - c])

    kept = ({}, {})
    for p in range(EARLY):
        for keep, save, out in zip(kept, (heat_save, pore_save), (heat_kept, pore_kept)):
            keep[p] = [save[p, side, j] for j in span]
            for j in span:
                out[p, j] = save[p, 1 - side, j]

    def keep_now(field, state, p, c):
        low, high = state[c], state[width - 1 - c]
        kept[field][p] = pick(low, high)
        for j, v in enumerate(pick(high, low)):
            (heat_kept, pore_kept)[field][p, j] = v

    waiting = []

    def block_half(step):
        p, k = EARLY + step // 4, step % 4
        pore = k >= 2
        lo = DEEP + 2 * p + (2 if pore else 1)
        if k % 2 == 0:
            keep_now(int(pore), q if pore else h, p, lo)
        half = (lo, width // 2) if k % 2 == 0 else (width // 2, width - lo)
        return (pore, h, q, *half, mask)

    for p in range(PAIRS):
        for pore in (False, True):
            step = 2 * p + pore
            lo = 2 * p + 1 + pore
            end = block_half(step)
            if pore:
                hw[lo + DEEP - 1], hw[lo + DEEP] = at(h, lo + DEEP - 1), at(h, lo + DEEP)
                then = dict(qw)
                then[lo + DEEP] = kept[1][p]
                part = (True, hw, then, lo, lo + DEEP, mask_w)
            else:
                c = lo + DEEP - 1
                hw[c] = at(h, c)
                qw[c], qw[c + 1] = at(q, c), at(q, c + 1)
                then = dict(hw)
                then[c + 1] = kept[0][p]
                part = (False, then, qw, lo, lo + DEEP, mask_w)
            new, ours = advance(part, end)
            (qw if pore else hw).update(new)
            waiting.append(ours)
            if step % 2 == 1:
                for result in waiting:
                    (q if end[0] else h).update(result)
                waiting = []

    strips(hw, qw, left, wide, turn, rows, n)
    for field, out in ((0, heat_strip), (1, pore_strip)):
        for r in range(rows):
            out[r] = turn[field, pl.ds(r, DEEP, stride=rows), :]
    for field, state, edge, mid in ((0, h, heat_edge, heat_mid), (1, q, pore_edge, pore_mid)):
        for c in range(DEEP + 1):
            for j, v in enumerate(pick(state[width - 1 - DEEP - c], state[DEEP + c])):
                edge[c, j] = v
        back(
            [state[c] for c in range(2 * DEEP, width - 2 * DEEP)], wide_mid.at[field],
            turn_mid.at[field], rows, total, field == 0,
        )
        for r in range(rows):
            for g in range(0, cols - 2 * DEEP, SUB):
                mid[r, g : g + SUB] = turn_mid[field, pl.ds(g * rows + r, SUB, stride=rows), :]


def far_edge(
    mask_ref, heat_edge, pore_edge, heat_kept, pore_kept, heat_mid, pore_mid, flag_ref, got_ref,
    heat_near, pore_near, heat_out, pore_out, send_ref, later_ref, wide, turn, block,
):
    rows, cols = heat_mid.shape[0], heat_mid.shape[1] + 2 * DEEP
    n = heat_edge.shape[1]
    tx, ty = rows // 2, cols // 2
    span = range(n)
    side, left, (h, q), mask = halo(False, flag_ref, got_ref, wide, rows, n)
    for state, edge in ((h, heat_edge), (q, pore_edge)):
        for c in range(DEEP + 1):
            state[DEEP + c] = [edge[c, j] for j in span]
    for p in range(PAIRS):
        lo = 2 * p + 1
        then = dict(h)
        then[lo + DEEP] = [heat_kept[p, j] for j in span]
        h.update(*advance((False, then, q, lo, lo + DEEP, mask), twice=False))
        lo = lo + 1
        then = dict(q)
        then[lo + DEEP] = [pore_kept[p, j] for j in span]
        q.update(*advance((True, h, then, lo, lo + DEEP, mask), twice=False))
    strips(h, q, left, wide, turn, rows, n)
    end = cols - DEEP
    far_at = pl.ds(pl.multiple_of(end * side, SUB), DEEP)
    near_at = pl.ds(pl.multiple_of(end - end * side, SUB), DEEP)
    for field, mid, near, out in (
        (0, heat_mid, heat_near, heat_out),
        (1, pore_mid, pore_near, pore_out),
    ):
        for r in range(rows):
            block[field, r, DEEP:end] = mid[r]
            block[field, r, near_at] = near[r]
            block[field, r, far_at] = turn[field, pl.ds(r, DEEP, stride=rows), :]
        for i in range(2):
            for k in range(2):
                out[2 * i + k] = block[field, i * tx : (i + 1) * tx, k * ty : (k + 1) * ty, :]
    ranks = send_ref.shape[0]
    choose = mask_at(ranks)[0]
    shape = (tx, ty, LANES)
    for field, src, scale, shift in (
        (0, heat_out, HEAT_SCALE, HEAT_SHIFT),
        (1, pore_out, PORE_SCALE, PORE_SHIFT),
    ):
        for i, out in ((0, send_ref), (1, later_ref)):
            for k in range(ranks):
                v = src[0]
                for s in range(1, 4):
                    v = jnp.where(held(mask_ref, choose(i, k, s), shape), src[s], v)
                out[k, field] = encode(v, scale, shift)


def held(mask_ref, row, shape):
    m = mask_ref[row]
    m = jnp.concatenate([m] * (shape[1] // SUB), axis=0)
    return jnp.broadcast_to(m[None], shape) > 0.5


def resend(mask_ref, got_ref, local_ref, send_ref):
    ranks = got_ref.shape[0]
    shape = got_ref.shape[2:]
    again = mask_at(ranks)[2]
    for k in range(ranks):
        for f in range(2):
            v = local_ref[k, f].astype(jnp.int32)
            for r in range(ranks):
                v = jnp.where(
                    held(mask_ref, again(k, r), shape), got_ref[r, f].astype(jnp.int32), v
                )
            send_ref[k, f] = v.astype(jnp.int16)


def place(mask_ref, heat_ref, pore_ref, first_ref, second_ref, heat_out, pore_out):
    ranks = first_ref.shape[0]
    shape = first_ref.shape[2:]
    taken = mask_at(ranks)[1]
    for field, src, out, scale, shift in (
        (0, heat_ref, heat_out, HEAT_SCALE, HEAT_SHIFT),
        (1, pore_ref, pore_out, PORE_SCALE, PORE_SHIFT),
    ):
        came = [
            (i, r, decode(got[r, field], scale, shift))
            for i, got in ((0, first_ref), (1, second_ref))
            for r in range(ranks)
        ]
        for s in range(4):
            v = src[s]
            for i, r, tile in came:
                v = jnp.where(held(mask_ref, taken(i, r, s), shape), tile, v)
            out[s] = v


def call(body, spec, outs, scratch=(), out_space=pltpu.VMEM):
    def run(*args):
        space = {"s": pltpu.SMEM, "v": pltpu.VMEM, "V": pltpu.VMEM}
        args = [
            pltpu.with_memory_space_constraint(a, pltpu.VMEM if c == "V" else pltpu.HBM)
            for c, a in zip(spec, args)
        ]
        shapes = [
            pltpu.VMEM(s, d) if out_space is not None else jax.ShapeDtypeStruct(s, d)
            for s, d in outs
        ]
        return pl.pallas_call(
            body,
            in_specs=[pl.BlockSpec(memory_space=space[c]) for c in spec],
            out_specs=[pl.BlockSpec(memory_space=pltpu.VMEM) for _ in outs],
            out_shape=shapes,
            scratch_shapes=list(scratch),
            compiler_params=pltpu.CompilerParams(vmem_limit_bytes=VMEM_LIMIT),
        )(*args)

    return run


def permute(value, partner):
    nx, ny = lax.axis_size("gx"), lax.axis_size("gy")
    pairs = []
    for x in range(nx):
        for y in range(ny):
            u, v = partner(x, y)
            pairs.append((x * ny + y, u * ny + v))
    return lax.ppermute(value, ("gx", "gy"), pairs)


def exchange_x(value):
    nx, ny = lax.axis_size("gx"), lax.axis_size("gy")

    def partner(x, y, near):
        if near:
            return x ^ 1, y
        if 0 < x < nx - 1:
            return ((x + 1) ^ 1) - 1, y
        return (x, y ^ 2) if ny % 4 == 0 else (x, y)

    first = permute(value, lambda x, y: partner(x, y, y % 2 == 0))
    second = permute(value, lambda x, y: partner(x, y, y % 2 == 1))
    return first, second


def exchange_y(near, far):
    ny = lax.axis_size("gy")

    def partner(x, y):
        if 0 < y < ny - 1:
            return x, ((y + 1) ^ 1) - 1
        return x ^ 1, y

    far = permute(far, partner)
    near = permute(near, lambda x, y: (x, y ^ 1))
    return near, far


def swap(value, axis):
    n = lax.axis_size(axis)
    return lax.ppermute(value, axis, [(i, (i + n // 2) % n) for i in range(n)])


def per_device(enthalpy, porosity, active, move_count, move_slot):
    rows, cols, depth = enthalpy.shape
    tx, ty = rows // 2, cols // 2
    count = move_count.reshape(2)
    slots = move_slot.reshape(2, move_slot.shape[-1])
    ranks = slots.shape[1]
    f32, bf16, i16 = jnp.float32, jnp.bfloat16, jnp.int16

    block = ((rows, cols, depth), f32)
    masks = ((mask_at(ranks)[3], SUB, LANES), f32)
    own, enthalpy, porosity, masks = call(
        pack_x, "sssvv", [((2 * rows + 1, cols, depth), bf16), block, block, masks]
    )(active, count, slots, enthalpy, porosity)
    x_near, x_far = exchange_x(own)
    side = ((4 * rows + 1, DEEP, depth), bf16)
    near, far = call(pack_y, "VVV", [side, side])(own, x_near, x_far)
    y_near, y_far = exchange_y(near, far)
    total = rows + 2 * DEEP
    n = total // SUB
    tiles = ((4, tx, ty, depth), f32)
    parcel = ((ranks, 2, tx, ty, depth), i16)
    column = (n, SUB, depth)
    whole = ((cols, *column), f32)
    save = ((EARLY, 2, *column), f32)
    edge = ((DEEP + 1, *column), f32)
    kept = ((PAIRS, *column), f32)
    mid = ((rows, cols - 2 * DEEP, depth), f32)
    strip = ((rows, DEEP, depth), f32)
    state = call(
        inner, "VVVVV", [whole, whole, save, save, ((2, *column), f32)],
        [pltpu.VMEM((2, total * cols, depth), f32)],
    )(own, enthalpy, porosity, x_near, x_far)
    scratch = [
        pltpu.VMEM((2, total * DEEP, depth), f32),
        pltpu.VMEM((2, rows * DEEP, depth), f32),
    ]
    heat_near, pore_near, heat_mid, pore_mid, *ends = call(
        middle, "V" * 6, [strip, strip, mid, mid, edge, edge, kept, kept],
        scratch
        + [
            pltpu.VMEM((2, total * (cols - 2 * DEEP), depth), f32),
            pltpu.VMEM((2, rows * (cols - 2 * DEEP), depth), f32),
        ],
    )(*state, y_near)
    heat, pore, first, later = call(
        far_edge, "V" * 11, [tiles, tiles, parcel, parcel],
        scratch + [pltpu.VMEM((2, rows, cols, depth), f32)],
    )(masks, *ends, heat_mid, pore_mid, state[4], y_far, heat_near, pore_near)
    first = swap(first, "gx")
    (second,) = call(resend, "VVV", [parcel])(masks, first, later)
    second = swap(second, "gy")
    heat, pore = call(place, "VVVVV", [tiles, tiles], out_space=None)(
        masks, heat, pore, first, second
    )
    return heat[None, None], pore[None, None]


def solution(mesh):
    placed = (
        P("gx", "gy", None),
        P("gx", "gy", None),
        P("gx", "gy"),
        P("gx", "gy", None),
        P("gx", "gy", None, None),
    )
    out = P("gx", "gy", None, None, None, None)

    return jax.shard_map(
        per_device, mesh=mesh, in_specs=placed, out_specs=(out, out), check_vma=False
    )
```

```python
import jax
import jax.numpy as jnp
from jax import lax
from jax.experimental import pallas as pl
from jax.experimental.pallas import tpu as pltpu
from jax.sharding import PartitionSpec as P


PAIRS = 4
DEEP = 2 * PAIRS
EARLY = PAIRS // 2
SUB = 8
LANES = 128
VMEM_LIMIT = 16 * 2**20

HEAT_SCALE = 16000.0
HEAT_SHIFT = 20000.0
PORE_SCALE = 25000.0
PORE_SHIFT = 7750.0


def encode(values, scale, shift):
    codes = jnp.floor(values * scale + (0.5 - shift))
    return jnp.clip(codes, -32768.0, 32767.0).astype(jnp.int32).astype(jnp.int16)


def decode(codes, scale, shift):
    return (codes.astype(jnp.int32).astype(jnp.float32) + shift) * (1.0 / scale)


def flag_tile(active_ref):
    lane = lax.broadcasted_iota(jnp.int32, (SUB, LANES), 1)
    sub = lax.broadcasted_iota(jnp.int32, (SUB, LANES), 0)

    def flag(i):
        return jnp.where(sub < SUB // 2, active_ref[i, 0], active_ref[i, 1])

    return jnp.where(lane < LANES // 2, flag(0), flag(1)).astype(jnp.float32)


def flags_at(tile, k):
    at = k * SUB // 2
    return jnp.broadcast_to(tile[at : at + 1], tile.shape)


def mask_at(ranks):
    choose = lambda i, k, s: (i * ranks + k) * 4 + s
    taken = lambda i, r, s: 8 * ranks + (i * ranks + r) * 4 + s
    again = lambda k, r: 16 * ranks + k * ranks + r
    return choose, taken, again, 16 * ranks + ranks * ranks


def pack_x(
    active_ref, count_ref, slot_ref, heat_ref, pore_ref, out_ref, heat_out, pore_out, mask_ref
):
    rows, cols = heat_ref.shape[0], heat_ref.shape[1]
    ranks = slot_ref.shape[1]
    groups = rows * cols // SUB
    out_ref[0:groups] = heat_ref[...].reshape(groups, SUB, LANES).astype(jnp.bfloat16)
    out_ref[groups : 2 * groups] = pore_ref[...].reshape(groups, SUB, LANES).astype(jnp.bfloat16)
    out_ref[2 * groups] = flag_tile(active_ref).astype(jnp.bfloat16)
    heat_out[...] = heat_ref[...]
    pore_out[...] = pore_ref[...]
    choose, taken, again, _ = mask_at(ranks)

    def put(row, holds):
        mask_ref[row] = jnp.full((SUB, LANES), jnp.where(holds, 1.0, 0.0), jnp.float32)

    for i in range(2):
        for k in range(ranks):
            for s in range(4):
                here = slot_ref[i, k] == s
                put(choose(i, k, s), here)
                put(taken(i, k, s), here & (k < count_ref[i]))
    for k in range(ranks):
        for r in range(ranks):
            put(again(k, r), (slot_ref[1, k] == slot_ref[0, r]) & (r < count_ref[0]))


def inside(axis, below):
    at = lax.axis_index(axis)
    has = at < lax.axis_size(axis) - 1 if below else at > 0
    return jnp.where(has, 1.0, 0.0).astype(jnp.float32)


def x_parts(own_ref, first_ref, second_ref):
    odd = lax.rem(lax.axis_index("gx") + lax.axis_index("gy"), 2)
    return ((2 - 2 * odd, first_ref), (1, own_ref), (2 * odd, second_ref))


def pack_y(own_ref, first_ref, second_ref, near_out, far_out):
    rows = near_out.shape[0] // 4
    per = (own_ref.shape[0] - 1) // (2 * rows)
    side = 2 * rows
    odd = lax.rem(lax.axis_index("gy"), 2)
    edge = per - 1
    sub = lax.broadcasted_iota(jnp.int32, (DEEP, LANES), 0)
    sides = ((near_out, edge - edge * odd, odd == 0), (far_out, edge * odd, odd == 1))
    for out_ref, at, right in sides:
        flags = jnp.zeros((DEEP, LANES), jnp.float32)
        for i, part in x_parts(own_ref, first_ref, second_ref):
            tile = part[2 * rows * per].astype(jnp.float32)
            flags = jnp.where(
                sub == i, jnp.where(right, flags_at(tile, 1), flags_at(tile, 0)), flags
            )
            for f in range(2):
                if part is own_ref:
                    for r in range(rows):
                        out_ref[f * side + r] = part[(f * rows + r) * per + at]
                    continue
                for d in range(1, rows // 2 + 1):
                    a, b = (
                        part[(f * rows + jnp.where(i == 0, rows - e, e - 1)) * per + at].astype(
                            jnp.float32
                        )
                        for e in (d, rows - d)
                    )
                    if d < rows - d:
                        a = jnp.where(
                            right,
                            jnp.where(sub >= d, a, pltpu.roll(b, d, 0)),
                            jnp.where(sub < DEEP - d, a, pltpu.roll(b, DEEP - d, 0)),
                        )
                    out_ref[f * side + rows + (i // 2) * (rows // 2) + d - 1] = a.astype(jnp.bfloat16)
        out_ref[2 * side] = flags.astype(jnp.bfloat16)


def edge_row(part, field, x, rows, right):
    side = 2 * rows
    if rows <= x < 2 * rows:
        return part[field * side + x - rows].astype(jnp.float32)
    d = rows - x if x < rows else x - 2 * rows + 1
    at = field * side + rows + (0 if x < rows else rows // 2) - 1
    if d <= rows // 2:
        return part[at + d].astype(jnp.float32)
    if d == rows:
        return part[at + rows // 2].astype(jnp.float32)
    v = part[at + rows - d].astype(jnp.float32)
    return jnp.where(right, pltpu.roll(v, d, 0), pltpu.roll(v, DEEP - d, 0))


def flux_sums(parts, twice):
    lane = lax.broadcasted_iota(jnp.int32, (SUB, LANES), 1)
    depths = []
    for val, wgt, lo, hi in parts:
        depths.append(
            {
                (c, j): [
                    (pltpu.roll(v, by, 1), pltpu.roll(w, by, 1))
                    for by in ((LANES - 1,) if twice else (LANES - 1, 1))
                ]
                for c in range(lo, hi)
                for j, (v, w) in enumerate(zip(val[c], wgt[c]))
            }
        )
    for (val, wgt, _, _), depth in zip(parts, depths):
        for (c, j), shifted in depth.items():
            f = None
            for (v, w), ok in zip(shifted, (lane < LANES - 1, lane > 0)):
                g = jnp.where(ok, (wgt[c][j] + w) * (v - val[c][j]), 0.0)
                f = g if f is None else f + g
            depth[c, j] = f
    for depth in depths:
        for at, f in depth.items():
            depth[at] = f - pltpu.roll(f, 1, 1) if twice else f

    sums = []
    for (val, wgt, lo, hi), depth in zip(parts, depths):
        n = len(val[lo])
        span = range(n)

        def toward(c):
            return [(wgt[c][j] + wgt[c + 1][j]) * (val[c + 1][j] - val[c][j]) for j in span]

        out = {}
        last = toward(lo - 1)
        for c in range(lo, hi):
            v, w = val[c], wgt[c]
            ahead = toward(c)
            down = [(w[j] + w[j + 1]) * (v[j + 1] - v[j]) for j in range(n - 1)]
            down.append(
                (w[n - 1] + pltpu.roll(w[0], SUB - 1, 0))
                * (pltpu.roll(v[0], SUB - 1, 0) - v[n - 1])
            )
            up = [pltpu.roll(down[-1], 1, 0)] + down[:-1]
            out[c] = [(ahead[j] - last[j]) + (down[j] - up[j]) + depth[c, j] for j in span]
            last = ahead
        sums.append(out)
    return sums


def advance(*parts, twice=True):
    fluxes = []
    for pore, h, q, lo, hi, _ in parts:
        val, wgt = {}, {}
        for c in range(lo - 1, hi + 1):
            t = [jnp.tanh(v) for v in h[c]]
            temp = [2.5 * v - u for v, u in zip(h[c], t)]
            if pore:
                val[c] = q[c]
                wgt[c] = [1.0 + jnp.tanh(v) for v in temp]
            else:
                val[c] = temp
                wgt[c] = [(1.0 - v) * (1.0 - v) * (u + 7.0 / 3.0) for v, u in zip(q[c], t)]
        fluxes.append((val, wgt, lo, hi))
    results = []
    for (pore, h, q, lo, hi, mask), (val, wgt, _, _), acc in zip(parts, fluxes, flux_sums(fluxes, twice)):
        new = {}
        for c in range(lo, hi):
            if pore:
                new[c] = [
                    v + m * (a - 4.0 * r * v)
                    for v, m, a, r in zip(q[c], mask(c, 1), acc[c], wgt[c])
                ]
            else:
                new[c] = [v + m * a for v, m, a in zip(h[c], mask(c, 0), acc[c])]
        results.append(new)
    return results


def tile_rows(marks, i, tx, n, out):
    low = lax.broadcasted_iota(jnp.int32, (SUB, LANES), 1) < LANES // 2
    sub = lax.broadcasted_iota(jnp.int32, (SUB, LANES), 0)
    other = pltpu.roll(marks, LANES // 2, 1)
    for h, flag in ((0, jnp.where(low, marks, other)), (1, jnp.where(low, other, marks))):
        first = (2 * i + h) * tx
        for j in range(n):
            x = sub * n + j
            out[j] = jnp.where((x >= first) & (x < first + tx), flag, out[j])
    return out


def scalings(flags):
    return ([0.009 * f for f in flags], [0.0375 * f for f in flags])


def back(columns, wide, turn, rows, total, heat):
    for c, column in enumerate(columns):
        n = len(column)
        for j, v in enumerate(column):
            wide[pl.ds(c * total + j, SUB, stride=n), :] = 0.5 * v + 1.0 if heat else v
    for c in range(len(columns)):
        turn[pl.ds(c * rows, rows), :] = wide[pl.ds(c * total + DEEP, rows), :]


def inner(
    own_ref, heat_ref, pore_ref, xa_ref, xb_ref,
    heat_out, pore_out, heat_save, pore_save, flag_out, wide,
):
    rows, cols = heat_ref.shape[0], heat_ref.shape[1]
    total = rows + 2 * DEEP
    width = cols + 2 * DEEP
    n = total // SUB
    tx, ty = rows // 2, cols // 2
    f32 = jnp.float32
    odd = lax.rem(lax.axis_index("gx") + lax.axis_index("gy"), 2)

    per = cols // SUB

    def take(i, at, count):
        at = pl.ds(at, count)
        if i == 1:
            return own_ref[at].astype(f32)
        pair = (xa_ref[at], xb_ref[at]) if i == 0 else (xb_ref[at], xa_ref[at])
        v = jnp.where(odd == 1, *pair).astype(f32)
        return v * inside("gx", i == 2)

    flags = []
    marks = [take(i, 2 * rows * per, 1)[0] for i in range(3)]
    for k in range(2):
        f = [jnp.zeros((SUB, LANES), f32) for _ in range(n)]
        for i in range(3):
            f = tile_rows(flags_at(marks[i], k), i, tx, n, f)
        for j in range(n):
            flag_out[k, j] = f[j]
        flags.append(scalings(f))

    def mask(c, kind):
        return flags[0 if c < DEEP + ty else 1][kind]

    h, q = {}, {}
    for field, home, state in ((0, heat_ref, h), (1, pore_ref, q)):
        for i in range(3):
            for r in range(rows):
                v = home[r] if i == 1 else take(i, (field * rows + r) * per, per)
                v = v.reshape(cols, LANES)
                v = 2.0 * v - 2.0 if field == 0 else v
                for g in range(0, cols, SUB):
                    at = g * total + (i * rows + r) * SUB
                    wide[field, at : at + SUB, :] = v[g : g + SUB]
        for c in range(cols):
            at = c // SUB * SUB * total + c % SUB
            state[DEEP + c] = [
                wide[field, pl.ds(at + j * SUB, SUB, stride=n * SUB), :] for j in range(n)
            ]

    for p in range(EARLY):
        lo, hi = DEEP + 2 * p + 1, width - DEEP - 2 * p - 1
        for side, c in ((0, lo), (1, hi - 1)):
            for j in range(n):
                heat_save[p, side, j] = h[c][j]
        h.update(*advance((False, h, q, lo, hi, mask)))
        lo, hi = lo + 1, hi - 1
        for side, c in ((0, lo), (1, hi - 1)):
            for j in range(n):
                pore_save[p, side, j] = q[c][j]
        q.update(*advance((True, h, q, lo, hi, mask)))
    for state, out in ((h, heat_out), (q, pore_out)):
        for c in range(cols):
            for j in range(n):
                out[c, j] = state[DEEP + c][j]


def halo(near, flag_ref, got_ref, wide, rows, n):
    total = n * SUB
    tx = rows // 2
    f32 = jnp.float32
    odd = lax.rem(lax.axis_index("gy"), 2)
    side = 1 - odd if near else odd
    left = side == 0
    has = None if near else jnp.where(left, inside("gy", False), inside("gy", True))
    row_open = (inside("gx", False), None, inside("gx", True))

    def scaled(v, *by):
        for s in by:
            v = v if s is None else v * s
        return v

    marks = scaled(got_ref[4 * rows].astype(f32), has)
    beyond = [jnp.zeros((SUB, LANES), f32) for _ in range(n)]
    for i in range(3):
        row = jnp.broadcast_to(scaled(marks[i : i + 1], row_open[i]), (SUB, LANES))
        beyond = tile_rows(row, i, tx, n, beyond)
    flags = [scalings(beyond), scalings([flag_ref[side, j] for j in range(n)])]

    def mask(c, kind):
        return flags[0 if c < DEEP else 1][kind]

    states = ({}, {})
    for field, state in enumerate(states):
        for x in range(total):
            v = scaled(edge_row(got_ref, field, x, rows, left), has, row_open[x // rows])
            wide[field, x * DEEP : (x + 1) * DEEP, :] = 2.0 * v - 2.0 if field == 0 else v
        for c in range(DEEP):
            state[c] = [
                jnp.where(
                    left,
                    wide[field, pl.ds(j * DEEP + c, SUB, stride=n * DEEP), :],
                    wide[field, pl.ds(j * DEEP + DEEP - 1 - c, SUB, stride=n * DEEP), :],
                )
                for j in range(n)
            ]
    return side, left, states, mask


def strips(h, q, left, wide, turn, rows, n):
    total = n * SUB
    for field, state in ((0, h), (1, q)):
        for c in range(DEEP):
            for j, v in enumerate(state[DEEP + c]):
                wide[field, pl.ds(c * total + j, SUB, stride=n), :] = (
                    0.5 * v + 1.0 if field == 0 else v
                )
        for c in range(DEEP):
            at = pl.multiple_of(jnp.where(left, c, DEEP - 1 - c) * rows, SUB)
            turn[field, pl.ds(at, rows), :] = wide[field, pl.ds(c * total + DEEP, rows), :]


def middle(
    heat_in, pore_in, heat_save, pore_save, flag_ref, got_ref,
    heat_strip, pore_strip, heat_mid, pore_mid, heat_edge, pore_edge, heat_kept, pore_kept,
    wide, turn, wide_mid, turn_mid,
):
    rows, cols = heat_mid.shape[0], heat_in.shape[0]
    n = heat_in.shape[1]
    width = cols + 2 * DEEP
    total = n * SUB
    ty = cols // 2
    span = range(n)
    side, left, (hw, qw), mask_w = halo(True, flag_ref, got_ref, wide, rows, n)
    flags = [scalings([flag_ref[k, j] for j in span]) for k in range(2)]

    def mask(c, kind):
        return flags[0 if c < DEEP + ty else 1][kind]

    h = {DEEP + c: [heat_in[c, j] for j in span] for c in range(cols)}
    q = {DEEP + c: [pore_in[c, j] for j in span] for c in range(cols)}

    def pick(low, high):
        return [jnp.where(left, a, b) for a, b in zip(low, high)]

    def at(state, c):
        return pick(state[c], state[width - 1 - c])

    kept = ({}, {})
    for p in range(EARLY):
        for keep, save, out in zip(kept, (heat_save, pore_save), (heat_kept, pore_kept)):
            keep[p] = [save[p, side, j] for j in span]
            for j in span:
                out[p, j] = save[p, 1 - side, j]

    def keep_now(field, state, p, c):
        low, high = state[c], state[width - 1 - c]
        kept[field][p] = pick(low, high)
        for j, v in enumerate(pick(high, low)):
            (heat_kept, pore_kept)[field][p, j] = v

    waiting = []

    def block_half(step):
        p, k = EARLY + step // 4, step % 4
        pore = k >= 2
        lo = DEEP + 2 * p + (2 if pore else 1)
        if k % 2 == 0:
            keep_now(int(pore), q if pore else h, p, lo)
        half = (lo, width // 2) if k % 2 == 0 else (width // 2, width - lo)
        return (pore, h, q, *half, mask)

    for p in range(PAIRS):
        for pore in (False, True):
            step = 2 * p + pore
            lo = 2 * p + 1 + pore
            end = block_half(step)
            if pore:
                hw[lo + DEEP - 1], hw[lo + DEEP] = at(h, lo + DEEP - 1), at(h, lo + DEEP)
                then = dict(qw)
                then[lo + DEEP] = kept[1][p]
                part = (True, hw, then, lo, lo + DEEP, mask_w)
            else:
                c = lo + DEEP - 1
                hw[c] = at(h, c)
                qw[c], qw[c + 1] = at(q, c), at(q, c + 1)
                then = dict(hw)
                then[c + 1] = kept[0][p]
                part = (False, then, qw, lo, lo + DEEP, mask_w)
            new, ours = advance(part, end)
            (qw if pore else hw).update(new)
            waiting.append(ours)
            if step % 2 == 1:
                for result in waiting:
                    (q if end[0] else h).update(result)
                waiting = []

    strips(hw, qw, left, wide, turn, rows, n)
    for field, out in ((0, heat_strip), (1, pore_strip)):
        for r in range(rows):
            out[r] = turn[field, pl.ds(r, DEEP, stride=rows), :]
    for field, state, edge, mid in ((0, h, heat_edge, heat_mid), (1, q, pore_edge, pore_mid)):
        for c in range(DEEP + 1):
            for j, v in enumerate(pick(state[width - 1 - DEEP - c], state[DEEP + c])):
                edge[c, j] = v
        back(
            [state[c] for c in range(2 * DEEP, width - 2 * DEEP)], wide_mid.at[field],
            turn_mid.at[field], rows, total, field == 0,
        )
        for r in range(rows):
            for g in range(0, cols - 2 * DEEP, SUB):
                mid[r, g : g + SUB] = turn_mid[field, pl.ds(g * rows + r, SUB, stride=rows), :]


def far_edge(
    mask_ref, heat_edge, pore_edge, heat_kept, pore_kept, heat_mid, pore_mid, flag_ref, got_ref,
    heat_near, pore_near, block, send_ref, wide, turn,
):
    rows, cols = heat_mid.shape[0], heat_mid.shape[1] + 2 * DEEP
    n = heat_edge.shape[1]
    span = range(n)
    side, left, (h, q), mask = halo(False, flag_ref, got_ref, wide, rows, n)
    for state, edge in ((h, heat_edge), (q, pore_edge)):
        for c in range(DEEP + 1):
            state[DEEP + c] = [edge[c, j] for j in span]
    for p in range(PAIRS):
        lo = 2 * p + 1
        then = dict(h)
        then[lo + DEEP] = [heat_kept[p, j] for j in span]
        h.update(*advance((False, then, q, lo, lo + DEEP, mask), twice=False))
        lo = lo + 1
        then = dict(q)
        then[lo + DEEP] = [pore_kept[p, j] for j in span]
        q.update(*advance((True, h, then, lo, lo + DEEP, mask), twice=False))
    strips(h, q, left, wide, turn, rows, n)
    end = cols - DEEP
    far_at = pl.ds(pl.multiple_of(end * side, SUB), DEEP)
    near_at = pl.ds(pl.multiple_of(end - end * side, SUB), DEEP)
    for field, mid, near in ((0, heat_mid, heat_near), (1, pore_mid, pore_near)):
        for r in range(rows):
            block[field, r, DEEP:end] = mid[r]
            block[field, r, near_at] = near[r]
            block[field, r, far_at] = turn[field, pl.ds(r, DEEP, stride=rows), :]
    chosen(mask_ref, 0, block, send_ref)


def tile_of(block, field, s):
    tx, ty = block.shape[1] // 2, block.shape[2] // 2
    i, k = s // 2, s % 2
    return block[field, i * tx : (i + 1) * tx, k * ty : (k + 1) * ty, :]


def chosen(mask_ref, i, block, out):
    choose = mask_at(out.shape[0])[0]
    for field, scale, shift in ((0, HEAT_SCALE, HEAT_SHIFT), (1, PORE_SCALE, PORE_SHIFT)):
        for k in range(out.shape[0]):
            v = tile_of(block, field, 0)
            for s in range(1, 4):
                v = jnp.where(
                    held(mask_ref, choose(i, k, s), v.shape), tile_of(block, field, s), v
                )
            out[k, field] = encode(v, scale, shift)


def split(mask_ref, block, heat_out, pore_out, later_ref):
    for field, out in ((0, heat_out), (1, pore_out)):
        for s in range(4):
            out[s] = tile_of(block, field, s)
    chosen(mask_ref, 1, block, later_ref)


def held(mask_ref, row, shape):
    m = mask_ref[row]
    m = jnp.concatenate([m] * (shape[1] // SUB), axis=0)
    return jnp.broadcast_to(m[None], shape) > 0.5


def resend(mask_ref, got_ref, local_ref, send_ref):
    ranks = got_ref.shape[0]
    shape = got_ref.shape[2:]
    again = mask_at(ranks)[2]
    for k in range(ranks):
        for f in range(2):
            v = local_ref[k, f].astype(jnp.int32)
            for r in range(ranks):
                v = jnp.where(
                    held(mask_ref, again(k, r), shape), got_ref[r, f].astype(jnp.int32), v
                )
            send_ref[k, f] = v.astype(jnp.int16)


def place(mask_ref, heat_ref, pore_ref, first_ref, second_ref, heat_out, pore_out):
    ranks = first_ref.shape[0]
    shape = first_ref.shape[2:]
    taken = mask_at(ranks)[1]
    for field, src, out, scale, shift in (
        (0, heat_ref, heat_out, HEAT_SCALE, HEAT_SHIFT),
        (1, pore_ref, pore_out, PORE_SCALE, PORE_SHIFT),
    ):
        came = [
            (i, r, decode(got[r, field], scale, shift))
            for i, got in ((0, first_ref), (1, second_ref))
            for r in range(ranks)
        ]
        for s in range(4):
            v = src[s]
            for i, r, tile in came:
                v = jnp.where(held(mask_ref, taken(i, r, s), shape), tile, v)
            out[s] = v


def call(body, spec, outs, scratch=(), out_space=pltpu.VMEM):
    def run(*args):
        space = {"s": pltpu.SMEM, "v": pltpu.VMEM, "V": pltpu.VMEM}
        args = [
            pltpu.with_memory_space_constraint(a, pltpu.VMEM if c == "V" else pltpu.HBM)
            for c, a in zip(spec, args)
        ]
        shapes = [
            pltpu.VMEM(s, d) if out_space is not None else jax.ShapeDtypeStruct(s, d)
            for s, d in outs
        ]
        return pl.pallas_call(
            body,
            in_specs=[pl.BlockSpec(memory_space=space[c]) for c in spec],
            out_specs=[pl.BlockSpec(memory_space=pltpu.VMEM) for _ in outs],
            out_shape=shapes,
            scratch_shapes=list(scratch),
            compiler_params=pltpu.CompilerParams(vmem_limit_bytes=VMEM_LIMIT),
        )(*args)

    return run


def permute(value, partner):
    nx, ny = lax.axis_size("gx"), lax.axis_size("gy")
    pairs = []
    for x in range(nx):
        for y in range(ny):
            u, v = partner(x, y)
            pairs.append((x * ny + y, u * ny + v))
    return lax.ppermute(value, ("gx", "gy"), pairs)


def exchange_x(value):
    nx, ny = lax.axis_size("gx"), lax.axis_size("gy")

    def partner(x, y, near):
        if near:
            return x ^ 1, y
        if 0 < x < nx - 1:
            return ((x + 1) ^ 1) - 1, y
        return (x, y ^ 2) if ny % 4 == 0 else (x, y)

    first = permute(value, lambda x, y: partner(x, y, y % 2 == 0))
    second = permute(value, lambda x, y: partner(x, y, y % 2 == 1))
    return first, second


def exchange_y(near, far):
    ny = lax.axis_size("gy")

    def partner(x, y):
        if 0 < y < ny - 1:
            return x, ((y + 1) ^ 1) - 1
        return x ^ 1, y

    far = permute(far, partner)
    near = permute(near, lambda x, y: (x, y ^ 1))
    return near, far


def swap(value, axis):
    n = lax.axis_size(axis)
    return lax.ppermute(value, axis, [(i, (i + n // 2) % n) for i in range(n)])


def per_device(enthalpy, porosity, active, move_count, move_slot):
    rows, cols, depth = enthalpy.shape
    tx, ty = rows // 2, cols // 2
    count = move_count.reshape(2)
    slots = move_slot.reshape(2, move_slot.shape[-1])
    ranks = slots.shape[1]
    f32, bf16, i16 = jnp.float32, jnp.bfloat16, jnp.int16

    block = ((rows, cols, depth), f32)
    masks = ((mask_at(ranks)[3], SUB, LANES), f32)
    own, enthalpy, porosity, masks = call(
        pack_x, "sssvv",
        [((2 * rows * cols // SUB + 1, SUB, depth), bf16), block, block, masks],
    )(active, count, slots, enthalpy, porosity)
    x_near, x_far = exchange_x(own)
    side = ((4 * rows + 1, DEEP, depth), bf16)
    near, far = call(pack_y, "VVV", [side, side])(own, x_near, x_far)
    y_near, y_far = exchange_y(near, far)
    total = rows + 2 * DEEP
    n = total // SUB
    tiles = ((4, tx, ty, depth), f32)
    parcel = ((ranks, 2, tx, ty, depth), i16)
    column = (n, SUB, depth)
    whole = ((cols, *column), f32)
    save = ((EARLY, 2, *column), f32)
    edge = ((DEEP + 1, *column), f32)
    kept = ((PAIRS, *column), f32)
    mid = ((rows, cols - 2 * DEEP, depth), f32)
    strip = ((rows, DEEP, depth), f32)
    state = call(
        inner, "VVVVV", [whole, whole, save, save, ((2, *column), f32)],
        [pltpu.VMEM((2, total * cols, depth), f32)],
    )(own, enthalpy, porosity, x_near, x_far)
    scratch = [
        pltpu.VMEM((2, total * DEEP, depth), f32),
        pltpu.VMEM((2, rows * DEEP, depth), f32),
    ]
    heat_near, pore_near, heat_mid, pore_mid, *ends = call(
        middle, "V" * 6, [strip, strip, mid, mid, edge, edge, kept, kept],
        scratch
        + [
            pltpu.VMEM((2, total * (cols - 2 * DEEP), depth), f32),
            pltpu.VMEM((2, rows * (cols - 2 * DEEP), depth), f32),
        ],
    )(*state, y_near)
    last, first = call(
        far_edge, "V" * 11, [((2, rows, cols, depth), f32), parcel], scratch
    )(masks, *ends, heat_mid, pore_mid, state[4], y_far, heat_near, pore_near)
    heat, pore, later = call(split, "VV", [tiles, tiles, parcel])(masks, last)
    first = swap(first, "gx")
    (second,) = call(resend, "VVV", [parcel])(masks, first, later)
    second = swap(second, "gy")
    heat, pore = call(place, "VVVVV", [tiles, tiles], out_space=None)(
        masks, heat, pore, first, second
    )
    return heat[None, None], pore[None, None]


def solution(mesh):
    placed = (
        P("gx", "gy", None),
        P("gx", "gy", None),
        P("gx", "gy"),
        P("gx", "gy", None),
        P("gx", "gy", None, None),
    )
    out = P("gx", "gy", None, None, None, None)

    return jax.shard_map(
        per_device, mesh=mesh, in_specs=placed, out_specs=(out, out), check_vma=False
    )
```

```python
import jax
import jax.numpy as jnp
from jax import lax
from jax.experimental import pallas as pl
from jax.experimental.pallas import tpu as pltpu
from jax.sharding import PartitionSpec as P


PAIRS = 4
DEEP = 2 * PAIRS
EARLY = PAIRS // 2
SUB = 8
LANES = 128
VMEM_LIMIT = 16 * 2**20

HEAT_SCALE = 16000.0
HEAT_SHIFT = 20000.0
PORE_SCALE = 25000.0
PORE_SHIFT = 7750.0


def encode(values, scale, shift):
    codes = jnp.floor(values * scale + (0.5 - shift))
    return jnp.clip(codes, -32768.0, 32767.0).astype(jnp.int32).astype(jnp.int16)


def decode(codes, scale, shift):
    return (codes.astype(jnp.int32).astype(jnp.float32) + shift) * (1.0 / scale)


def flag_rows(active_ref, cols):
    lane = lax.broadcasted_iota(jnp.int32, (cols, LANES), 1)
    col = lax.broadcasted_iota(jnp.int32, (cols, LANES), 0)

    def flag(i):
        return jnp.where(col < cols // 2, active_ref[i, 0], active_ref[i, 1])

    return jnp.where(lane < LANES // 2, flag(0), flag(1)).astype(jnp.float32)


def mask_at(ranks):
    choose = lambda i, k, s: (i * ranks + k) * 4 + s
    taken = lambda i, r, s: 8 * ranks + (i * ranks + r) * 4 + s
    again = lambda k, r: 16 * ranks + k * ranks + r
    return choose, taken, again, 16 * ranks + ranks * ranks


def pack_x(
    active_ref, count_ref, slot_ref, heat_ref, pore_ref, out_ref, heat_out, pore_out, mask_ref
):
    rows, cols = heat_ref.shape[0], heat_ref.shape[1]
    ranks = slot_ref.shape[1]
    out_ref[0:rows] = heat_ref[...].astype(jnp.bfloat16)
    out_ref[rows : 2 * rows] = pore_ref[...].astype(jnp.bfloat16)
    out_ref[2 * rows] = flag_rows(active_ref, cols).astype(jnp.bfloat16)
    heat_out[...] = heat_ref[...]
    pore_out[...] = pore_ref[...]
    choose, taken, again, _ = mask_at(ranks)

    def put(row, holds):
        mask_ref[row] = jnp.full((SUB, LANES), jnp.where(holds, 1.0, 0.0), jnp.float32)

    for i in range(2):
        for k in range(ranks):
            for s in range(4):
                here = slot_ref[i, k] == s
                put(choose(i, k, s), here)
                put(taken(i, k, s), here & (k < count_ref[i]))
    for k in range(ranks):
        for r in range(ranks):
            put(again(k, r), (slot_ref[1, k] == slot_ref[0, r]) & (r < count_ref[0]))


def inside(axis, below):
    at = lax.axis_index(axis)
    has = at < lax.axis_size(axis) - 1 if below else at > 0
    return jnp.where(has, 1.0, 0.0).astype(jnp.float32)


def x_parts(own_ref, first_ref, second_ref):
    odd = lax.rem(lax.axis_index("gx") + lax.axis_index("gy"), 2)
    return ((2 - 2 * odd, first_ref), (1, own_ref), (2 * odd, second_ref))


def pack_y(own_ref, first_ref, second_ref, near_out, far_out):
    rows = (own_ref.shape[0] - 1) // 2
    cols = own_ref.shape[1]
    side = 2 * rows
    odd = lax.rem(lax.axis_index("gy"), 2)
    edge = cols - DEEP
    sub = lax.broadcasted_iota(jnp.int32, (DEEP, LANES), 0)
    sides = ((near_out, edge - edge * odd, odd == 0), (far_out, edge * odd, odd == 1))
    for out_ref, start, right in sides:
        at = pl.ds(pl.multiple_of(start, DEEP), DEEP)
        flags = jnp.zeros((DEEP, LANES), jnp.float32)
        for i, part in x_parts(own_ref, first_ref, second_ref):
            flags = jnp.where(sub == i, part[2 * rows, at, :].astype(jnp.float32), flags)
            for f in range(2):
                if part is own_ref:
                    out_ref[pl.ds(f * side, rows)] = part[pl.ds(f * rows, rows), at, :]
                    continue
                for d in range(1, rows // 2 + 1):
                    a, b = (
                        part[f * rows + jnp.where(i == 0, rows - e, e - 1), at, :].astype(jnp.float32)
                        for e in (d, rows - d)
                    )
                    if d < rows - d:
                        a = jnp.where(
                            right,
                            jnp.where(sub >= d, a, pltpu.roll(b, d, 0)),
                            jnp.where(sub < DEEP - d, a, pltpu.roll(b, DEEP - d, 0)),
                        )
                    out_ref[f * side + rows + (i // 2) * (rows // 2) + d - 1] = a.astype(jnp.bfloat16)
        out_ref[2 * side] = flags.astype(jnp.bfloat16)


def edge_row(part, field, x, rows, right):
    side = 2 * rows
    if rows <= x < 2 * rows:
        return part[field * side + x - rows].astype(jnp.float32)
    d = rows - x if x < rows else x - 2 * rows + 1
    at = field * side + rows + (0 if x < rows else rows // 2) - 1
    if d <= rows // 2:
        return part[at + d].astype(jnp.float32)
    if d == rows:
        return part[at + rows // 2].astype(jnp.float32)
    v = part[at + rows - d].astype(jnp.float32)
    return jnp.where(right, pltpu.roll(v, d, 0), pltpu.roll(v, DEEP - d, 0))


def flux_sums(parts, twice):
    lane = lax.broadcasted_iota(jnp.int32, (SUB, LANES), 1)
    depths = []
    for val, wgt, lo, hi in parts:
        depths.append(
            {
                (c, j): [
                    (pltpu.roll(v, by, 1), pltpu.roll(w, by, 1))
                    for by in ((LANES - 1,) if twice else (LANES - 1, 1))
                ]
                for c in range(lo, hi)
                for j, (v, w) in enumerate(zip(val[c], wgt[c]))
            }
        )
    for (val, wgt, _, _), depth in zip(parts, depths):
        for (c, j), shifted in depth.items():
            f = None
            for (v, w), ok in zip(shifted, (lane < LANES - 1, lane > 0)):
                g = jnp.where(ok, (wgt[c][j] + w) * (v - val[c][j]), 0.0)
                f = g if f is None else f + g
            depth[c, j] = f
    for depth in depths:
        for at, f in depth.items():
            depth[at] = f - pltpu.roll(f, 1, 1) if twice else f

    sums = []
    for (val, wgt, lo, hi), depth in zip(parts, depths):
        n = len(val[lo])
        span = range(n)

        def toward(c):
            return [(wgt[c][j] + wgt[c + 1][j]) * (val[c + 1][j] - val[c][j]) for j in span]

        out = {}
        last = toward(lo - 1)
        for c in range(lo, hi):
            v, w = val[c], wgt[c]
            ahead = toward(c)
            down = [(w[j] + w[j + 1]) * (v[j + 1] - v[j]) for j in range(n - 1)]
            down.append(
                (w[n - 1] + pltpu.roll(w[0], SUB - 1, 0))
                * (pltpu.roll(v[0], SUB - 1, 0) - v[n - 1])
            )
            up = [pltpu.roll(down[-1], 1, 0)] + down[:-1]
            out[c] = [(ahead[j] - last[j]) + (down[j] - up[j]) + depth[c, j] for j in span]
            last = ahead
        sums.append(out)
    return sums


def advance(*parts, twice=True):
    fluxes = []
    for pore, h, q, lo, hi, _ in parts:
        val, wgt = {}, {}
        for c in range(lo - 1, hi + 1):
            t = [jnp.tanh(v) for v in h[c]]
            temp = [2.5 * v - u for v, u in zip(h[c], t)]
            if pore:
                val[c] = q[c]
                wgt[c] = [1.0 + jnp.tanh(v) for v in temp]
            else:
                val[c] = temp
                wgt[c] = [(1.0 - v) * (1.0 - v) * (u + 7.0 / 3.0) for v, u in zip(q[c], t)]
        fluxes.append((val, wgt, lo, hi))
    results = []
    for (pore, h, q, lo, hi, mask), (val, wgt, _, _), acc in zip(parts, fluxes, flux_sums(fluxes, twice)):
        new = {}
        for c in range(lo, hi):
            if pore:
                new[c] = [
                    v + m * (a - 4.0 * r * v)
                    for v, m, a, r in zip(q[c], mask(c, 1), acc[c], wgt[c])
                ]
            else:
                new[c] = [v + m * a for v, m, a in zip(h[c], mask(c, 0), acc[c])]
        results.append(new)
    return results


def tile_rows(marks, i, tx, n, out):
    low = lax.broadcasted_iota(jnp.int32, (SUB, LANES), 1) < LANES // 2
    sub = lax.broadcasted_iota(jnp.int32, (SUB, LANES), 0)
    other = pltpu.roll(marks, LANES // 2, 1)
    for h, flag in ((0, jnp.where(low, marks, other)), (1, jnp.where(low, other, marks))):
        first = (2 * i + h) * tx
        for j in range(n):
            x = sub * n + j
            out[j] = jnp.where((x >= first) & (x < first + tx), flag, out[j])
    return out


def scalings(flags):
    return ([0.009 * f for f in flags], [0.0375 * f for f in flags])


def back(columns, wide, turn, rows, total, heat):
    for c, column in enumerate(columns):
        n = len(column)
        for j, v in enumerate(column):
            wide[pl.ds(c * total + j, SUB, stride=n), :] = 0.5 * v + 1.0 if heat else v
    for c in range(len(columns)):
        turn[pl.ds(c * rows, rows), :] = wide[pl.ds(c * total + DEEP, rows), :]


def inner(
    own_ref, heat_ref, pore_ref, xa_ref, xb_ref,
    heat_out, pore_out, heat_save, pore_save, flag_out, wide,
):
    rows, cols = heat_ref.shape[0], heat_ref.shape[1]
    total = rows + 2 * DEEP
    width = cols + 2 * DEEP
    n = total // SUB
    tx, ty = rows // 2, cols // 2
    f32 = jnp.float32
    odd = lax.rem(lax.axis_index("gx") + lax.axis_index("gy"), 2)

    def row(i, r):
        if i == 1:
            return own_ref[r].astype(f32)
        pair = (xa_ref[r], xb_ref[r]) if i == 0 else (xb_ref[r], xa_ref[r])
        v = jnp.where(odd == 1, *pair).astype(f32)
        return v * inside("gx", i == 2)

    flags = []
    marks = [row(i, 2 * rows) for i in range(3)]
    for k in range(2):
        f = [jnp.zeros((SUB, LANES), f32) for _ in range(n)]
        for i in range(3):
            f = tile_rows(marks[i][k * ty : k * ty + SUB], i, tx, n, f)
        for j in range(n):
            flag_out[k, j] = f[j]
        flags.append(scalings(f))

    def mask(c, kind):
        return flags[0 if c < DEEP + ty else 1][kind]

    h, q = {}, {}
    for field, home, state in ((0, heat_ref, h), (1, pore_ref, q)):
        for i in range(3):
            for r in range(rows):
                v = home[r] if i == 1 else row(i, field * rows + r)
                v = 2.0 * v - 2.0 if field == 0 else v
                for g in range(0, cols, SUB):
                    at = g * total + (i * rows + r) * SUB
                    wide[field, at : at + SUB, :] = v[g : g + SUB]
        for c in range(cols):
            at = c // SUB * SUB * total + c % SUB
            state[DEEP + c] = [
                wide[field, pl.ds(at + j * SUB, SUB, stride=n * SUB), :] for j in range(n)
            ]

    for p in range(EARLY):
        lo, hi = DEEP + 2 * p + 1, width - DEEP - 2 * p - 1
        for side, c in ((0, lo), (1, hi - 1)):
            for j in range(n):
                heat_save[p, side, j] = h[c][j]
        h.update(*advance((False, h, q, lo, hi, mask)))
        lo, hi = lo + 1, hi - 1
        for side, c in ((0, lo), (1, hi - 1)):
            for j in range(n):
                pore_save[p, side, j] = q[c][j]
        q.update(*advance((True, h, q, lo, hi, mask)))
    for state, out in ((h, heat_out), (q, pore_out)):
        for c in range(cols):
            for j in range(n):
                out[c, j] = state[DEEP + c][j]


def halo(near, flag_ref, got_ref, wide, rows, n):
    total = n * SUB
    tx = rows // 2
    f32 = jnp.float32
    odd = lax.rem(lax.axis_index("gy"), 2)
    side = 1 - odd if near else odd
    left = side == 0
    has = None if near else jnp.where(left, inside("gy", False), inside("gy", True))
    row_open = (inside("gx", False), None, inside("gx", True))

    def scaled(v, *by):
        for s in by:
            v = v if s is None else v * s
        return v

    marks = scaled(got_ref[4 * rows].astype(f32), has)
    beyond = [jnp.zeros((SUB, LANES), f32) for _ in range(n)]
    for i in range(3):
        row = jnp.broadcast_to(scaled(marks[i : i + 1], row_open[i]), (SUB, LANES))
        beyond = tile_rows(row, i, tx, n, beyond)
    flags = [scalings(beyond), scalings([flag_ref[side, j] for j in range(n)])]

    def mask(c, kind):
        return flags[0 if c < DEEP else 1][kind]

    states = ({}, {})
    for field, state in enumerate(states):
        for x in range(total):
            v = scaled(edge_row(got_ref, field, x, rows, left), has, row_open[x // rows])
            wide[field, x * DEEP : (x + 1) * DEEP, :] = 2.0 * v - 2.0 if field == 0 else v
        for c in range(DEEP):
            state[c] = [
                jnp.where(
                    left,
                    wide[field, pl.ds(j * DEEP + c, SUB, stride=n * DEEP), :],
                    wide[field, pl.ds(j * DEEP + DEEP - 1 - c, SUB, stride=n * DEEP), :],
                )
                for j in range(n)
            ]
    return side, left, states, mask


def strips(h, q, left, wide, turn, rows, n):
    total = n * SUB
    for field, state in ((0, h), (1, q)):
        for c in range(DEEP):
            for j, v in enumerate(state[DEEP + c]):
                wide[field, pl.ds(c * total + j, SUB, stride=n), :] = (
                    0.5 * v + 1.0 if field == 0 else v
                )
        for c in range(DEEP):
            at = pl.multiple_of(jnp.where(left, c, DEEP - 1 - c) * rows, SUB)
            turn[field, pl.ds(at, rows), :] = wide[field, pl.ds(c * total + DEEP, rows), :]


def middle(
    heat_in, pore_in, heat_save, pore_save, flag_ref, got_ref,
    heat_strip, pore_strip, heat_mid, pore_mid, heat_edge, pore_edge, heat_kept, pore_kept,
    wide, turn, wide_mid, turn_mid,
):
    rows, cols = heat_mid.shape[0], heat_in.shape[0]
    n = heat_in.shape[1]
    width = cols + 2 * DEEP
    total = n * SUB
    ty = cols // 2
    span = range(n)
    side, left, (hw, qw), mask_w = halo(True, flag_ref, got_ref, wide, rows, n)
    flags = [scalings([flag_ref[k, j] for j in span]) for k in range(2)]

    def mask(c, kind):
        return flags[0 if c < DEEP + ty else 1][kind]

    h = {DEEP + c: [heat_in[c, j] for j in span] for c in range(cols)}
    q = {DEEP + c: [pore_in[c, j] for j in span] for c in range(cols)}

    def pick(low, high):
        return [jnp.where(left, a, b) for a, b in zip(low, high)]

    def at(state, c):
        return pick(state[c], state[width - 1 - c])

    kept = ({}, {})
    for p in range(EARLY):
        for keep, save, out in zip(kept, (heat_save, pore_save), (heat_kept, pore_kept)):
            keep[p] = [save[p, side, j] for j in span]
            for j in span:
                out[p, j] = save[p, 1 - side, j]

    def keep_now(field, state, p, c):
        low, high = state[c], state[width - 1 - c]
        kept[field][p] = pick(low, high)
        for j, v in enumerate(pick(high, low)):
            (heat_kept, pore_kept)[field][p, j] = v

    waiting = []

    def block_half(step):
        p, k = EARLY + step // 4, step % 4
        pore = k >= 2
        lo = DEEP + 2 * p + (2 if pore else 1)
        if k % 2 == 0:
            keep_now(int(pore), q if pore else h, p, lo)
        half = (lo, width // 2) if k % 2 == 0 else (width // 2, width - lo)
        return (pore, h, q, *half, mask)

    for p in range(PAIRS):
        for pore in (False, True):
            step = 2 * p + pore
            lo = 2 * p + 1 + pore
            end = block_half(step)
            if pore:
                hw[lo + DEEP - 1], hw[lo + DEEP] = at(h, lo + DEEP - 1), at(h, lo + DEEP)
                then = dict(qw)
                then[lo + DEEP] = kept[1][p]
                part = (True, hw, then, lo, lo + DEEP, mask_w)
            else:
                c = lo + DEEP - 1
                hw[c] = at(h, c)
                qw[c], qw[c + 1] = at(q, c), at(q, c + 1)
                then = dict(hw)
                then[c + 1] = kept[0][p]
                part = (False, then, qw, lo, lo + DEEP, mask_w)
            new, ours = advance(part, end)
            (qw if pore else hw).update(new)
            waiting.append(ours)
            if step % 2 == 1:
                for result in waiting:
                    (q if end[0] else h).update(result)
                waiting = []

    strips(hw, qw, left, wide, turn, rows, n)
    for field, out in ((0, heat_strip), (1, pore_strip)):
        for r in range(rows):
            out[r] = turn[field, pl.ds(r, DEEP, stride=rows), :]
    for field, state, edge, mid in ((0, h, heat_edge, heat_mid), (1, q, pore_edge, pore_mid)):
        for c in range(DEEP + 1):
            for j, v in enumerate(pick(state[width - 1 - DEEP - c], state[DEEP + c])):
                edge[c, j] = v
        back(
            [state[c] for c in range(2 * DEEP, width - 2 * DEEP)], wide_mid.at[field],
            turn_mid.at[field], rows, total, field == 0,
        )
        for r in range(rows):
            for g in range(0, cols - 2 * DEEP, SUB):
                mid[r, g : g + SUB] = turn_mid[field, pl.ds(g * rows + r, SUB, stride=rows), :]


def far_edge(
    mask_ref, heat_edge, pore_edge, heat_kept, pore_kept, heat_mid, pore_mid, flag_ref, got_ref,
    heat_near, pore_near, block, send_ref, wide, turn,
):
    rows, cols = heat_mid.shape[0], heat_mid.shape[1] + 2 * DEEP
    n = heat_edge.shape[1]
    span = range(n)
    side, left, (h, q), mask = halo(False, flag_ref, got_ref, wide, rows, n)
    for state, edge in ((h, heat_edge), (q, pore_edge)):
        for c in range(DEEP + 1):
            state[DEEP + c] = [edge[c, j] for j in span]
    for p in range(PAIRS):
        lo = 2 * p + 1
        then = dict(h)
        then[lo + DEEP] = [heat_kept[p, j] for j in span]
        h.update(*advance((False, then, q, lo, lo + DEEP, mask), twice=False))
        lo = lo + 1
        then = dict(q)
        then[lo + DEEP] = [pore_kept[p, j] for j in span]
        q.update(*advance((True, h, then, lo, lo + DEEP, mask), twice=False))
    strips(h, q, left, wide, turn, rows, n)
    end = cols - DEEP
    far_at = pl.ds(pl.multiple_of(end * side, SUB), DEEP)
    near_at = pl.ds(pl.multiple_of(end - end * side, SUB), DEEP)
    for field, mid, near in ((0, heat_mid, heat_near), (1, pore_mid, pore_near)):
        for r in range(rows):
            block[field, r, DEEP:end] = mid[r]
            block[field, r, near_at] = near[r]
            block[field, r, far_at] = turn[field, pl.ds(r, DEEP, stride=rows), :]
    chosen(mask_ref, 0, block, send_ref)


def tile_of(block, field, s):
    tx, ty = block.shape[1] // 2, block.shape[2] // 2
    i, k = s // 2, s % 2
    return block[field, i * tx : (i + 1) * tx, k * ty : (k + 1) * ty, :]


def chosen(mask_ref, i, block, out):
    choose = mask_at(out.shape[0])[0]
    for field, scale, shift in ((0, HEAT_SCALE, HEAT_SHIFT), (1, PORE_SCALE, PORE_SHIFT)):
        for k in range(out.shape[0]):
            v = tile_of(block, field, 0)
            for s in range(1, 4):
                v = jnp.where(
                    held(mask_ref, choose(i, k, s), v.shape), tile_of(block, field, s), v
                )
            out[k, field] = encode(v, scale, shift)


def split(mask_ref, block, heat_out, pore_out, later_ref):
    for field, out in ((0, heat_out), (1, pore_out)):
        for s in range(4):
            out[s] = tile_of(block, field, s)
    chosen(mask_ref, 1, block, later_ref)


def held(mask_ref, row, shape):
    m = mask_ref[row]
    m = jnp.concatenate([m] * (shape[1] // SUB), axis=0)
    return jnp.broadcast_to(m[None], shape) > 0.5


def resend(mask_ref, got_ref, local_ref, send_ref):
    ranks = got_ref.shape[0]
    shape = got_ref.shape[2:]
    again = mask_at(ranks)[2]
    for k in range(ranks):
        for f in range(2):
            v = local_ref[k, f].astype(jnp.int32)
            for r in range(ranks):
                v = jnp.where(
                    held(mask_ref, again(k, r), shape), got_ref[r, f].astype(jnp.int32), v
                )
            send_ref[k, f] = v.astype(jnp.int16)


def place(mask_ref, heat_ref, pore_ref, first_ref, second_ref, heat_out, pore_out):
    ranks = first_ref.shape[0]
    shape = first_ref.shape[2:]
    taken = mask_at(ranks)[1]
    for field, src, out, scale, shift in (
        (0, heat_ref, heat_out, HEAT_SCALE, HEAT_SHIFT),
        (1, pore_ref, pore_out, PORE_SCALE, PORE_SHIFT),
    ):
        came = [
            (i, r, decode(got[r, field], scale, shift))
            for i, got in ((0, first_ref), (1, second_ref))
            for r in range(ranks)
        ]
        for s in range(4):
            v = src[s]
            for i, r, tile in came:
                v = jnp.where(held(mask_ref, taken(i, r, s), shape), tile, v)
            out[s] = v


def call(body, spec, outs, scratch=(), out_space=pltpu.VMEM):
    def run(*args):
        space = {"s": pltpu.SMEM, "v": pltpu.VMEM, "V": pltpu.VMEM}
        args = [
            pltpu.with_memory_space_constraint(a, pltpu.VMEM if c == "V" else pltpu.HBM)
            for c, a in zip(spec, args)
        ]
        shapes = [
            pltpu.VMEM(s, d) if out_space is not None else jax.ShapeDtypeStruct(s, d)
            for s, d in outs
        ]
        return pl.pallas_call(
            body,
            in_specs=[pl.BlockSpec(memory_space=space[c]) for c in spec],
            out_specs=[pl.BlockSpec(memory_space=pltpu.VMEM) for _ in outs],
            out_shape=shapes,
            scratch_shapes=list(scratch),
            compiler_params=pltpu.CompilerParams(vmem_limit_bytes=VMEM_LIMIT),
        )(*args)

    return run


def permute(value, partner):
    nx, ny = lax.axis_size("gx"), lax.axis_size("gy")
    pairs = []
    for x in range(nx):
        for y in range(ny):
            u, v = partner(x, y)
            pairs.append((x * ny + y, u * ny + v))
    return lax.ppermute(value, ("gx", "gy"), pairs)


def exchange_x(value):
    nx, ny = lax.axis_size("gx"), lax.axis_size("gy")

    def partner(x, y, near):
        if near:
            return x ^ 1, y
        if 0 < x < nx - 1:
            return ((x + 1) ^ 1) - 1, y
        return (x, y ^ 2) if ny % 4 == 0 else (x, y)

    first = permute(value, lambda x, y: partner(x, y, y % 2 == 0))
    second = permute(value, lambda x, y: partner(x, y, y % 2 == 1))
    return first, second


def exchange_y(near, far):
    ny = lax.axis_size("gy")

    def partner(x, y):
        if 0 < y < ny - 1:
            return x, ((y + 1) ^ 1) - 1
        return x ^ 1, y

    far = permute(far, partner)
    near = permute(near, lambda x, y: (x, y ^ 1))
    return near, far


def swap(value, axis):
    n = lax.axis_size(axis)
    return lax.ppermute(value, axis, [(i, (i + n // 2) % n) for i in range(n)])


def per_device(enthalpy, porosity, active, move_count, move_slot):
    rows, cols, depth = enthalpy.shape
    tx, ty = rows // 2, cols // 2
    count = move_count.reshape(2)
    slots = move_slot.reshape(2, move_slot.shape[-1])
    ranks = slots.shape[1]
    f32, bf16, i16 = jnp.float32, jnp.bfloat16, jnp.int16

    block = ((rows, cols, depth), f32)
    masks = ((mask_at(ranks)[3], SUB, LANES), f32)
    own, enthalpy, porosity, masks = call(
        pack_x, "sssvv", [((2 * rows + 1, cols, depth), bf16), block, block, masks]
    )(active, count, slots, enthalpy, porosity)
    x_near, x_far = exchange_x(own)
    side = ((4 * rows + 1, DEEP, depth), bf16)
    near, far = call(pack_y, "VVV", [side, side])(own, x_near, x_far)
    y_near, y_far = exchange_y(near, far)
    total = rows + 2 * DEEP
    n = total // SUB
    tiles = ((4, tx, ty, depth), f32)
    parcel = ((ranks, 2, tx, ty, depth), i16)
    column = (n, SUB, depth)
    whole = ((cols, *column), f32)
    save = ((EARLY, 2, *column), f32)
    edge = ((DEEP + 1, *column), f32)
    kept = ((PAIRS, *column), f32)
    mid = ((rows, cols - 2 * DEEP, depth), f32)
    strip = ((rows, DEEP, depth), f32)
    state = call(
        inner, "VVVVV", [whole, whole, save, save, ((2, *column), f32)],
        [pltpu.VMEM((2, total * cols, depth), f32)],
    )(own, enthalpy, porosity, x_near, x_far)
    scratch = [
        pltpu.VMEM((2, total * DEEP, depth), f32),
        pltpu.VMEM((2, rows * DEEP, depth), f32),
    ]
    heat_near, pore_near, heat_mid, pore_mid, *ends = call(
        middle, "V" * 6, [strip, strip, mid, mid, edge, edge, kept, kept],
        scratch
        + [
            pltpu.VMEM((2, total * (cols - 2 * DEEP), depth), f32),
            pltpu.VMEM((2, rows * (cols - 2 * DEEP), depth), f32),
        ],
    )(*state, y_near)
    last, first = call(
        far_edge, "V" * 11, [((2, rows, cols, depth), f32), parcel], scratch
    )(masks, *ends, heat_mid, pore_mid, state[4], y_far, heat_near, pore_near)
    heat, pore, later = call(split, "VV", [tiles, tiles, parcel])(masks, last)
    first = swap(first, "gx")
    (second,) = call(resend, "VVV", [parcel])(masks, first, later)
    second = swap(second, "gy")
    heat, pore = call(place, "VVVVV", [tiles, tiles], out_space=None)(
        masks, heat, pore, first, second
    )
    return heat[None, None], pore[None, None]


def solution(mesh):
    placed = (
        P("gx", "gy", None),
        P("gx", "gy", None),
        P("gx", "gy"),
        P("gx", "gy", None),
        P("gx", "gy", None, None),
    )
    out = P("gx", "gy", None, None, None, None)

    return jax.shard_map(
        per_device, mesh=mesh, in_specs=placed, out_specs=(out, out), check_vma=False
    )
```

```python
import jax
import jax.numpy as jnp
from jax import lax
from jax.experimental import pallas as pl
from jax.experimental.pallas import tpu as pltpu
from jax.sharding import PartitionSpec as P


PAIRS = 4
DEEP = 2 * PAIRS
EARLY = PAIRS // 2
SUB = 8
LANES = 128
VMEM_LIMIT = 16 * 2**20

HEAT_SCALE = 25000.0
HEAT_SHIFT = 32000.0
PORE_SCALE = 40000.0
PORE_SHIFT = 7000.0


def encode(values, scale, shift):
    return jnp.floor(values * scale + (0.5 - shift)).astype(jnp.int32).astype(jnp.int16)


def decode(codes, scale, shift):
    return (codes.astype(jnp.int32).astype(jnp.float32) + shift) * (1.0 / scale)


def flag_rows(active_ref, cols):
    lane = lax.broadcasted_iota(jnp.int32, (cols, LANES), 1)
    col = lax.broadcasted_iota(jnp.int32, (cols, LANES), 0)

    def flag(i):
        return jnp.where(col < cols // 2, active_ref[i, 0], active_ref[i, 1])

    return jnp.where(lane < LANES // 2, flag(0), flag(1)).astype(jnp.float32)


def mask_at(ranks):
    choose = lambda i, k, s: (i * ranks + k) * 4 + s
    taken = lambda i, r, s: 8 * ranks + (i * ranks + r) * 4 + s
    again = lambda k, r: 16 * ranks + k * ranks + r
    return choose, taken, again, 16 * ranks + ranks * ranks


def pack_x(
    active_ref, count_ref, slot_ref, heat_ref, pore_ref, out_ref, heat_out, pore_out, mask_ref
):
    rows, cols = heat_ref.shape[0], heat_ref.shape[1]
    ranks = slot_ref.shape[1]
    out_ref[0:rows] = heat_ref[...].astype(jnp.bfloat16)
    out_ref[rows : 2 * rows] = pore_ref[...].astype(jnp.bfloat16)
    out_ref[2 * rows] = flag_rows(active_ref, cols).astype(jnp.bfloat16)
    heat_out[...] = heat_ref[...]
    pore_out[...] = pore_ref[...]
    choose, taken, again, _ = mask_at(ranks)

    def put(row, holds):
        mask_ref[row] = jnp.full((SUB, LANES), jnp.where(holds, 1.0, 0.0), jnp.float32)

    for i in range(2):
        for k in range(ranks):
            for s in range(4):
                here = slot_ref[i, k] == s
                put(choose(i, k, s), here)
                put(taken(i, k, s), here & (k < count_ref[i]))
    for k in range(ranks):
        for r in range(ranks):
            put(again(k, r), (slot_ref[1, k] == slot_ref[0, r]) & (r < count_ref[0]))


def inside(axis, below):
    at = lax.axis_index(axis)
    has = at < lax.axis_size(axis) - 1 if below else at > 0
    return jnp.where(has, 1.0, 0.0).astype(jnp.float32)


def x_parts(own_ref, first_ref, second_ref):
    odd = lax.rem(lax.axis_index("gx") + lax.axis_index("gy"), 2)
    return ((2 - 2 * odd, first_ref), (1, own_ref), (2 * odd, second_ref))


def pack_y(own_ref, first_ref, second_ref, near_out, far_out):
    rows = (own_ref.shape[0] - 1) // 2
    cols = own_ref.shape[1]
    side = 2 * rows
    odd = lax.rem(lax.axis_index("gy"), 2)
    edge = cols - DEEP
    sub = lax.broadcasted_iota(jnp.int32, (DEEP, LANES), 0)
    sides = ((near_out, edge - edge * odd, odd == 0), (far_out, edge * odd, odd == 1))
    for out_ref, start, right in sides:
        at = pl.ds(pl.multiple_of(start, DEEP), DEEP)
        flags = jnp.zeros((DEEP, LANES), jnp.float32)
        for i, part in x_parts(own_ref, first_ref, second_ref):
            flags = jnp.where(sub == i, part[2 * rows, at, :].astype(jnp.float32), flags)
            for f in range(2):
                if part is own_ref:
                    out_ref[pl.ds(f * side, rows)] = part[pl.ds(f * rows, rows), at, :]
                    continue
                for d in range(1, rows // 2 + 1):
                    a, b = (
                        part[f * rows + jnp.where(i == 0, rows - e, e - 1), at, :].astype(jnp.float32)
                        for e in (d, rows - d)
                    )
                    if d < rows - d:
                        a = jnp.where(
                            right,
                            jnp.where(sub >= d, a, pltpu.roll(b, d, 0)),
                            jnp.where(sub < DEEP - d, a, pltpu.roll(b, DEEP - d, 0)),
                        )
                    out_ref[f * side + rows + (i // 2) * (rows // 2) + d - 1] = a.astype(jnp.bfloat16)
        out_ref[2 * side] = flags.astype(jnp.bfloat16)


def edge_row(part, field, x, rows, right):
    side = 2 * rows
    if rows <= x < 2 * rows:
        return part[field * side + x - rows].astype(jnp.float32)
    d = rows - x if x < rows else x - 2 * rows + 1
    at = field * side + rows + (0 if x < rows else rows // 2) - 1
    if d <= rows // 2:
        return part[at + d].astype(jnp.float32)
    if d == rows:
        return part[at + rows // 2].astype(jnp.float32)
    v = part[at + rows - d].astype(jnp.float32)
    return jnp.where(right, pltpu.roll(v, d, 0), pltpu.roll(v, DEEP - d, 0))


def flux_sums(parts, twice):
    lane = lax.broadcasted_iota(jnp.int32, (SUB, LANES), 1)
    depths = []
    for val, wgt, lo, hi in parts:
        depths.append(
            {
                (c, j): [
                    (pltpu.roll(v, by, 1), pltpu.roll(w, by, 1))
                    for by in ((LANES - 1,) if twice else (LANES - 1, 1))
                ]
                for c in range(lo, hi)
                for j, (v, w) in enumerate(zip(val[c], wgt[c]))
            }
        )
    for (val, wgt, _, _), depth in zip(parts, depths):
        for (c, j), shifted in depth.items():
            f = None
            for (v, w), ok in zip(shifted, (lane < LANES - 1, lane > 0)):
                g = jnp.where(ok, (wgt[c][j] + w) * (v - val[c][j]), 0.0)
                f = g if f is None else f + g
            depth[c, j] = f
    for depth in depths:
        for at, f in depth.items():
            depth[at] = f - pltpu.roll(f, 1, 1) if twice else f

    sums = []
    for (val, wgt, lo, hi), depth in zip(parts, depths):
        n = len(val[lo])
        span = range(n)

        def toward(c):
            return [(wgt[c][j] + wgt[c + 1][j]) * (val[c + 1][j] - val[c][j]) for j in span]

        out = {}
        last = toward(lo - 1)
        for c in range(lo, hi):
            v, w = val[c], wgt[c]
            ahead = toward(c)
            down = [(w[j] + w[j + 1]) * (v[j + 1] - v[j]) for j in range(n - 1)]
            down.append(
                (w[n - 1] + pltpu.roll(w[0], SUB - 1, 0))
                * (pltpu.roll(v[0], SUB - 1, 0) - v[n - 1])
            )
            up = [pltpu.roll(down[-1], 1, 0)] + down[:-1]
            out[c] = [(ahead[j] - last[j]) + (down[j] - up[j]) + depth[c, j] for j in span]
            last = ahead
        sums.append(out)
    return sums


def advance(*parts, twice=True):
    fluxes = []
    for pore, h, q, lo, hi, _ in parts:
        val, wgt = {}, {}
        for c in range(lo - 1, hi + 1):
            t = [jnp.tanh(v) for v in h[c]]
            temp = [2.5 * v - u for v, u in zip(h[c], t)]
            if pore:
                val[c] = q[c]
                wgt[c] = [1.0 + jnp.tanh(v) for v in temp]
            else:
                val[c] = temp
                wgt[c] = [(1.0 - v) * (1.0 - v) * (u + 7.0 / 3.0) for v, u in zip(q[c], t)]
        fluxes.append((val, wgt, lo, hi))
    results = []
    for (pore, h, q, lo, hi, mask), (val, wgt, _, _), acc in zip(parts, fluxes, flux_sums(fluxes, twice)):
        new = {}
        for c in range(lo, hi):
            if pore:
                new[c] = [
                    v + m * (a - 4.0 * r * v)
                    for v, m, a, r in zip(q[c], mask(c, 1), acc[c], wgt[c])
                ]
            else:
                new[c] = [v + m * a for v, m, a in zip(h[c], mask(c, 0), acc[c])]
        results.append(new)
    return results


def tile_rows(marks, i, tx, n, out):
    low = lax.broadcasted_iota(jnp.int32, (SUB, LANES), 1) < LANES // 2
    sub = lax.broadcasted_iota(jnp.int32, (SUB, LANES), 0)
    other = pltpu.roll(marks, LANES // 2, 1)
    for h, flag in ((0, jnp.where(low, marks, other)), (1, jnp.where(low, other, marks))):
        first = (2 * i + h) * tx
        for j in range(n):
            x = sub * n + j
            out[j] = jnp.where((x >= first) & (x < first + tx), flag, out[j])
    return out


def scalings(flags):
    return ([0.009 * f for f in flags], [0.0375 * f for f in flags])


def back(columns, wide, turn, rows, total, heat):
    for c, column in enumerate(columns):
        n = len(column)
        for j, v in enumerate(column):
            wide[pl.ds(c * total + j, SUB, stride=n), :] = 0.5 * v + 1.0 if heat else v
    for c in range(len(columns)):
        turn[pl.ds(c * rows, rows), :] = wide[pl.ds(c * total + DEEP, rows), :]


def inner(
    own_ref, heat_ref, pore_ref, xa_ref, xb_ref,
    heat_out, pore_out, heat_save, pore_save, flag_out, wide,
):
    rows, cols = heat_ref.shape[0], heat_ref.shape[1]
    total = rows + 2 * DEEP
    width = cols + 2 * DEEP
    n = total // SUB
    tx, ty = rows // 2, cols // 2
    f32 = jnp.float32
    odd = lax.rem(lax.axis_index("gx") + lax.axis_index("gy"), 2)

    def row(i, r):
        if i == 1:
            return own_ref[r].astype(f32)
        pair = (xa_ref[r], xb_ref[r]) if i == 0 else (xb_ref[r], xa_ref[r])
        v = jnp.where(odd == 1, *pair).astype(f32)
        return v * inside("gx", i == 2)

    flags = []
    marks = [row(i, 2 * rows) for i in range(3)]
    for k in range(2):
        f = [jnp.zeros((SUB, LANES), f32) for _ in range(n)]
        for i in range(3):
            f = tile_rows(marks[i][k * ty : k * ty + SUB], i, tx, n, f)
        for j in range(n):
            flag_out[k, j] = f[j]
        flags.append(scalings(f))

    def mask(c, kind):
        return flags[0 if c < DEEP + ty else 1][kind]

    h, q = {}, {}
    for field, home, state in ((0, heat_ref, h), (1, pore_ref, q)):
        for i in range(3):
            for r in range(rows):
                v = home[r] if i == 1 else row(i, field * rows + r)
                v = 2.0 * v - 2.0 if field == 0 else v
                for g in range(0, cols, SUB):
                    at = g * total + (i * rows + r) * SUB
                    wide[field, at : at + SUB, :] = v[g : g + SUB]
        for c in range(cols):
            at = c // SUB * SUB * total + c % SUB
            state[DEEP + c] = [
                wide[field, pl.ds(at + j * SUB, SUB, stride=n * SUB), :] for j in range(n)
            ]

    for p in range(EARLY):
        lo, hi = DEEP + 2 * p + 1, width - DEEP - 2 * p - 1
        for side, c in ((0, lo), (1, hi - 1)):
            for j in range(n):
                heat_save[p, side, j] = h[c][j]
        h.update(*advance((False, h, q, lo, hi, mask)))
        lo, hi = lo + 1, hi - 1
        for side, c in ((0, lo), (1, hi - 1)):
            for j in range(n):
                pore_save[p, side, j] = q[c][j]
        q.update(*advance((True, h, q, lo, hi, mask)))
    for state, out in ((h, heat_out), (q, pore_out)):
        for c in range(cols):
            for j in range(n):
                out[c, j] = state[DEEP + c][j]


def halo(near, flag_ref, got_ref, wide, rows, n):
    total = n * SUB
    tx = rows // 2
    f32 = jnp.float32
    odd = lax.rem(lax.axis_index("gy"), 2)
    side = 1 - odd if near else odd
    left = side == 0
    has = None if near else jnp.where(left, inside("gy", False), inside("gy", True))
    row_open = (inside("gx", False), None, inside("gx", True))

    def scaled(v, *by):
        for s in by:
            v = v if s is None else v * s
        return v

    marks = scaled(got_ref[4 * rows].astype(f32), has)
    beyond = [jnp.zeros((SUB, LANES), f32) for _ in range(n)]
    for i in range(3):
        row = jnp.broadcast_to(scaled(marks[i : i + 1], row_open[i]), (SUB, LANES))
        beyond = tile_rows(row, i, tx, n, beyond)
    flags = [scalings(beyond), scalings([flag_ref[side, j] for j in range(n)])]

    def mask(c, kind):
        return flags[0 if c < DEEP else 1][kind]

    states = ({}, {})
    for field, state in enumerate(states):
        for x in range(total):
            v = scaled(edge_row(got_ref, field, x, rows, left), has, row_open[x // rows])
            wide[field, x * DEEP : (x + 1) * DEEP, :] = 2.0 * v - 2.0 if field == 0 else v
        for c in range(DEEP):
            state[c] = [
                jnp.where(
                    left,
                    wide[field, pl.ds(j * DEEP + c, SUB, stride=n * DEEP), :],
                    wide[field, pl.ds(j * DEEP + DEEP - 1 - c, SUB, stride=n * DEEP), :],
                )
                for j in range(n)
            ]
    return side, left, states, mask


def strips(h, q, left, wide, turn, rows, n):
    total = n * SUB
    for field, state in ((0, h), (1, q)):
        for c in range(DEEP):
            for j, v in enumerate(state[DEEP + c]):
                wide[field, pl.ds(c * total + j, SUB, stride=n), :] = (
                    0.5 * v + 1.0 if field == 0 else v
                )
        for c in range(DEEP):
            at = pl.multiple_of(jnp.where(left, c, DEEP - 1 - c) * rows, SUB)
            turn[field, pl.ds(at, rows), :] = wide[field, pl.ds(c * total + DEEP, rows), :]


def middle(
    heat_in, pore_in, heat_save, pore_save, flag_ref, got_ref,
    heat_strip, pore_strip, heat_mid, pore_mid, heat_edge, pore_edge, heat_kept, pore_kept,
    wide, turn, wide_mid, turn_mid,
):
    rows, cols = heat_mid.shape[0], heat_in.shape[0]
    n = heat_in.shape[1]
    width = cols + 2 * DEEP
    total = n * SUB
    ty = cols // 2
    span = range(n)
    side, left, (hw, qw), mask_w = halo(True, flag_ref, got_ref, wide, rows, n)
    flags = [scalings([flag_ref[k, j] for j in span]) for k in range(2)]

    def mask(c, kind):
        return flags[0 if c < DEEP + ty else 1][kind]

    h = {DEEP + c: [heat_in[c, j] for j in span] for c in range(cols)}
    q = {DEEP + c: [pore_in[c, j] for j in span] for c in range(cols)}

    def pick(low, high):
        return [jnp.where(left, a, b) for a, b in zip(low, high)]

    def at(state, c):
        return pick(state[c], state[width - 1 - c])

    kept = ({}, {})
    for p in range(EARLY):
        for keep, save, out in zip(kept, (heat_save, pore_save), (heat_kept, pore_kept)):
            keep[p] = [save[p, side, j] for j in span]
            for j in span:
                out[p, j] = save[p, 1 - side, j]

    def keep_now(field, state, p, c):
        low, high = state[c], state[width - 1 - c]
        kept[field][p] = pick(low, high)
        for j, v in enumerate(pick(high, low)):
            (heat_kept, pore_kept)[field][p, j] = v

    waiting = []

    def block_half(step):
        p, k = EARLY + step // 4, step % 4
        pore = k >= 2
        lo = DEEP + 2 * p + (2 if pore else 1)
        if k % 2 == 0:
            keep_now(int(pore), q if pore else h, p, lo)
        half = (lo, width // 2) if k % 2 == 0 else (width // 2, width - lo)
        return (pore, h, q, *half, mask)

    for p in range(PAIRS):
        for pore in (False, True):
            step = 2 * p + pore
            lo = 2 * p + 1 + pore
            end = block_half(step)
            if pore:
                hw[lo + DEEP - 1], hw[lo + DEEP] = at(h, lo + DEEP - 1), at(h, lo + DEEP)
                then = dict(qw)
                then[lo + DEEP] = kept[1][p]
                part = (True, hw, then, lo, lo + DEEP, mask_w)
            else:
                c = lo + DEEP - 1
                hw[c] = at(h, c)
                qw[c], qw[c + 1] = at(q, c), at(q, c + 1)
                then = dict(hw)
                then[c + 1] = kept[0][p]
                part = (False, then, qw, lo, lo + DEEP, mask_w)
            new, ours = advance(part, end, twice=step < 2 * PAIRS - 2)
            (qw if pore else hw).update(new)
            waiting.append(ours)
            if step % 2 == 1:
                for result in waiting:
                    (q if end[0] else h).update(result)
                waiting = []

    strips(hw, qw, left, wide, turn, rows, n)
    for field, out in ((0, heat_strip), (1, pore_strip)):
        for r in range(rows):
            out[r] = turn[field, pl.ds(r, DEEP, stride=rows), :]
    for field, state, edge, mid in ((0, h, heat_edge, heat_mid), (1, q, pore_edge, pore_mid)):
        for c in range(DEEP + 1):
            for j, v in enumerate(pick(state[width - 1 - DEEP - c], state[DEEP + c])):
                edge[c, j] = v
        back(
            [state[c] for c in range(2 * DEEP, width - 2 * DEEP)], wide_mid.at[field],
            turn_mid.at[field], rows, total, field == 0,
        )
        for r in range(rows):
            for g in range(0, cols - 2 * DEEP, SUB):
                mid[r, g : g + SUB] = turn_mid[field, pl.ds(g * rows + r, SUB, stride=rows), :]


def far_edge(
    mask_ref, heat_edge, pore_edge, heat_kept, pore_kept, heat_mid, pore_mid, flag_ref, got_ref,
    heat_near, pore_near, block, send_ref, wide, turn,
):
    rows, cols = heat_mid.shape[0], heat_mid.shape[1] + 2 * DEEP
    n = heat_edge.shape[1]
    span = range(n)
    side, left, (h, q), mask = halo(False, flag_ref, got_ref, wide, rows, n)
    for state, edge in ((h, heat_edge), (q, pore_edge)):
        for c in range(DEEP + 1):
            state[DEEP + c] = [edge[c, j] for j in span]
    for p in range(PAIRS):
        lo = 2 * p + 1
        then = dict(h)
        then[lo + DEEP] = [heat_kept[p, j] for j in span]
        h.update(*advance((False, then, q, lo, lo + DEEP, mask), twice=False))
        lo = lo + 1
        then = dict(q)
        then[lo + DEEP] = [pore_kept[p, j] for j in span]
        q.update(*advance((True, h, then, lo, lo + DEEP, mask), twice=False))
    strips(h, q, left, wide, turn, rows, n)
    end = cols - DEEP
    far_at = pl.ds(pl.multiple_of(end * side, SUB), DEEP)
    near_at = pl.ds(pl.multiple_of(end - end * side, SUB), DEEP)
    for field, mid, near in ((0, heat_mid, heat_near), (1, pore_mid, pore_near)):
        for r in range(rows):
            block[field, r, DEEP:end] = mid[r]
            block[field, r, near_at] = near[r]
            block[field, r, far_at] = turn[field, pl.ds(r, DEEP, stride=rows), :]
    chosen(mask_ref, 0, block, send_ref)


def tile_of(block, field, s):
    tx, ty = block.shape[1] // 2, block.shape[2] // 2
    i, k = s // 2, s % 2
    return block[field, i * tx : (i + 1) * tx, k * ty : (k + 1) * ty, :]


def chosen(mask_ref, i, block, out):
    choose = mask_at(out.shape[0])[0]
    for field, scale, shift in ((0, HEAT_SCALE, HEAT_SHIFT), (1, PORE_SCALE, PORE_SHIFT)):
        for k in range(out.shape[0]):
            v = tile_of(block, field, 0)
            for s in range(1, 4):
                v = jnp.where(
                    held(mask_ref, choose(i, k, s), v.shape), tile_of(block, field, s), v
                )
            out[k, field] = encode(v, scale, shift)


def split(mask_ref, block, heat_out, pore_out, later_ref):
    for field, out in ((0, heat_out), (1, pore_out)):
        for s in range(4):
            out[s] = tile_of(block, field, s)
    chosen(mask_ref, 1, block, later_ref)


def held(mask_ref, row, shape):
    m = mask_ref[row]
    m = jnp.concatenate([m] * (shape[1] // SUB), axis=0)
    return jnp.broadcast_to(m[None], shape) > 0.5


def resend(mask_ref, got_ref, local_ref, send_ref):
    ranks = got_ref.shape[0]
    shape = got_ref.shape[2:]
    again = mask_at(ranks)[2]
    for k in range(ranks):
        for f in range(2):
            v = local_ref[k, f].astype(jnp.int32)
            for r in range(ranks):
                v = jnp.where(
                    held(mask_ref, again(k, r), shape), got_ref[r, f].astype(jnp.int32), v
                )
            send_ref[k, f] = v.astype(jnp.int16)


def place(mask_ref, heat_ref, pore_ref, first_ref, second_ref, heat_out, pore_out):
    ranks = first_ref.shape[0]
    shape = first_ref.shape[2:]
    taken = mask_at(ranks)[1]
    for field, src, out, scale, shift in (
        (0, heat_ref, heat_out, HEAT_SCALE, HEAT_SHIFT),
        (1, pore_ref, pore_out, PORE_SCALE, PORE_SHIFT),
    ):
        came = [
            (i, r, decode(got[r, field], scale, shift))
            for i, got in ((0, first_ref), (1, second_ref))
            for r in range(ranks)
        ]
        for s in range(4):
            v = src[s]
            for i, r, tile in came:
                v = jnp.where(held(mask_ref, taken(i, r, s), shape), tile, v)
            out[s] = v


def call(body, spec, outs, scratch=(), out_space=pltpu.VMEM):
    def run(*args):
        space = {"s": pltpu.SMEM, "v": pltpu.VMEM, "V": pltpu.VMEM}
        args = [
            pltpu.with_memory_space_constraint(a, pltpu.VMEM if c == "V" else pltpu.HBM)
            for c, a in zip(spec, args)
        ]
        shapes = [
            pltpu.VMEM(s, d) if out_space is not None else jax.ShapeDtypeStruct(s, d)
            for s, d in outs
        ]
        return pl.pallas_call(
            body,
            in_specs=[pl.BlockSpec(memory_space=space[c]) for c in spec],
            out_specs=[pl.BlockSpec(memory_space=pltpu.VMEM) for _ in outs],
            out_shape=shapes,
            scratch_shapes=list(scratch),
            compiler_params=pltpu.CompilerParams(vmem_limit_bytes=VMEM_LIMIT),
        )(*args)

    return run


def permute(value, partner):
    nx, ny = lax.axis_size("gx"), lax.axis_size("gy")
    pairs = []
    for x in range(nx):
        for y in range(ny):
            u, v = partner(x, y)
            pairs.append((x * ny + y, u * ny + v))
    return lax.ppermute(value, ("gx", "gy"), pairs)


def exchange_x(value):
    nx, ny = lax.axis_size("gx"), lax.axis_size("gy")

    def partner(x, y, near):
        if near:
            return x ^ 1, y
        if 0 < x < nx - 1:
            return ((x + 1) ^ 1) - 1, y
        return (x, y ^ 2) if ny % 4 == 0 else (x, y)

    first = permute(value, lambda x, y: partner(x, y, y % 2 == 0))
    second = permute(value, lambda x, y: partner(x, y, y % 2 == 1))
    return first, second


def exchange_y(near, far):
    ny = lax.axis_size("gy")

    def partner(x, y):
        if 0 < y < ny - 1:
            return x, ((y + 1) ^ 1) - 1
        return x ^ 1, y

    far = permute(far, partner)
    near = permute(near, lambda x, y: (x, y ^ 1))
    return near, far


def swap(value, axis):
    n = lax.axis_size(axis)
    return lax.ppermute(value, axis, [(i, (i + n // 2) % n) for i in range(n)])


def per_device(enthalpy, porosity, active, move_count, move_slot):
    rows, cols, depth = enthalpy.shape
    tx, ty = rows // 2, cols // 2
    count = move_count.reshape(2)
    slots = move_slot.reshape(2, move_slot.shape[-1])
    ranks = slots.shape[1]
    f32, bf16, i16 = jnp.float32, jnp.bfloat16, jnp.int16

    block = ((rows, cols, depth), f32)
    masks = ((mask_at(ranks)[3], SUB, LANES), f32)
    own, enthalpy, porosity, masks = call(
        pack_x, "sssvv", [((2 * rows + 1, cols, depth), bf16), block, block, masks]
    )(active, count, slots, enthalpy, porosity)
    x_near, x_far = exchange_x(own)
    side = ((4 * rows + 1, DEEP, depth), bf16)
    near, far = call(pack_y, "VVV", [side, side])(own, x_near, x_far)
    y_near, y_far = exchange_y(near, far)
    total = rows + 2 * DEEP
    n = total // SUB
    tiles = ((4, tx, ty, depth), f32)
    parcel = ((ranks, 2, tx, ty, depth), i16)
    column = (n, SUB, depth)
    whole = ((cols, *column), f32)
    save = ((EARLY, 2, *column), f32)
    edge = ((DEEP + 1, *column), f32)
    kept = ((PAIRS, *column), f32)
    mid = ((rows, cols - 2 * DEEP, depth), f32)
    strip = ((rows, DEEP, depth), f32)
    state = call(
        inner, "VVVVV", [whole, whole, save, save, ((2, *column), f32)],
        [pltpu.VMEM((2, total * cols, depth), f32)],
    )(own, enthalpy, porosity, x_near, x_far)
    scratch = [
        pltpu.VMEM((2, total * DEEP, depth), f32),
        pltpu.VMEM((2, rows * DEEP, depth), f32),
    ]
    heat_near, pore_near, heat_mid, pore_mid, *ends = call(
        middle, "V" * 6, [strip, strip, mid, mid, edge, edge, kept, kept],
        scratch
        + [
            pltpu.VMEM((2, total * (cols - 2 * DEEP), depth), f32),
            pltpu.VMEM((2, rows * (cols - 2 * DEEP), depth), f32),
        ],
    )(*state, y_near)
    last, first = call(
        far_edge, "V" * 11, [((2, rows, cols, depth), f32), parcel], scratch
    )(masks, *ends, heat_mid, pore_mid, state[4], y_far, heat_near, pore_near)
    heat, pore, later = call(split, "VV", [tiles, tiles, parcel])(masks, last)
    first = swap(first, "gx")
    (second,) = call(resend, "VVV", [parcel])(masks, first, later)
    second = swap(second, "gy")
    heat, pore = call(place, "VVVVV", [tiles, tiles], out_space=None)(
        masks, heat, pore, first, second
    )
    return heat[None, None], pore[None, None]


def solution(mesh):
    placed = (
        P("gx", "gy", None),
        P("gx", "gy", None),
        P("gx", "gy"),
        P("gx", "gy", None),
        P("gx", "gy", None, None),
    )
    out = P("gx", "gy", None, None, None, None)

    return jax.shard_map(
        per_device, mesh=mesh, in_specs=placed, out_specs=(out, out), check_vma=False
    )
```
